256 devices in a mesh: ctx: 32 (over z, y), fsdp: 4 (over x_lo, core), tp: 2 (over x_hi).
Axes of the slice: x: 4 (x_hi: 2, x_lo: 2; x = x_hi * 2 + x_lo), y: 4, z: 8, core: 2. Of those that a mesh axis runs over, the one named last changes fastest.
Arguments:
- features: bfloat16 [4608, 3, 4096], P('ctx', None, ('fsdp', 'tp')), may hold values from -6 to 6
- short_filter: float32 [3, 7, 256], replicated, may hold values from -2 to 2
- long_filter_taps: float32 [128, 256], replicated, may hold values from -0.5 to 0.5
- queries: bfloat16 [4608, 4096], P('ctx', ('fsdp', 'tp')), may hold values from -4.5 to 4.5
- key_vectors: bfloat16 [4608, 4096], P('ctx', ('fsdp', 'tp')), may hold values from -4.5 to 4.5
- value_vectors: bfloat16 [4608, 4096], P('ctx', ('fsdp', 'tp')), may hold values from -6 to 6
- grad_mixed: bfloat16 [4608, 4096], P('ctx', ('fsdp', 'tp')), may hold values from -6 to 6
- grad_attended: bfloat16 [4608, 4096], P('ctx', ('fsdp', 'tp')), may hold values from -6 to 6
Outputs:
- mixed_tokens: bfloat16 [4608, 4096], P('ctx', ('fsdp', 'tp'))
- attended: bfloat16 [4608, 4096], P('ctx', ('fsdp', 'tp'))
- grad_features: float32 [4608, 3, 4096], P('ctx', None, ('fsdp', 'tp'))
- grad_short: float32 [3, 7, 256], replicated
- grad_long: float32 [128, 256], replicated
- grad_queries: float32 [4608, 4096], P('ctx', ('fsdp', 'tp'))
- grad_key_vectors: float32 [4608, 4096], P('ctx', ('fsdp', 'tp'))
- grad_value_vectors: float32 [4608, 4096], P('ctx', ('fsdp', 'tp'))
The draws below stay inside these ranges and needn't reach their ends.
All inputs are finite; a program needn't handle non-finite values.
Results may differ from the reference program's by a relative error of at most 0.01.
Values may be sent and summed in bfloat16 or wider, within the bound.
No kernel may reach another device: no remote copies, remote signals or barrier semaphores. Data moves between devices by JAX's collectives and lax.ppermute only.
A program may use at most 128 MiB of HBM per device.

```python
import jax
import jax.numpy as jnp
from jax import lax

C = 4096
HEADS = 32
HD = 128
FILTER_TOTAL = 256
LONG_FILTER_TAPS = 128
SHORT = 7
SEQ = 4608
HH = 4096


def drawn_normal(key, salt_value):
    sample = jax.random.normal(jax.random.fold_in(key, salt_value), (SEQ, HEADS * HD), jnp.float32)
    return jnp.clip(sample, -4.5, 4.5)


def draw_queries(key, part):
    sample = drawn_normal(key, 1)
    return sample.astype(jnp.bfloat16)


def draw_key_vectors(key, part):
    sample = drawn_normal(key, 2)
    return sample.astype(jnp.bfloat16)


def draw_grad_mixed(key, part):
    rising = 0.5 + jnp.arange(SEQ).astype(jnp.float32) / SEQ
    sample = jnp.clip(jax.random.normal(jax.random.fold_in(key, 5), (SEQ, C), jnp.float32), -4.0, 4.0)
    sample = sample * rising[:, None]
    return sample.astype(jnp.bfloat16)


def steps_of(own_key, shape, cuts, low, largest):
    loudness = 1.0
    for position, blocks in cuts:
        draws = jax.random.uniform(jax.random.fold_in(jax.random.fold_in(own_key, 6), position), (blocks,), jnp.float32, low / len(cuts), largest / len(cuts))
        loudness = loudness * jnp.repeat(jnp.exp(draws), shape[position] // blocks).reshape((-1,) + (1,) * (len(shape) - 1 - position))
    return loudness


def scatter_about(key, extent, spread, reach, cuts=(), kind=jnp.bfloat16):
    gain = steps_of(key, extent, cuts, -0.22, 0.18) if cuts else 1.0
    values = jax.random.normal(key, extent, jnp.float32) * spread * gain
    return jnp.minimum(jnp.maximum(values, -reach), reach).astype(kind)


def setup_inputs(seed: int = 0) -> dict:
    splits = jax.random.split(jax.random.key(seed), 9)
    return {
        "features": scatter_about(splits[0], (SEQ, 3, C), 1.0, 6.0, ((0, 32), (2, 8))),
        "short_filter": scatter_about(splits[1], (3, SHORT, FILTER_TOTAL), SHORT ** -0.5, 2.0, (), jnp.float32),
        "long_filter_taps": scatter_about(splits[2], (LONG_FILTER_TAPS, FILTER_TOTAL), LONG_FILTER_TAPS ** -0.5, 0.5, (), jnp.float32),
        "queries": draw_queries(jax.random.fold_in(splits[8], 71), 0),
        "key_vectors": draw_key_vectors(jax.random.fold_in(splits[8], 71), 0),
        "value_vectors": scatter_about(splits[5], (SEQ, HH), 1.0, 6.0, ((0, 32), (1, 8))),
        "grad_mixed": draw_grad_mixed(jax.random.fold_in(splits[8], 71), 0),
        "grad_attended": scatter_about(splits[7], (SEQ, HH), 1.0, 6.0, ((0, 32), (1, 8))),
    }


def tile_filter(filters, width_cols):
    return jnp.tile(filters, (1, width_cols // filters.shape[1]))


def conv_apply(padded, kernel, row_total, turn_taps):
    length = kernel.shape[0]

    def advance(turn_index, summed):
        for offset_tap in range(turn_taps):
            tap_index = turn_index * turn_taps + offset_tap
            window = lax.dynamic_slice_in_dim(padded, length - 1 - tap_index, row_total, 0)
            summed = summed + lax.dynamic_index_in_dim(kernel, tap_index, 0, False) * window
        return summed

    return lax.fori_loop(0, length // turn_taps, advance, jnp.zeros((row_total, padded.shape[1]), jnp.float32))


def conv_adjoint(grad_out, kernel, turn_taps):
    length = kernel.shape[0]
    border = jnp.zeros((length - 1, grad_out.shape[1]), jnp.float32)
    extended = jnp.concatenate([border, grad_out, border], 0)
    out_rows = grad_out.shape[0] + length - 1

    def advance(turn_index, summed):
        for offset_tap in range(turn_taps):
            tap_index = turn_index * turn_taps + offset_tap
            window = lax.dynamic_slice_in_dim(extended, tap_index, out_rows, 0)
            summed = summed + lax.dynamic_index_in_dim(kernel, tap_index, 0, False) * window
        return summed

    return lax.fori_loop(0, length // turn_taps, advance, jnp.zeros((out_rows, grad_out.shape[1]), jnp.float32))


def kernel_adjoint(grad_out, padded, filter_count, turn_taps):
    row_total = grad_out.shape[0]
    length = padded.shape[0] - row_total + 1

    def advance(turn_index, result):
        for offset_tap in range(turn_taps):
            tap_index = turn_index * turn_taps + offset_tap
            window = lax.dynamic_slice_in_dim(padded, length - 1 - tap_index, row_total, 0)
            column = jnp.sum(grad_out * window, axis=0)
            folded = jnp.sum(column.reshape(-1, filter_count), axis=0)
            result = lax.dynamic_update_index_in_dim(result, folded, tap_index, 0)
        return result

    return lax.fori_loop(0, length // turn_taps, advance, jnp.zeros((length, filter_count), jnp.float32))


def hyena_reference(features, short_filter, long_filter_taps, grad_mixed):
    total_rows = features.shape[0]
    channels = features.shape[2]
    short_taps = short_filter.shape[1]
    long_taps = long_filter_taps.shape[0]
    filter_count = long_filter_taps.shape[1]
    inputs = features.astype(jnp.float32)
    leading = jnp.zeros((short_taps - 1, channels), jnp.float32)
    short_tiles = [tile_filter(short_filter[g], channels) for g in range(3)]
    padded_in = [jnp.concatenate([leading, inputs[:, g]], 0) for g in range(3)]
    featured = [conv_apply(padded_in[g], short_tiles[g], total_rows, short_taps) for g in range(3)]
    product = featured[0] * featured[2]
    long_tile = tile_filter(long_filter_taps, channels)
    history = jnp.concatenate([jnp.zeros((long_taps - 1, channels), jnp.float32), product], 0)
    memory = conv_apply(history, long_tile, total_rows, 8)
    gating = featured[1]
    mixed_tokens = (gating * memory).astype(jnp.bfloat16)
    upstream = grad_mixed.astype(jnp.float32)
    grad_memory = upstream * gating
    grad_gate = upstream * memory
    grad_product = conv_adjoint(grad_memory, long_tile, 8)[long_taps - 1:]
    grad_long = kernel_adjoint(grad_memory, history, filter_count, 8)
    grad_feat = [grad_product * featured[2], grad_gate, grad_product * featured[0]]
    grad_inputs = [conv_adjoint(grad_feat[g], short_tiles[g], short_taps)[short_taps - 1:] for g in range(3)]
    grad_short = jnp.stack([kernel_adjoint(grad_feat[g], padded_in[g], filter_count, short_taps) for g in range(3)], 0)
    return mixed_tokens, jnp.stack(grad_inputs, 1), grad_short, grad_long


def attention_reference(queries, key_vectors, value_vectors, grad_attended):
    total_rows = queries.shape[0]
    head_count = queries.shape[1] // HD
    score_scale = HD ** -0.5
    positions = jnp.arange(total_rows, dtype=jnp.int32)
    causal = positions[:, None] >= positions[None, :]

    def to_heads(x):
        return x.reshape(total_rows, head_count, HD).transpose(1, 0, 2)

    def from_heads(x):
        return x.transpose(1, 0, 2).reshape(total_rows, head_count * HD)

    def one_head(operands):
        q, k, v, d = operands
        scores = jnp.dot(q, k.T, preferred_element_type=jnp.float32) * score_scale
        scores = jnp.where(causal, scores, -jnp.inf)
        row_max = jnp.max(scores, axis=1, keepdims=True)
        log_total = row_max + jnp.log(jnp.sum(jnp.exp(scores - row_max), axis=1, keepdims=True))
        weights = jnp.exp(scores - log_total)
        weights_low = weights.astype(jnp.bfloat16)
        output = jnp.dot(weights_low, v, preferred_element_type=jnp.float32)
        output_low = output.astype(jnp.bfloat16)
        row_delta = jnp.sum(d.astype(jnp.float32) * lax.optimization_barrier(output_low).astype(jnp.float32), axis=1, keepdims=True)
        grad_weights = jnp.dot(d, v.T, preferred_element_type=jnp.float32)
        grad_scores = (weights * (grad_weights - row_delta)).astype(jnp.bfloat16)
        grad_query = score_scale * jnp.dot(grad_scores, k, preferred_element_type=jnp.float32)
        grad_key = score_scale * jnp.dot(grad_scores.T, q, preferred_element_type=jnp.float32)
        grad_value = jnp.dot(weights_low.T, d, preferred_element_type=jnp.float32)
        return output_low, grad_query, grad_key, grad_value

    results = lax.map(one_head, (to_heads(queries), to_heads(key_vectors), to_heads(value_vectors), to_heads(grad_attended)))
    return tuple(from_heads(x) for x in results)


def reference(features, short_filter, long_filter_taps, queries, key_vectors, value_vectors, grad_mixed, grad_attended):
    mixed_tokens, grad_features, grad_short, grad_long = hyena_reference(features, short_filter, long_filter_taps, grad_mixed)
    attended, grad_queries, grad_key_vectors, grad_value_vectors = attention_reference(queries, key_vectors, value_vectors, grad_attended)
    return (mixed_tokens, attended, grad_features, grad_short, grad_long, grad_queries, grad_key_vectors, grad_value_vectors)
```

```python
import jax
import jax.numpy as jnp
import numpy as np
from jax import lax
from jax.experimental import pallas as pl
from jax.experimental.pallas import tpu as pltpu
from jax.sharding import Mesh, PartitionSpec as P

HD = 128
ROWS = 144
GROUP = 576
SEQ = 4608
CHUNK = 512
CHUNKS = SEQ // CHUNK
LOG2E = 1.4426950408889634
SCALE = HD ** -0.5
VMEM_BYTES = 56 * 1024 * 1024
F32 = jnp.float32
BF16 = jnp.bfloat16
CTX = ("cz", "cy")
FT = ("fsdp", "tp")


def after(value, *others):
    return lax.optimization_barrier((value,) + others)[0]


def call(body, out_shape, name, **options):
    return pl.pallas_call(
        body,
        out_shape=out_shape,
        name=name,
        compiler_params=pltpu.CompilerParams(vmem_limit_bytes=VMEM_BYTES),
        **options,
    )


def struct(shape, dtype):
    return jax.ShapeDtypeStruct(shape, dtype)


def nt(a, b):
    return lax.dot_general(a, b, (((1,), (1,)), ((), ())), preferred_element_type=F32)


def nn(a, b):
    return lax.dot_general(a, b, (((1,), (0,)), ((), ())), preferred_element_type=F32)


def pack_body(a_ref, b_ref, out_ref):
    for h in range(4):
        out_ref[h, :, :HD] = a_ref[:, h * HD : (h + 1) * HD]
        out_ref[h, :, HD:] = b_ref[:, h * HD : (h + 1) * HD]


def pack(a, b):
    return call(pack_body, struct((4, ROWS, 2 * HD), BF16), "pack")(a, b)


def unpack_body(x_ref, a_ref, b_ref):
    for h in range(4):
        a_ref[:, h * HD : (h + 1) * HD] = x_ref[h, :, :HD].astype(a_ref.dtype)
        b_ref[:, h * HD : (h + 1) * HD] = x_ref[h, :, HD:].astype(b_ref.dtype)


def unpack(x, kind_a, kind_b):
    return call(
        unpack_body,
        (struct((ROWS, 4 * HD), kind_a), struct((ROWS, 4 * HD), kind_b)),
        "unpack",
    )(x)


def hyena_body(
    feat_ref, prev_ref, next_ref, up_ref, short_ref, long_ref,
    mixed_ref, gfeat_ref, glong_ref, gshort_ref,
    x_ref, x1_ref, p_ref, ps_ref, gm_ref, gs_ref, f_ref, gf_ref, wb_ref, gl_ref,
):
    turn = pl.program_id(1)
    for slot, g in enumerate((0, 2)):
        x_ref[slot, 0:136] = prev_ref[g].astype(F32)
        x_ref[slot, 136:280] = feat_ref[g].astype(F32)
        x_ref[slot, 280:288] = next_ref[272 + 8 * slot : 280 + 8 * slot].astype(F32)
    x1_ref[0:136] = prev_ref[1].astype(F32)
    x1_ref[136:280] = feat_ref[1].astype(F32)
    x1_ref[280:416] = next_ref[0:136].astype(F32)
    taps = [[short_ref[g, s : s + 1, :] for s in range(7)] for g in range(3)]

    def featured(read, g):
        total = taps[g][0] * read(0)
        for s in range(1, 7):
            total = total + taps[g][s] * read(s)
        return total

    f0 = featured(lambda s: x_ref[0, 8 - s : 288 - s], 0)
    f2 = featured(lambda s: x_ref[1, 8 - s : 288 - s], 2)
    p_ref[8:288] = f0 * f2
    f_ref[0] = f0[128:280]
    f_ref[2] = f2[128:280]
    f1 = featured(lambda s: x1_ref[136 - s : 416 - s], 1)
    f_ref[1] = f1[0:152]
    gm_ref[0:144] = up_ref[...].astype(F32) * f1[0:144]
    gm_ref[144:280] = next_ref[136:272].astype(F32) * f1[144:280]
    for b in range(8):
        ps_ref[b, 16:288] = p_ref[16 - b : 288 - b]
        gs_ref[b] = gm_ref[b : 272 + b]
    wb_ref[...] = jnp.broadcast_to(long_ref[...][:, None, :], (128, 8, 128))

    def forward(a, total):
        base = pl.multiple_of(136 - 8 * a, 8)
        for b in range(8):
            tap = 8 * a + b
            x = ps_ref[b, pl.ds(base, 152), :].reshape(19, 8, 128)
            total = total + wb_ref[tap][None] * x
            gm = gm_ref[0:144].reshape(18, 8, 128)
            gl_ref[tap] = jnp.sum(gm * x[:18], axis=0)
        return total

    memory = lax.fori_loop(0, 16, forward, jnp.zeros((19, 8, 128), F32)).reshape(152, 128)
    mixed_ref[...] = (f_ref[1, 0:144] * memory[0:144]).astype(BF16)
    gf_ref[1, 0:144] = up_ref[...].astype(F32) * memory[0:144]
    gf_ref[1, 144:152] = next_ref[136:144].astype(F32) * memory[144:152]

    def backward(a, total):
        base = pl.multiple_of(8 * a, 8)
        for b in range(8):
            y = gs_ref[b, pl.ds(base, 152), :].reshape(19, 8, 128)
            total = total + wb_ref[8 * a + b][None] * y
        return total

    gp = lax.fori_loop(0, 16, backward, jnp.zeros((19, 8, 128), F32)).reshape(152, 128)
    gf_ref[0] = gp * f_ref[2]
    gf_ref[2] = gp * f_ref[0]
    glong = jnp.sum(gl_ref[...], axis=1)

    @pl.when(turn == 0)
    def _():
        glong_ref[...] = glong
        gshort_ref[...] = jnp.zeros_like(gshort_ref)

    @pl.when(turn != 0)
    def _():
        glong_ref[...] += glong

    for g in range(3):
        total = taps[g][0] * gf_ref[g, 0:144]
        for s in range(1, 7):
            total = total + taps[g][s] * gf_ref[g, s : 144 + s]
        gfeat_ref[g] = total
        own = gf_ref[g, 0:144]
        for s in range(7):
            if g == 1:
                x = x1_ref[136 - s : 280 - s]
            else:
                x = x_ref[g // 2, 136 - s : 280 - s]
            column = jnp.sum((own * x).reshape(18, 8, 128), axis=0)
            gshort_ref[g, s : s + 1, :] += jnp.sum(column, axis=0, keepdims=True)


def hyena(feat, prev, nxt, up, short8, long_taps):
    def cols(*lead):
        return pl.BlockSpec(lead + (128,), lambda f, k: (0,) * len(lead) + (2 * k + f,))

    def filters(*lead):
        return pl.BlockSpec(lead + (128,), lambda f, k: (0,) * len(lead) + (f,))

    return call(
        hyena_body,
        (
            struct((ROWS, 512), BF16),
            struct((3, ROWS, 512), F32),
            struct((128, 256), F32),
            struct((3, 8, 256), F32),
        ),
        "hyena",
        grid=(2, 2),
        in_specs=[
            cols(3, ROWS), cols(3, 136), cols(288), cols(ROWS), filters(3, 8), filters(128),
        ],
        out_specs=(cols(ROWS), cols(3, ROWS), filters(128), filters(3, 8)),
        scratch_shapes=[
            pltpu.VMEM((2, 288, 128), F32),
            pltpu.VMEM((416, 128), F32),
            pltpu.VMEM((288, 128), F32),
            pltpu.VMEM((8, 288, 128), F32),
            pltpu.VMEM((280, 128), F32),
            pltpu.VMEM((8, 272, 128), F32),
            pltpu.VMEM((3, 152, 128), F32),
            pltpu.VMEM((3, 152, 128), F32),
            pltpu.VMEM((128, 8, 128), F32),
            pltpu.VMEM((128, 8, 128), F32),
        ],
    )(feat, prev, nxt, up, short8, long_taps)


def lane_max(x):
    best = x[:, 0:128]
    for j in range(1, CHUNK // 128):
        best = jnp.maximum(best, x[:, j * 128 : (j + 1) * 128])
    return best


def lane_sum(x):
    total = x[:, 0:128]
    for j in range(1, CHUNK // 128):
        total = total + x[:, j * 128 : (j + 1) * 128]
    return total


def query_body(where_ref, own_ref, kv_ref, out_ref, stat_ref, s_ref, mx_ref, l_ref, o_ref, st_ref):
    first = where_ref[0] * GROUP
    clear = first // CHUNK
    total = (first + GROUP + CHUNK - 1) // CHUNK
    mx_ref[...] = jnp.full_like(mx_ref, -jnp.inf)
    l_ref[...] = jnp.zeros_like(l_ref)
    o_ref[...] = jnp.zeros_like(o_ref)

    def rows_of(c):
        return pl.ds(pl.multiple_of(c * CHUNK, CHUNK), CHUNK)

    def scores(c, masked):
        s = nt(own_ref[:, :HD], kv_ref[rows_of(c), :HD]) * (SCALE * LOG2E)
        if masked:
            q = first + lax.broadcasted_iota(jnp.int32, (GROUP, CHUNK), 0)
            k = c * CHUNK + lax.broadcasted_iota(jnp.int32, (GROUP, CHUNK), 1)
            s = jnp.where(q >= k, s, -jnp.inf)
        s_ref[c] = s
        mx_ref[...] = jnp.maximum(mx_ref[...], lane_max(s))

    @pl.loop(0, clear)
    def _(c):
        scores(c, False)

    @pl.loop(clear, total)
    def _(c):
        scores(c, True)

    peak = jnp.max(mx_ref[...], axis=1, keepdims=True)

    @pl.loop(0, total)
    def _(c):
        p = jnp.exp2(s_ref[c] - peak)
        s_ref[c] = p
        l_ref[...] += lane_sum(p)
        o_ref[...] += nn(p.astype(BF16), kv_ref[rows_of(c), HD:])

    norm = jnp.sum(l_ref[...], axis=1, keepdims=True)
    inverse = 1.0 / norm
    attended = (o_ref[...] * inverse).astype(BF16)
    out_ref[:, :HD] = attended
    delta = jnp.sum(
        own_ref[:, HD:].astype(F32) * attended.astype(F32), axis=1, keepdims=True
    )
    o_ref[...] = jnp.zeros_like(o_ref)

    @pl.loop(0, total)
    def _(c):
        rows = rows_of(c)
        gw = nt(own_ref[:, HD:], kv_ref[rows, HD:])
        gs = (s_ref[c] * (gw - delta)).astype(BF16)
        o_ref[...] += nn(gs, kv_ref[rows, :HD])

    out_ref[:, HD:] = (o_ref[...] * (inverse * SCALE)).astype(BF16)
    lane = lax.broadcasted_iota(jnp.int32, (GROUP, HD), 1)
    st_ref[0:GROUP] = jnp.where(lane == 0, peak + jnp.log2(norm), delta)
    st_ref[GROUP:640] = jnp.zeros((640 - GROUP, HD), F32)
    stat_ref[...] = st_ref[...].T[0:8]


def query_pass(where, own, kv):
    return call(
        query_body,
        (struct((GROUP, 2 * HD), BF16), struct((8, 640), F32)),
        "query_pass",
        in_specs=[
            pl.BlockSpec(memory_space=pltpu.SMEM),
            pl.BlockSpec(memory_space=pltpu.VMEM),
            pl.BlockSpec(memory_space=pltpu.VMEM),
        ],
        scratch_shapes=[
            pltpu.VMEM((CHUNKS, GROUP, CHUNK), F32),
            pltpu.VMEM((GROUP, HD), F32),
            pltpu.VMEM((GROUP, HD), F32),
            pltpu.VMEM((GROUP, HD), F32),
            pltpu.VMEM((640, HD), F32),
        ],
    )(where, own, kv)


def key_body(where_ref, own_ref, qd_ref, stat_ref, out_ref, gk_ref, gv_ref):
    first = where_ref[0] * GROUP
    begin = first // CHUNK
    clear = (first + GROUP - 1 + CHUNK - 1) // CHUNK
    gk_ref[...] = jnp.zeros_like(gk_ref)
    gv_ref[...] = jnp.zeros_like(gv_ref)

    def visit(c, masked):
        rows = pl.ds(pl.multiple_of(c * CHUNK, CHUNK), CHUNK)
        log_row = stat_ref[c, 0:1, :]
        delta_row = stat_ref[c, 1:2, :]
        q = qd_ref[rows, :HD]
        d = qd_ref[rows, HD:]
        s = nt(own_ref[:, :HD], q) * (SCALE * LOG2E)
        p = jnp.exp2(s - log_row)
        if masked:
            k_at = first + lax.broadcasted_iota(jnp.int32, (GROUP, CHUNK), 0)
            q_at = c * CHUNK + lax.broadcasted_iota(jnp.int32, (GROUP, CHUNK), 1)
            p = jnp.where(q_at >= k_at, p, 0.0)
        gv_ref[...] += nn(p.astype(BF16), d)
        gw = nt(own_ref[:, HD:], d)
        gs = (p * (gw - delta_row)).astype(BF16)
        gk_ref[...] += nn(gs, q)

    @pl.loop(begin, jnp.minimum(clear, CHUNKS))
    def _(c):
        visit(c, True)

    @pl.loop(clear, CHUNKS)
    def _(c):
        visit(c, False)

    out_ref[:, :HD] = (gk_ref[...] * SCALE).astype(BF16)
    out_ref[:, HD:] = gv_ref[...].astype(BF16)


def key_pass(where, own, qd, stats):
    return call(
        key_body,
        struct((GROUP, 2 * HD), BF16),
        "key_pass",
        in_specs=[
            pl.BlockSpec(memory_space=pltpu.SMEM),
            pl.BlockSpec(memory_space=pltpu.VMEM),
            pl.BlockSpec(memory_space=pltpu.VMEM),
            pl.BlockSpec(memory_space=pltpu.VMEM),
        ],
        scratch_shapes=[pltpu.VMEM((GROUP, HD), F32), pltpu.VMEM((GROUP, HD), F32)],
    )(where, own, qd, stats)


def exchange(x, axis):
    return lax.all_to_all(x, axis, 0, 0, tiled=True)


def share(x, axis, count):
    return exchange(jnp.broadcast_to(x[None], (count,) + x.shape), axis)


def body(
    features, short_filter, long_filter_taps, queries, key_vectors, value_vectors,
    grad_mixed, grad_attended,
):
    feat = features.transpose(1, 0, 2)
    prev = lax.ppermute(feat[:, 8:], CTX, [(i, i + 1) for i in range(31)])
    rim = jnp.concatenate([feat[1, :136], grad_mixed[:136], feat[0, :8], feat[2, :8]], 0)
    nxt = lax.ppermute(rim, CTX, [(i + 1, i) for i in range(31)])

    where = lax.axis_index("cz").astype(jnp.int32).reshape(1)
    own_kv = exchange(pack(key_vectors, value_vectors), "cy").reshape(GROUP, 2 * HD)
    all_kv = lax.all_gather(own_kv, "cz", axis=0, tiled=True)
    own_qd = exchange(pack(queries, grad_attended), "cy").reshape(GROUP, 2 * HD)
    all_qd = lax.all_gather(own_qd, "cz", axis=0, tiled=True)

    short8 = jnp.pad(short_filter, ((0, 0), (0, 1), (0, 0)))
    mixed, gfeat, glong, gshort = hyena(
        feat, prev, nxt, after(grad_mixed, own_qd), short8, long_filter_taps
    )
    grads = jnp.concatenate([glong, gshort.reshape(24, 256), jnp.zeros((8, 256), F32)], 0)
    part = jnp.sum(exchange(grads.reshape(8, 40, HD), FT), axis=0)

    out_q, stats = query_pass(where, after(own_qd, part), all_kv)
    small = jnp.concatenate([stats[:2].reshape(10, HD), part], 0)
    small = share(small, "cz", 8)
    part = jnp.sum(small[:, 10:], axis=0)
    stats = small[:, :10].reshape(8, 2, 640)[:, :, :GROUP].transpose(1, 0, 2)
    stats = stats.reshape(2, CHUNKS, CHUNK).transpose(1, 0, 2)

    out_q = exchange(after(out_q, small).reshape(4, ROWS, 2 * HD), "cy")
    attended, grad_queries = unpack(out_q, BF16, F32)
    part = jnp.sum(share(after(part, out_q), "cy", 4), axis=0)
    grads = share(part, FT, 8).reshape(160, 256)
    grad_long = grads[:128]
    grad_short = grads[128:152].reshape(3, 8, 256)[:, :7]

    out_k = key_pass(where, after(own_kv, grads), all_qd, stats)
    out_k = exchange(out_k.reshape(4, ROWS, 2 * HD), "cy")
    grad_keys, grad_values = unpack(out_k, F32, F32)
    return (
        mixed, attended, gfeat.transpose(1, 0, 2), grad_short, grad_long,
        grad_queries, grad_keys, grad_values,
    )


def solution(mesh):
    fine = Mesh(np.asarray(mesh.devices).reshape(8, 4, 4, 2), ("cz", "cy", "fsdp", "tp"))
    rows = P(CTX, FT)
    wide = P(CTX, None, FT)
    return jax.shard_map(
        body,
        mesh=fine,
        in_specs=(wide, P(), P(), rows, rows, rows, rows, rows),
        out_specs=(rows, rows, wide, P(), P(), rows, rows, rows),
        check_vma=False,
    )
```

```python
import jax
import jax.numpy as jnp
import numpy as np
from jax import lax
from jax.experimental import pallas as pl
from jax.experimental.pallas import tpu as pltpu
from jax.sharding import Mesh, PartitionSpec as P

HD = 128
ROWS = 144
GROUP = 576
SEQ = 4608
CHUNK = 512
CHUNKS = SEQ // CHUNK
LOG2E = 1.4426950408889634
SCALE = HD ** -0.5
VMEM_BYTES = 56 * 1024 * 1024
F32 = jnp.float32
BF16 = jnp.bfloat16
CTX = ("cz", "cy")
FT = ("fsdp", "tp")


def after(value, *others):
    return lax.optimization_barrier((value,) + others)[0]


def call(body, out_shape, name, **options):
    return pl.pallas_call(
        body,
        out_shape=out_shape,
        name=name,
        compiler_params=pltpu.CompilerParams(vmem_limit_bytes=VMEM_BYTES),
        **options,
    )


def struct(shape, dtype):
    return jax.ShapeDtypeStruct(shape, dtype)


def nt(a, b):
    return lax.dot_general(a, b, (((1,), (1,)), ((), ())), preferred_element_type=F32)


def nn(a, b):
    return lax.dot_general(a, b, (((1,), (0,)), ((), ())), preferred_element_type=F32)


def pack_body(*refs):
    out_ref = refs[-1]
    for h in range(4):
        for slot, ref in enumerate(refs[:-1]):
            out_ref[h, :, slot * HD : (slot + 1) * HD] = ref[:, h * HD : (h + 1) * HD]


def pack(*parts):
    return call(pack_body, struct((4, ROWS, len(parts) * HD), BF16), "pack")(*parts)


def unpack_body(x_ref, a_ref, b_ref):
    for h in range(4):
        a_ref[:, h * HD : (h + 1) * HD] = x_ref[h, :, :HD].astype(a_ref.dtype)
        b_ref[:, h * HD : (h + 1) * HD] = x_ref[h, :, HD:].astype(b_ref.dtype)


def unpack(x, kind_a, kind_b):
    return call(
        unpack_body,
        (struct((ROWS, 4 * HD), kind_a), struct((ROWS, 4 * HD), kind_b)),
        "unpack",
    )(x)


def hyena_body(
    feat_ref, prev_ref, next_ref, up_ref, short_ref, long_ref,
    mixed_ref, gfeat_ref, glong_ref, gshort_ref,
    x_ref, x1_ref, p_ref, ps_ref, gm_ref, gs_ref, f_ref, gf_ref, wb_ref, gl_ref,
):
    turn = pl.program_id(1)
    for slot, g in enumerate((0, 2)):
        x_ref[slot, 0:136] = prev_ref[g].astype(F32)
        x_ref[slot, 136:280] = feat_ref[g].astype(F32)
        x_ref[slot, 280:288] = next_ref[272 + 8 * slot : 280 + 8 * slot].astype(F32)
    x1_ref[0:136] = prev_ref[1].astype(F32)
    x1_ref[136:280] = feat_ref[1].astype(F32)
    x1_ref[280:416] = next_ref[0:136].astype(F32)
    taps = [[short_ref[g, s : s + 1, :] for s in range(7)] for g in range(3)]

    def featured(read, g):
        total = taps[g][0] * read(0)
        for s in range(1, 7):
            total = total + taps[g][s] * read(s)
        return total

    f0 = featured(lambda s: x_ref[0, 8 - s : 288 - s], 0)
    f2 = featured(lambda s: x_ref[1, 8 - s : 288 - s], 2)
    p_ref[8:288] = f0 * f2
    f_ref[0] = f0[128:280]
    f_ref[2] = f2[128:280]
    f1 = featured(lambda s: x1_ref[136 - s : 416 - s], 1)
    f_ref[1] = f1[0:152]
    gm_ref[0:144] = up_ref[...].astype(F32) * f1[0:144]
    gm_ref[144:280] = next_ref[136:272].astype(F32) * f1[144:280]
    for b in range(8):
        ps_ref[b, 16:288] = p_ref[16 - b : 288 - b]
        gs_ref[b] = gm_ref[b : 272 + b]
    wb_ref[...] = jnp.broadcast_to(long_ref[...][:, None, :], (128, 8, 128))

    def forward(a, total):
        base = pl.multiple_of(136 - 8 * a, 8)
        for b in range(8):
            tap = 8 * a + b
            x = ps_ref[b, pl.ds(base, 152), :].reshape(19, 8, 128)
            total = total + wb_ref[tap][None] * x
            gm = gm_ref[0:144].reshape(18, 8, 128)
            gl_ref[tap] = jnp.sum(gm * x[:18], axis=0)
        return total

    memory = lax.fori_loop(0, 16, forward, jnp.zeros((19, 8, 128), F32)).reshape(152, 128)
    mixed_ref[...] = (f_ref[1, 0:144] * memory[0:144]).astype(BF16)
    gf_ref[1, 0:144] = up_ref[...].astype(F32) * memory[0:144]
    gf_ref[1, 144:152] = next_ref[136:144].astype(F32) * memory[144:152]

    def backward(a, total):
        base = pl.multiple_of(8 * a, 8)
        for b in range(8):
            y = gs_ref[b, pl.ds(base, 152), :].reshape(19, 8, 128)
            total = total + wb_ref[8 * a + b][None] * y
        return total

    gp = lax.fori_loop(0, 16, backward, jnp.zeros((19, 8, 128), F32)).reshape(152, 128)
    gf_ref[0] = gp * f_ref[2]
    gf_ref[2] = gp * f_ref[0]
    glong = jnp.sum(gl_ref[...], axis=1)

    @pl.when(turn == 0)
    def _():
        glong_ref[...] = glong
        gshort_ref[...] = jnp.zeros_like(gshort_ref)

    @pl.when(turn != 0)
    def _():
        glong_ref[...] += glong

    for g in range(3):
        total = taps[g][0] * gf_ref[g, 0:144]
        for s in range(1, 7):
            total = total + taps[g][s] * gf_ref[g, s : 144 + s]
        gfeat_ref[g] = total
        own = gf_ref[g, 0:144]
        for s in range(7):
            if g == 1:
                x = x1_ref[136 - s : 280 - s]
            else:
                x = x_ref[g // 2, 136 - s : 280 - s]
            column = jnp.sum((own * x).reshape(18, 8, 128), axis=0)
            gshort_ref[g, s : s + 1, :] += jnp.sum(column, axis=0, keepdims=True)


def hyena(feat, prev, nxt, up, short8, long_taps):
    def cols(*lead):
        return pl.BlockSpec(lead + (128,), lambda f, k: (0,) * len(lead) + (2 * k + f,))

    def filters(*lead):
        return pl.BlockSpec(lead + (128,), lambda f, k: (0,) * len(lead) + (f,))

    return call(
        hyena_body,
        (
            struct((ROWS, 512), BF16),
            struct((3, ROWS, 512), F32),
            struct((128, 256), F32),
            struct((3, 8, 256), F32),
        ),
        "hyena",
        grid=(2, 2),
        in_specs=[
            cols(3, ROWS), cols(3, 136), cols(288), cols(ROWS), filters(3, 8), filters(128),
        ],
        out_specs=(cols(ROWS), cols(3, ROWS), filters(128), filters(3, 8)),
        scratch_shapes=[
            pltpu.VMEM((2, 288, 128), F32),
            pltpu.VMEM((416, 128), F32),
            pltpu.VMEM((288, 128), F32),
            pltpu.VMEM((8, 288, 128), F32),
            pltpu.VMEM((280, 128), F32),
            pltpu.VMEM((8, 272, 128), F32),
            pltpu.VMEM((3, 152, 128), F32),
            pltpu.VMEM((3, 152, 128), F32),
            pltpu.VMEM((128, 8, 128), F32),
            pltpu.VMEM((128, 8, 128), F32),
        ],
    )(feat, prev, nxt, up, short8, long_taps)


def half(rows, side):
    return pl.BlockSpec((rows, 2 * HD), lambda i: (0, side), pipeline_mode=pl.Buffered(1))


def lane_max(x):
    best = x[:, 0:128]
    for j in range(1, CHUNK // 128):
        best = jnp.maximum(best, x[:, j * 128 : (j + 1) * 128])
    return best


def lane_sum(x):
    total = x[:, 0:128]
    for j in range(1, CHUNK // 128):
        total = total + x[:, j * 128 : (j + 1) * 128]
    return total


def query_body(where_ref, own_ref, kv_ref, out_ref, stat_ref, s_ref, mx_ref, l_ref, o_ref, st_ref):
    first = where_ref[0] * GROUP
    clear = first // CHUNK
    total = (first + GROUP + CHUNK - 1) // CHUNK
    mx_ref[...] = jnp.full_like(mx_ref, -jnp.inf)
    l_ref[...] = jnp.zeros_like(l_ref)
    o_ref[...] = jnp.zeros_like(o_ref)

    def rows_of(c):
        return pl.ds(pl.multiple_of(c * CHUNK, CHUNK), CHUNK)

    def scores(c, masked):
        s = nt(own_ref[:, :HD], kv_ref[rows_of(c), :HD]) * (SCALE * LOG2E)
        if masked:
            q = first + lax.broadcasted_iota(jnp.int32, (GROUP, CHUNK), 0)
            k = c * CHUNK + lax.broadcasted_iota(jnp.int32, (GROUP, CHUNK), 1)
            s = jnp.where(q >= k, s, -jnp.inf)
        s_ref[c] = s
        mx_ref[...] = jnp.maximum(mx_ref[...], lane_max(s))

    @pl.loop(0, clear)
    def _(c):
        scores(c, False)

    @pl.loop(clear, total)
    def _(c):
        scores(c, True)

    peak = jnp.max(mx_ref[...], axis=1, keepdims=True)

    @pl.loop(0, total)
    def _(c):
        p = jnp.exp2(s_ref[c] - peak)
        s_ref[c] = p
        l_ref[...] += lane_sum(p)
        o_ref[...] += nn(p.astype(BF16), kv_ref[rows_of(c), HD:])

    norm = jnp.sum(l_ref[...], axis=1, keepdims=True)
    inverse = 1.0 / norm
    attended = (o_ref[...] * inverse).astype(BF16)
    out_ref[:, :HD] = attended
    delta = jnp.sum(
        own_ref[:, HD:].astype(F32) * attended.astype(F32), axis=1, keepdims=True
    )
    o_ref[...] = jnp.zeros_like(o_ref)

    @pl.loop(0, total)
    def _(c):
        rows = rows_of(c)
        gw = nt(own_ref[:, HD:], kv_ref[rows, HD:])
        gs = (s_ref[c] * (gw - delta)).astype(BF16)
        o_ref[...] += nn(gs, kv_ref[rows, :HD])

    out_ref[:, HD:] = (o_ref[...] * (inverse * SCALE)).astype(BF16)
    lane = lax.broadcasted_iota(jnp.int32, (GROUP, HD), 1)
    st_ref[0:GROUP] = jnp.where(lane == 0, peak + jnp.log2(norm), delta)
    st_ref[GROUP:640] = jnp.zeros((640 - GROUP, HD), F32)
    stat_ref[...] = st_ref[...].T[0:8]


def query_pass(where, own, kv):
    return call(
        query_body,
        (struct((GROUP, 2 * HD), BF16), struct((8, 640), F32)),
        "query_pass",
        grid=(1,),
        in_specs=[
            pl.BlockSpec(memory_space=pltpu.SMEM),
            half(GROUP, 0),
            half(SEQ, 1),
        ],
        scratch_shapes=[
            pltpu.VMEM((CHUNKS, GROUP, CHUNK), F32),
            pltpu.VMEM((GROUP, HD), F32),
            pltpu.VMEM((GROUP, HD), F32),
            pltpu.VMEM((GROUP, HD), F32),
            pltpu.VMEM((640, HD), F32),
        ],
    )(where, own, kv)


def key_body(where_ref, own_ref, qd_ref, stat_ref, out_ref, gk_ref, gv_ref):
    first = where_ref[0] * GROUP
    begin = first // CHUNK
    clear = (first + GROUP - 1 + CHUNK - 1) // CHUNK
    gk_ref[...] = jnp.zeros_like(gk_ref)
    gv_ref[...] = jnp.zeros_like(gv_ref)

    def visit(c, masked):
        rows = pl.ds(pl.multiple_of(c * CHUNK, CHUNK), CHUNK)
        log_row = stat_ref[c, 0:1, :]
        delta_row = stat_ref[c, 1:2, :]
        q = qd_ref[rows, :HD]
        d = qd_ref[rows, HD:]
        s = nt(own_ref[:, :HD], q) * (SCALE * LOG2E)
        p = jnp.exp2(s - log_row)
        if masked:
            k_at = first + lax.broadcasted_iota(jnp.int32, (GROUP, CHUNK), 0)
            q_at = c * CHUNK + lax.broadcasted_iota(jnp.int32, (GROUP, CHUNK), 1)
            p = jnp.where(q_at >= k_at, p, 0.0)
        gv_ref[...] += nn(p.astype(BF16), d)
        gw = nt(own_ref[:, HD:], d)
        gs = (p * (gw - delta_row)).astype(BF16)
        gk_ref[...] += nn(gs, q)

    @pl.loop(begin, jnp.minimum(clear, CHUNKS))
    def _(c):
        visit(c, True)

    @pl.loop(clear, CHUNKS)
    def _(c):
        visit(c, False)

    out_ref[:, :HD] = (gk_ref[...] * SCALE).astype(BF16)
    out_ref[:, HD:] = gv_ref[...].astype(BF16)


def key_pass(where, own, qd, stats):
    return call(
        key_body,
        struct((GROUP, 2 * HD), BF16),
        "key_pass",
        grid=(1,),
        in_specs=[
            pl.BlockSpec(memory_space=pltpu.SMEM),
            half(GROUP, 1),
            half(SEQ, 0),
            pl.BlockSpec(memory_space=pltpu.VMEM),
        ],
        scratch_shapes=[pltpu.VMEM((GROUP, HD), F32), pltpu.VMEM((GROUP, HD), F32)],
    )(where, own, qd, stats)


def exchange(x, axis):
    return lax.all_to_all(x, axis, 0, 0, tiled=True)


def share(x, axis, count):
    return exchange(jnp.broadcast_to(x[None], (count,) + x.shape), axis)


def body(
    features, short_filter, long_filter_taps, queries, key_vectors, value_vectors,
    grad_mixed, grad_attended,
):
    feat = features.transpose(1, 0, 2)
    prev = lax.ppermute(feat[:, 8:], CTX, [(i, i + 1) for i in range(31)])
    rim = jnp.concatenate([feat[1, :136], grad_mixed[:136], feat[0, :8], feat[2, :8]], 0)
    nxt = lax.ppermute(rim, CTX, [(i + 1, i) for i in range(31)])

    where = lax.axis_index("cz").astype(jnp.int32).reshape(1)
    packed = pack(queries, grad_attended, key_vectors, value_vectors)
    own = exchange(packed, "cy").reshape(GROUP, 4 * HD)
    everything = lax.all_gather(own, "cz", axis=0, tiled=True)

    short8 = jnp.pad(short_filter, ((0, 0), (0, 1), (0, 0)))
    mixed, gfeat, glong, gshort = hyena(
        feat, prev, nxt, after(grad_mixed, own), short8, long_filter_taps
    )
    grads = jnp.concatenate([glong, gshort.reshape(24, 256), jnp.zeros((8, 256), F32)], 0)
    part = jnp.sum(exchange(grads.reshape(8, 40, HD), FT), axis=0)
    part = jnp.sum(share(part, "cz", 8), axis=0)
    part = jnp.sum(share(part, "cy", 4), axis=0)
    grads = share(part, FT, 8).reshape(160, 256)
    grad_long = grads[:128]
    grad_short = grads[128:152].reshape(3, 8, 256)[:, :7]

    out_q, stats = query_pass(where, after(own, grads), everything)
    stats = share(stats[:2, :GROUP], "cz", 8).transpose(1, 0, 2)
    stats = stats.reshape(2, CHUNKS, CHUNK).transpose(1, 0, 2)
    out_q = exchange(after(out_q, stats).reshape(4, ROWS, 2 * HD), "cy")

    out_k = key_pass(where, own, everything, stats)
    out_k = exchange(out_k.reshape(4, ROWS, 2 * HD), "cy")
    attended, grad_queries = unpack(out_q, BF16, F32)
    grad_keys, grad_values = unpack(out_k, F32, F32)
    return (
        mixed, attended, gfeat.transpose(1, 0, 2), grad_short, grad_long,
        grad_queries, grad_keys, grad_values,
    )


def solution(mesh):
    fine = Mesh(np.asarray(mesh.devices).reshape(8, 4, 4, 2), ("cz", "cy", "fsdp", "tp"))
    rows = P(CTX, FT)
    wide = P(CTX, None, FT)
    return jax.shard_map(
        body,
        mesh=fine,
        in_specs=(wide, P(), P(), rows, rows, rows, rows, rows),
        out_specs=(rows, rows, wide, P(), P(), rows, rows, rows),
        check_vma=False,
    )
```

```python
import functools

import jax
import jax.numpy as jnp
import numpy as np
from jax import lax
from jax.experimental import pallas as pl
from jax.experimental.pallas import tpu as pltpu
from jax.sharding import Mesh, PartitionSpec as P

HD = 128
ROWS = 144
GROUP = 576
KEYS = GROUP // 2
SEQ = 4608
CHUNK = 512
CHUNKS = SEQ // CHUNK
LOG2E = 1.4426950408889634
SCALE = HD ** -0.5
VMEM_BYTES = 56 * 1024 * 1024
F32 = jnp.float32
BF16 = jnp.bfloat16
CTX = ("cz", "cy")
FT = ("fsdp", "tp")
YFT = ("cy", "fsdp", "tp")


def after(value, *others):
    return lax.optimization_barrier((value,) + others)[0]


def call(body, out_shape, name, **options):
    return pl.pallas_call(
        body,
        out_shape=out_shape,
        name=name,
        compiler_params=pltpu.CompilerParams(vmem_limit_bytes=VMEM_BYTES),
        **options,
    )


def struct(shape, dtype):
    return jax.ShapeDtypeStruct(shape, dtype)


def nt(a, b):
    return lax.dot_general(a, b, (((1,), (1,)), ((), ())), preferred_element_type=F32)


def nn(a, b):
    return lax.dot_general(a, b, (((1,), (0,)), ((), ())), preferred_element_type=F32)


def pack_body(*refs):
    out_ref = refs[-1]
    for h in range(4):
        for slot, ref in enumerate(refs[:-1]):
            out_ref[h, :, slot * HD : (slot + 1) * HD] = ref[:, h * HD : (h + 1) * HD]


def pack(*parts):
    return call(pack_body, struct((4, ROWS, len(parts) * HD), BF16), "pack")(*parts)


def unpack_body(x_ref, a_ref, b_ref):
    for h in range(4):
        a_ref[:, h * HD : (h + 1) * HD] = x_ref[h, :, :HD].astype(a_ref.dtype)
        b_ref[:, h * HD : (h + 1) * HD] = x_ref[h, :, HD:].astype(b_ref.dtype)


def unpack(x, kind_a, kind_b):
    return call(
        unpack_body,
        (struct((ROWS, 4 * HD), kind_a), struct((ROWS, 4 * HD), kind_b)),
        "unpack",
    )(x)


def hyena_body(
    feat_ref, prev_ref, next_ref, up_ref, short_ref, long_ref,
    mixed_ref, gfeat_ref, glong_ref, gshort_ref,
    x_ref, x1_ref, p_ref, ps_ref, gm_ref, gs_ref, f_ref, gf_ref, wb_ref, gl_ref,
):
    turn = pl.program_id(1)
    for slot, g in enumerate((0, 2)):
        x_ref[slot, 0:136] = prev_ref[g].astype(F32)
        x_ref[slot, 136:280] = feat_ref[g].astype(F32)
        x_ref[slot, 280:288] = next_ref[272 + 8 * slot : 280 + 8 * slot].astype(F32)
    x1_ref[0:136] = prev_ref[1].astype(F32)
    x1_ref[136:280] = feat_ref[1].astype(F32)
    x1_ref[280:416] = next_ref[0:136].astype(F32)
    taps = [[short_ref[g, s : s + 1, :] for s in range(7)] for g in range(3)]

    def featured(read, g):
        total = taps[g][0] * read(0)
        for s in range(1, 7):
            total = total + taps[g][s] * read(s)
        return total

    f0 = featured(lambda s: x_ref[0, 8 - s : 288 - s], 0)
    f2 = featured(lambda s: x_ref[1, 8 - s : 288 - s], 2)
    p_ref[8:288] = f0 * f2
    f_ref[0] = f0[128:280]
    f_ref[2] = f2[128:280]
    f1 = featured(lambda s: x1_ref[136 - s : 416 - s], 1)
    f_ref[1] = f1[0:152]
    gm_ref[0:144] = up_ref[...].astype(F32) * f1[0:144]
    gm_ref[144:280] = next_ref[136:272].astype(F32) * f1[144:280]
    for b in range(8):
        ps_ref[b, 16:288] = p_ref[16 - b : 288 - b]
        gs_ref[b] = gm_ref[b : 272 + b]
    wb_ref[...] = jnp.broadcast_to(long_ref[...][:, None, :], (128, 8, 128))

    def forward(a, total):
        base = pl.multiple_of(136 - 8 * a, 8)
        for b in range(8):
            tap = 8 * a + b
            x = ps_ref[b, pl.ds(base, 152), :].reshape(19, 8, 128)
            total = total + wb_ref[tap][None] * x
            gm = gm_ref[0:144].reshape(18, 8, 128)
            gl_ref[tap] = jnp.sum(gm * x[:18], axis=0)
        return total

    memory = lax.fori_loop(0, 16, forward, jnp.zeros((19, 8, 128), F32)).reshape(152, 128)
    mixed_ref[...] = (f_ref[1, 0:144] * memory[0:144]).astype(BF16)
    gf_ref[1, 0:144] = up_ref[...].astype(F32) * memory[0:144]
    gf_ref[1, 144:152] = next_ref[136:144].astype(F32) * memory[144:152]

    def backward(a, total):
        base = pl.multiple_of(8 * a, 8)
        for b in range(8):
            y = gs_ref[b, pl.ds(base, 152), :].reshape(19, 8, 128)
            total = total + wb_ref[8 * a + b][None] * y
        return total

    gp = lax.fori_loop(0, 16, backward, jnp.zeros((19, 8, 128), F32)).reshape(152, 128)
    gf_ref[0] = gp * f_ref[2]
    gf_ref[2] = gp * f_ref[0]
    glong = jnp.sum(gl_ref[...], axis=1)

    @pl.when(turn == 0)
    def _():
        glong_ref[...] = glong
        gshort_ref[...] = jnp.zeros_like(gshort_ref)

    @pl.when(turn != 0)
    def _():
        glong_ref[...] += glong

    for g in range(3):
        total = taps[g][0] * gf_ref[g, 0:144]
        for s in range(1, 7):
            total = total + taps[g][s] * gf_ref[g, s : 144 + s]
        gfeat_ref[g] = total
        own = gf_ref[g, 0:144]
        for s in range(7):
            if g == 1:
                x = x1_ref[136 - s : 280 - s]
            else:
                x = x_ref[g // 2, 136 - s : 280 - s]
            column = jnp.sum((own * x).reshape(18, 8, 128), axis=0)
            gshort_ref[g, s : s + 1, :] += jnp.sum(column, axis=0, keepdims=True)


def hyena(feat, prev, nxt, up, short8, long_taps):
    def cols(*lead):
        return pl.BlockSpec(lead + (128,), lambda f, k: (0,) * len(lead) + (2 * k + f,))

    def filters(*lead):
        return pl.BlockSpec(lead + (128,), lambda f, k: (0,) * len(lead) + (f,))

    return call(
        hyena_body,
        (
            struct((ROWS, 512), BF16),
            struct((3, ROWS, 512), F32),
            struct((128, 256), F32),
            struct((3, 8, 256), F32),
        ),
        "hyena",
        grid=(2, 2),
        in_specs=[
            cols(3, ROWS), cols(3, 136), cols(288), cols(ROWS), filters(3, 8), filters(128),
        ],
        out_specs=(cols(ROWS), cols(3, ROWS), filters(128), filters(3, 8)),
        scratch_shapes=[
            pltpu.VMEM((2, 288, 128), F32),
            pltpu.VMEM((416, 128), F32),
            pltpu.VMEM((288, 128), F32),
            pltpu.VMEM((8, 288, 128), F32),
            pltpu.VMEM((280, 128), F32),
            pltpu.VMEM((8, 272, 128), F32),
            pltpu.VMEM((3, 152, 128), F32),
            pltpu.VMEM((3, 152, 128), F32),
            pltpu.VMEM((128, 8, 128), F32),
            pltpu.VMEM((128, 8, 128), F32),
        ],
    )(feat, prev, nxt, up, short8, long_taps)


def half(rows, side):
    return pl.BlockSpec((rows, 2 * HD), lambda i: (0, side), pipeline_mode=pl.Buffered(1))


def lane_max(x):
    best = x[:, 0:128]
    for j in range(1, CHUNK // 128):
        best = jnp.maximum(best, x[:, j * 128 : (j + 1) * 128])
    return best


def lane_sum(x):
    total = x[:, 0:128]
    for j in range(1, CHUNK // 128):
        total = total + x[:, j * 128 : (j + 1) * 128]
    return total


def query_body(where_ref, own_ref, kv_ref, out_ref, stat_ref, s_ref, mx_ref, l_ref, o_ref, st_ref):
    first = where_ref[0] * GROUP
    clear = first // CHUNK
    total = (first + GROUP + CHUNK - 1) // CHUNK
    mx_ref[...] = jnp.full_like(mx_ref, -jnp.inf)
    l_ref[...] = jnp.zeros_like(l_ref)
    o_ref[...] = jnp.zeros_like(o_ref)

    def rows_of(c):
        return pl.ds(pl.multiple_of(c * CHUNK, CHUNK), CHUNK)

    def scores(c, masked):
        s = nt(own_ref[:, :HD], kv_ref[rows_of(c), :HD]) * (SCALE * LOG2E)
        if masked:
            q = first + lax.broadcasted_iota(jnp.int32, (GROUP, CHUNK), 0)
            k = c * CHUNK + lax.broadcasted_iota(jnp.int32, (GROUP, CHUNK), 1)
            s = jnp.where(q >= k, s, -jnp.inf)
        s_ref[c] = s
        mx_ref[...] = jnp.maximum(mx_ref[...], lane_max(s))

    @pl.loop(0, clear)
    def _(c):
        scores(c, False)

    @pl.loop(clear, total)
    def _(c):
        scores(c, True)

    peak = jnp.max(mx_ref[...], axis=1, keepdims=True)

    @pl.loop(0, total)
    def _(c):
        p = jnp.exp2(s_ref[c] - peak)
        s_ref[c] = p
        l_ref[...] += lane_sum(p)
        o_ref[...] += nn(p.astype(BF16), kv_ref[rows_of(c), HD:])

    norm = jnp.sum(l_ref[...], axis=1, keepdims=True)
    inverse = 1.0 / norm
    attended = (o_ref[...] * inverse).astype(BF16)
    out_ref[:, :HD] = attended
    delta = jnp.sum(
        own_ref[:, HD:].astype(F32) * attended.astype(F32), axis=1, keepdims=True
    )
    o_ref[...] = jnp.zeros_like(o_ref)

    @pl.loop(0, total)
    def _(c):
        rows = rows_of(c)
        gw = nt(own_ref[:, HD:], kv_ref[rows, HD:])
        gs = (s_ref[c] * (gw - delta)).astype(BF16)
        o_ref[...] += nn(gs, kv_ref[rows, :HD])

    out_ref[:, HD:] = (o_ref[...] * (inverse * SCALE)).astype(BF16)
    lane = lax.broadcasted_iota(jnp.int32, (GROUP, HD), 1)
    st_ref[0:GROUP] = jnp.where(lane == 0, peak + jnp.log2(norm), delta)
    st_ref[GROUP:640] = jnp.zeros((640 - GROUP, HD), F32)
    stat_ref[...] = st_ref[...].T[0:8]


def query_pass(where, own, kv):
    return call(
        query_body,
        (struct((GROUP, 2 * HD), BF16), struct((8, 640), F32)),
        "query_pass",
        grid=(1,),
        in_specs=[
            pl.BlockSpec(memory_space=pltpu.SMEM),
            half(GROUP, 0),
            half(SEQ, 1),
        ],
        scratch_shapes=[
            pltpu.VMEM((CHUNKS, GROUP, CHUNK), F32),
            pltpu.VMEM((GROUP, HD), F32),
            pltpu.VMEM((GROUP, HD), F32),
            pltpu.VMEM((GROUP, HD), F32),
            pltpu.VMEM((640, HD), F32),
        ],
    )(where, own, kv)


def key_body(part, where_ref, own_ref, qd_ref, stat_ref, out_ref, gk_ref, gv_ref):
    first = where_ref[0] * GROUP + part * KEYS
    begin = first // CHUNK
    clear = (first + KEYS - 1 + CHUNK - 1) // CHUNK
    gk_ref[...] = jnp.zeros_like(gk_ref)
    gv_ref[...] = jnp.zeros_like(gv_ref)

    def visit(c, masked):
        rows = pl.ds(pl.multiple_of(c * CHUNK, CHUNK), CHUNK)
        log_row = stat_ref[c, 0:1, :]
        delta_row = stat_ref[c, 1:2, :]
        q = qd_ref[rows, :HD]
        d = qd_ref[rows, HD:]
        s = nt(own_ref[:, :HD], q) * (SCALE * LOG2E)
        p = jnp.exp2(s - log_row)
        if masked:
            k_at = first + lax.broadcasted_iota(jnp.int32, (KEYS, CHUNK), 0)
            q_at = c * CHUNK + lax.broadcasted_iota(jnp.int32, (KEYS, CHUNK), 1)
            p = jnp.where(q_at >= k_at, p, 0.0)
        gv_ref[...] += nn(p.astype(BF16), d)
        gw = nt(own_ref[:, HD:], d)
        gs = (p * (gw - delta_row)).astype(BF16)
        gk_ref[...] += nn(gs, q)

    @pl.loop(begin, jnp.minimum(clear, CHUNKS))
    def _(c):
        visit(c, True)

    @pl.loop(clear, CHUNKS)
    def _(c):
        visit(c, False)

    out_ref[:, :HD] = (gk_ref[...] * SCALE).astype(BF16)
    out_ref[:, HD:] = gv_ref[...].astype(BF16)


def key_pass(part, where, own, qd, stats):
    return call(
        functools.partial(key_body, part),
        struct((KEYS, 2 * HD), BF16),
        "key_pass",
        cost_estimate=pl.CostEstimate(
            flops=8 * KEYS * SEQ * HD, transcendentals=KEYS * SEQ, bytes_accessed=16 << 20
        ),
        grid=(1,),
        in_specs=[
            pl.BlockSpec(memory_space=pltpu.SMEM),
            pl.BlockSpec((KEYS, 2 * HD), lambda i: (part, 1)),
            half(SEQ, 0),
            pl.BlockSpec(memory_space=pltpu.VMEM),
        ],
        scratch_shapes=[pltpu.VMEM((KEYS, HD), F32), pltpu.VMEM((KEYS, HD), F32)],
    )(where, own, qd, stats)


def exchange(x, axis):
    return lax.all_to_all(x, axis, 0, 0, tiled=True)


def share(x, axis, count):
    return exchange(jnp.broadcast_to(x[None], (count,) + x.shape), axis)


def body(
    features, short_filter, long_filter_taps, queries, key_vectors, value_vectors,
    grad_mixed, grad_attended,
):
    feat = features.transpose(1, 0, 2)
    prev = lax.ppermute(feat[:, 8:], CTX, [(i, i + 1) for i in range(31)])
    rim = jnp.concatenate([feat[1, :136], grad_mixed[:136], feat[0, :8], feat[2, :8]], 0)
    nxt = lax.ppermute(rim, CTX, [(i + 1, i) for i in range(31)])

    where = lax.axis_index("cz").astype(jnp.int32).reshape(1)
    packed = pack(queries, grad_attended, key_vectors, value_vectors)
    own = exchange(packed, "cy").reshape(GROUP, 4 * HD)
    everything = lax.all_gather(own, "cz", axis=0, tiled=True)

    short8 = jnp.pad(short_filter, ((0, 0), (0, 1), (0, 0)))
    mixed, gfeat, glong, gshort = hyena(
        feat, prev, nxt, after(grad_mixed, own), short8, long_filter_taps
    )
    grads = jnp.concatenate([glong, gshort.reshape(24, 256), jnp.zeros((8, 256), F32)], 0)
    part = jnp.sum(exchange(grads.reshape(32, 10, HD), YFT), axis=0)

    out_q, stats = query_pass(where, after(own, part), everything)
    small = jnp.concatenate([stats[:2].reshape(10, HD), part], 0)
    small = share(small, "cz", 8)
    stats = small[:, :10].reshape(8, 2, 640)[:, :, :GROUP].transpose(1, 0, 2)
    stats = stats.reshape(2, CHUNKS, CHUNK).transpose(1, 0, 2)
    part = jnp.sum(small[:, 10:], axis=0)
    grads = share(part, YFT, 32).reshape(160, 256)
    grad_long = grads[:128]
    grad_short = grads[128:152].reshape(3, 8, 256)[:, :7]
    out_k0 = key_pass(0, where, own, everything, stats)
    out_q = exchange(out_q.reshape(4, ROWS, 2 * HD), "cy")
    out_k1 = key_pass(1, where, own, everything, stats)
    out_k = exchange(jnp.concatenate([out_k0, out_k1], 0).reshape(4, ROWS, 2 * HD), "cy")
    attended, grad_queries = unpack(out_q, BF16, F32)
    grad_keys, grad_values = unpack(out_k, F32, F32)
    return (
        mixed, attended, gfeat.transpose(1, 0, 2), grad_short, grad_long,
        grad_queries, grad_keys, grad_values,
    )


def solution(mesh):
    fine = Mesh(np.asarray(mesh.devices).reshape(8, 4, 4, 2), ("cz", "cy", "fsdp", "tp"))
    rows = P(CTX, FT)
    wide = P(CTX, None, FT)
    return jax.shard_map(
        body,
        mesh=fine,
        in_specs=(wide, P(), P(), rows, rows, rows, rows, rows),
        out_specs=(rows, rows, wide, P(), P(), rows, rows, rows),
        check_vma=False,
    )
```

```python
import jax
import jax.numpy as jnp
import numpy as np
from jax import lax
from jax.experimental import pallas as pl
from jax.experimental.pallas import tpu as pltpu
from jax.sharding import Mesh, PartitionSpec as P

HD = 128
ROWS = 144
GROUP = 576
SEQ = 4608
CHUNK = 512
CHUNKS = SEQ // CHUNK
LOG2E = 1.4426950408889634
SCALE = HD ** -0.5
VMEM_BYTES = 56 * 1024 * 1024
F32 = jnp.float32
BF16 = jnp.bfloat16
CTX = ("cz", "cy")
FT = ("fsdp", "tp")
YFT = ("cy", "fsdp", "tp")


def after(value, *others):
    return lax.optimization_barrier((value,) + others)[0]


def call(body, out_shape, name, **options):
    return pl.pallas_call(
        body,
        out_shape=out_shape,
        name=name,
        compiler_params=pltpu.CompilerParams(vmem_limit_bytes=VMEM_BYTES),
        **options,
    )


def struct(shape, dtype):
    return jax.ShapeDtypeStruct(shape, dtype)


def nt(a, b):
    return lax.dot_general(a, b, (((1,), (1,)), ((), ())), preferred_element_type=F32)


def nn(a, b):
    return lax.dot_general(a, b, (((1,), (0,)), ((), ())), preferred_element_type=F32)


def pack_body(*refs):
    out_ref = refs[-1]
    for h in range(4):
        for slot, ref in enumerate(refs[:-1]):
            out_ref[h, :, slot * HD : (slot + 1) * HD] = ref[:, h * HD : (h + 1) * HD]


def pack(*parts):
    return call(pack_body, struct((4, ROWS, len(parts) * HD), BF16), "pack")(*parts)


def unpack_body(x_ref, attended_ref, gq_ref, gk_ref, gv_ref, grads_ref):
    for h in range(4):
        at = slice(h * HD, (h + 1) * HD)
        attended_ref[:, at] = x_ref[h, :ROWS, 0:HD]
        gq_ref[:, at] = x_ref[h, :ROWS, HD : 2 * HD].astype(F32)
        gk_ref[:, at] = x_ref[h, :ROWS, 2 * HD : 3 * HD].astype(F32)
        gv_ref[:, at] = x_ref[h, :ROWS, 3 * HD :].astype(F32)
        for side in range(2):
            high = x_ref[h, ROWS:, side * HD : (side + 1) * HD].astype(F32)
            low = x_ref[h, ROWS:, (side + 2) * HD : (side + 3) * HD].astype(F32)
            grads_ref[h, side * 40 : (side + 1) * 40] = high + low


def unpack(x):
    whole = struct((ROWS, 4 * HD), F32)
    return call(
        unpack_body,
        (struct((ROWS, 4 * HD), BF16), whole, whole, whole, struct((4, 80, HD), F32)),
        "unpack",
    )(x)


def hyena_body(
    feat_ref, prev_ref, next_ref, up_ref, short_ref, long_ref,
    mixed_ref, gfeat_ref, glong_ref, gshort_ref,
    x_ref, x1_ref, p_ref, ps_ref, gm_ref, gs_ref, f_ref, gf_ref, wb_ref, gl_ref,
):
    turn = pl.program_id(1)
    for slot, g in enumerate((0, 2)):
        x_ref[slot, 0:136] = prev_ref[g].astype(F32)
        x_ref[slot, 136:280] = feat_ref[g].astype(F32)
        x_ref[slot, 280:288] = next_ref[272 + 8 * slot : 280 + 8 * slot].astype(F32)
    x1_ref[0:136] = prev_ref[1].astype(F32)
    x1_ref[136:280] = feat_ref[1].astype(F32)
    x1_ref[280:416] = next_ref[0:136].astype(F32)
    taps = [[short_ref[g, s : s + 1, :] for s in range(7)] for g in range(3)]

    def featured(read, g):
        total = taps[g][0] * read(0)
        for s in range(1, 7):
            total = total + taps[g][s] * read(s)
        return total

    f0 = featured(lambda s: x_ref[0, 8 - s : 288 - s], 0)
    f2 = featured(lambda s: x_ref[1, 8 - s : 288 - s], 2)
    p_ref[8:288] = f0 * f2
    f_ref[0] = f0[128:280]
    f_ref[2] = f2[128:280]
    f1 = featured(lambda s: x1_ref[136 - s : 416 - s], 1)
    f_ref[1] = f1[0:152]
    gm_ref[0:144] = up_ref[...].astype(F32) * f1[0:144]
    gm_ref[144:280] = next_ref[136:272].astype(F32) * f1[144:280]
    for b in range(8):
        ps_ref[b, 16:288] = p_ref[16 - b : 288 - b]
        gs_ref[b] = gm_ref[b : 272 + b]
    wb_ref[...] = jnp.broadcast_to(long_ref[...][:, None, :], (128, 8, 128))

    def forward(a, total):
        base = pl.multiple_of(136 - 8 * a, 8)
        for b in range(8):
            tap = 8 * a + b
            x = ps_ref[b, pl.ds(base, 152), :].reshape(19, 8, 128)
            total = total + wb_ref[tap][None] * x
            gm = gm_ref[0:144].reshape(18, 8, 128)
            gl_ref[tap] = jnp.sum(gm * x[:18], axis=0)
        return total

    memory = lax.fori_loop(0, 16, forward, jnp.zeros((19, 8, 128), F32)).reshape(152, 128)
    mixed_ref[...] = (f_ref[1, 0:144] * memory[0:144]).astype(BF16)
    gf_ref[1, 0:144] = up_ref[...].astype(F32) * memory[0:144]
    gf_ref[1, 144:152] = next_ref[136:144].astype(F32) * memory[144:152]

    def backward(a, total):
        base = pl.multiple_of(8 * a, 8)
        for b in range(8):
            y = gs_ref[b, pl.ds(base, 152), :].reshape(19, 8, 128)
            total = total + wb_ref[8 * a + b][None] * y
        return total

    gp = lax.fori_loop(0, 16, backward, jnp.zeros((19, 8, 128), F32)).reshape(152, 128)
    gf_ref[0] = gp * f_ref[2]
    gf_ref[2] = gp * f_ref[0]
    glong = jnp.sum(gl_ref[...], axis=1)

    @pl.when(turn == 0)
    def _():
        glong_ref[...] = glong
        gshort_ref[...] = jnp.zeros_like(gshort_ref)

    @pl.when(turn != 0)
    def _():
        glong_ref[...] += glong

    for g in range(3):
        total = taps[g][0] * gf_ref[g, 0:144]
        for s in range(1, 7):
            total = total + taps[g][s] * gf_ref[g, s : 144 + s]
        gfeat_ref[g] = total
        own = gf_ref[g, 0:144]
        for s in range(7):
            if g == 1:
                x = x1_ref[136 - s : 280 - s]
            else:
                x = x_ref[g // 2, 136 - s : 280 - s]
            column = jnp.sum((own * x).reshape(18, 8, 128), axis=0)
            gshort_ref[g, s : s + 1, :] += jnp.sum(column, axis=0, keepdims=True)


def hyena(feat, prev, nxt, up, short8, long_taps):
    def cols(*lead):
        return pl.BlockSpec(lead + (128,), lambda f, k: (0,) * len(lead) + (2 * k + f,))

    def filters(*lead):
        return pl.BlockSpec(lead + (128,), lambda f, k: (0,) * len(lead) + (f,))

    return call(
        hyena_body,
        (
            struct((ROWS, 512), BF16),
            struct((3, ROWS, 512), F32),
            struct((128, 256), F32),
            struct((3, 8, 256), F32),
        ),
        "hyena",
        grid=(2, 2),
        in_specs=[
            cols(3, ROWS), cols(3, 136), cols(288), cols(ROWS), filters(3, 8), filters(128),
        ],
        out_specs=(cols(ROWS), cols(3, ROWS), filters(128), filters(3, 8)),
        scratch_shapes=[
            pltpu.VMEM((2, 288, 128), F32),
            pltpu.VMEM((416, 128), F32),
            pltpu.VMEM((288, 128), F32),
            pltpu.VMEM((8, 288, 128), F32),
            pltpu.VMEM((280, 128), F32),
            pltpu.VMEM((8, 272, 128), F32),
            pltpu.VMEM((3, 152, 128), F32),
            pltpu.VMEM((3, 152, 128), F32),
            pltpu.VMEM((128, 8, 128), F32),
            pltpu.VMEM((128, 8, 128), F32),
        ],
    )(feat, prev, nxt, up, short8, long_taps)


def half(rows, side):
    return pl.BlockSpec((rows, 2 * HD), lambda i: (0, side), pipeline_mode=pl.Buffered(1))


def lane_max(x):
    best = x[:, 0:128]
    for j in range(1, CHUNK // 128):
        best = jnp.maximum(best, x[:, j * 128 : (j + 1) * 128])
    return best


def lane_sum(x):
    total = x[:, 0:128]
    for j in range(1, CHUNK // 128):
        total = total + x[:, j * 128 : (j + 1) * 128]
    return total


def query_body(where_ref, own_ref, kv_ref, out_ref, stat_ref, s_ref, mx_ref, l_ref, o_ref, st_ref):
    first = where_ref[0] * GROUP
    clear = first // CHUNK
    total = (first + GROUP + CHUNK - 1) // CHUNK
    mx_ref[...] = jnp.full_like(mx_ref, -jnp.inf)
    l_ref[...] = jnp.zeros_like(l_ref)
    o_ref[...] = jnp.zeros_like(o_ref)

    def rows_of(c):
        return pl.ds(pl.multiple_of(c * CHUNK, CHUNK), CHUNK)

    def scores(c, masked):
        s = nt(own_ref[:, :HD], kv_ref[rows_of(c), :HD]) * (SCALE * LOG2E)
        if masked:
            q = first + lax.broadcasted_iota(jnp.int32, (GROUP, CHUNK), 0)
            k = c * CHUNK + lax.broadcasted_iota(jnp.int32, (GROUP, CHUNK), 1)
            s = jnp.where(q >= k, s, -jnp.inf)
        s_ref[c] = s
        mx_ref[...] = jnp.maximum(mx_ref[...], lane_max(s))

    @pl.loop(0, clear)
    def _(c):
        scores(c, False)

    @pl.loop(clear, total)
    def _(c):
        scores(c, True)

    peak = jnp.max(mx_ref[...], axis=1, keepdims=True)

    @pl.loop(0, total)
    def _(c):
        p = jnp.exp2(s_ref[c] - peak)
        s_ref[c] = p
        l_ref[...] += lane_sum(p)
        o_ref[...] += nn(p.astype(BF16), kv_ref[rows_of(c), HD:])

    norm = jnp.sum(l_ref[...], axis=1, keepdims=True)
    inverse = 1.0 / norm
    attended = (o_ref[...] * inverse).astype(BF16)
    out_ref[:, :HD] = attended
    delta = jnp.sum(
        own_ref[:, HD:].astype(F32) * attended.astype(F32), axis=1, keepdims=True
    )
    o_ref[...] = jnp.zeros_like(o_ref)

    @pl.loop(0, total)
    def _(c):
        rows = rows_of(c)
        gw = nt(own_ref[:, HD:], kv_ref[rows, HD:])
        gs = (s_ref[c] * (gw - delta)).astype(BF16)
        o_ref[...] += nn(gs, kv_ref[rows, :HD])

    out_ref[:, HD:] = (o_ref[...] * (inverse * SCALE)).astype(BF16)
    lane = lax.broadcasted_iota(jnp.int32, (GROUP, HD), 1)
    st_ref[0:GROUP] = jnp.where(lane == 0, peak + jnp.log2(norm), delta)
    st_ref[GROUP:640] = jnp.zeros((640 - GROUP, HD), F32)
    stat_ref[...] = st_ref[...].T[0:8]


def query_pass(where, own, kv):
    return call(
        query_body,
        (struct((GROUP, 2 * HD), BF16), struct((8, 640), F32)),
        "query_pass",
        grid=(1,),
        in_specs=[
            pl.BlockSpec(memory_space=pltpu.SMEM),
            half(GROUP, 0),
            half(SEQ, 1),
        ],
        scratch_shapes=[
            pltpu.VMEM((CHUNKS, GROUP, CHUNK), F32),
            pltpu.VMEM((GROUP, HD), F32),
            pltpu.VMEM((GROUP, HD), F32),
            pltpu.VMEM((GROUP, HD), F32),
            pltpu.VMEM((640, HD), F32),
        ],
    )(where, own, kv)


def key_body(where_ref, own_ref, qd_ref, stat_ref, oq_ref, part_ref, out_ref, gk_ref, gv_ref):
    first = where_ref[0] * GROUP
    begin = first // CHUNK
    clear = (first + GROUP - 1 + CHUNK - 1) // CHUNK
    gk_ref[...] = jnp.zeros_like(gk_ref)
    gv_ref[...] = jnp.zeros_like(gv_ref)

    def visit(c, masked):
        rows = pl.ds(pl.multiple_of(c * CHUNK, CHUNK), CHUNK)
        log_row = stat_ref[c, 0:1, :]
        delta_row = stat_ref[c, 1:2, :]
        q = qd_ref[rows, :HD]
        d = qd_ref[rows, HD:]
        s = nt(own_ref[:, :HD], q) * (SCALE * LOG2E)
        p = jnp.exp2(s - log_row)
        if masked:
            k_at = first + lax.broadcasted_iota(jnp.int32, (GROUP, CHUNK), 0)
            q_at = c * CHUNK + lax.broadcasted_iota(jnp.int32, (GROUP, CHUNK), 1)
            p = jnp.where(q_at >= k_at, p, 0.0)
        gv_ref[...] += nn(p.astype(BF16), d)
        gw = nt(own_ref[:, HD:], d)
        gs = (p * (gw - delta_row)).astype(BF16)
        gk_ref[...] += nn(gs, q)

    @pl.loop(begin, jnp.minimum(clear, CHUNKS))
    def _(c):
        visit(c, True)

    @pl.loop(clear, CHUNKS)
    def _(c):
        visit(c, False)

    for j in range(4):
        at = slice(j * ROWS, (j + 1) * ROWS)
        out_ref[j, :ROWS, : 2 * HD] = oq_ref[at]
        out_ref[j, :ROWS, 2 * HD : 3 * HD] = (gk_ref[at] * SCALE).astype(BF16)
        out_ref[j, :ROWS, 3 * HD :] = gv_ref[at].astype(BF16)
        for side in range(2):
            value = part_ref[side * 40 : (side + 1) * 40]
            high = value.astype(BF16)
            out_ref[j, ROWS:, side * HD : (side + 1) * HD] = high
            low = (value - high.astype(F32)).astype(BF16)
            out_ref[j, ROWS:, (side + 2) * HD : (side + 3) * HD] = low


def key_pass(where, own, qd, stats, out_q, part):
    return call(
        key_body,
        struct((4, ROWS + 40, 4 * HD), BF16),
        "key_pass",
        cost_estimate=pl.CostEstimate(
            flops=8 * GROUP * SEQ * HD, transcendentals=GROUP * SEQ, bytes_accessed=16 << 20
        ),
        grid=(1,),
        in_specs=[
            pl.BlockSpec(memory_space=pltpu.SMEM),
            half(GROUP, 1),
            half(SEQ, 0),
            pl.BlockSpec(memory_space=pltpu.VMEM),
            pl.BlockSpec(memory_space=pltpu.VMEM),
            pl.BlockSpec(memory_space=pltpu.VMEM),
        ],
        scratch_shapes=[pltpu.VMEM((GROUP, HD), F32), pltpu.VMEM((GROUP, HD), F32)],
    )(where, own, qd, stats, out_q, part)


def exchange(x, axis):
    return lax.all_to_all(x, axis, 0, 0, tiled=True)


def share(x, axis, count):
    return exchange(jnp.broadcast_to(x[None], (count,) + x.shape), axis)


def body(
    features, short_filter, long_filter_taps, queries, key_vectors, value_vectors,
    grad_mixed, grad_attended,
):
    feat = features.transpose(1, 0, 2)
    prev = lax.ppermute(feat[:, 8:], CTX, [(i, i + 1) for i in range(31)])
    rim = jnp.concatenate([feat[1, :136], grad_mixed[:136], feat[0, :8], feat[2, :8]], 0)
    nxt = lax.ppermute(rim, CTX, [(i + 1, i) for i in range(31)])

    where = lax.axis_index("cz").astype(jnp.int32).reshape(1)
    packed = pack(queries, grad_attended, key_vectors, value_vectors)
    own = exchange(packed, "cy").reshape(GROUP, 4 * HD)
    own, prev, nxt = lax.optimization_barrier((own, prev, nxt))
    everything = lax.all_gather(own, "cz", axis=0, tiled=True)

    short8 = jnp.pad(short_filter, ((0, 0), (0, 1), (0, 0)))
    mixed, gfeat, glong, gshort = hyena(
        feat, prev, nxt, after(grad_mixed, own), short8, long_filter_taps
    )
    grads = jnp.concatenate([glong, gshort.reshape(24, 256), jnp.zeros((8, 256), F32)], 0)
    part = jnp.sum(exchange(grads.reshape(32, 10, HD), YFT), axis=0)
    part = jnp.sum(share(part, "cz", 8), axis=0)
    part = share(part, FT, 8)

    out_q, stats = query_pass(where, after(own, part), everything)
    stats = share(stats[:2, :GROUP], "cz", 8).transpose(1, 0, 2)
    stats = stats.reshape(2, CHUNKS, CHUNK).transpose(1, 0, 2)
    result = key_pass(where, own, everything, stats, out_q, part.reshape(80, HD))
    attended, grad_queries, grad_keys, grad_values, grads = unpack(exchange(result, "cy"))
    grads = grads.reshape(160, 256)
    grad_long = grads[:128]
    grad_short = grads[128:152].reshape(3, 8, 256)[:, :7]
    return (
        mixed, attended, gfeat.transpose(1, 0, 2), grad_short, grad_long,
        grad_queries, grad_keys, grad_values,
    )


def solution(mesh):
    fine = Mesh(np.asarray(mesh.devices).reshape(8, 4, 4, 2), ("cz", "cy", "fsdp", "tp"))
    rows = P(CTX, FT)
    wide = P(CTX, None, FT)
    return jax.shard_map(
        body,
        mesh=fine,
        in_specs=(wide, P(), P(), rows, rows, rows, rows, rows),
        out_specs=(rows, rows, wide, P(), P(), rows, rows, rows),
        check_vma=False,
    )
```

```python
import jax
import jax.numpy as jnp
import numpy as np
from jax import lax
from jax.experimental import pallas as pl
from jax.experimental.pallas import tpu as pltpu
from jax.sharding import Mesh, PartitionSpec as P

HD = 128
ROWS = 144
GROUP = 576
SEQ = 4608
CHUNK = 512
CHUNKS = SEQ // CHUNK
LOG2E = 1.4426950408889634
SCALE = HD ** -0.5
VMEM_BYTES = 56 * 1024 * 1024
F32 = jnp.float32
BF16 = jnp.bfloat16
CTX = ("cz", "cy")
FT = ("fsdp", "tp")
YFT = ("cy", "fsdp", "tp")


def after(value, *others):
    return lax.optimization_barrier((value,) + others)[0]


def call(body, out_shape, name, **options):
    return pl.pallas_call(
        body,
        out_shape=out_shape,
        name=name,
        compiler_params=pltpu.CompilerParams(vmem_limit_bytes=VMEM_BYTES),
        **options,
    )


def struct(shape, dtype):
    return jax.ShapeDtypeStruct(shape, dtype)


def nt(a, b):
    return lax.dot_general(a, b, (((1,), (1,)), ((), ())), preferred_element_type=F32)


def nn(a, b):
    return lax.dot_general(a, b, (((1,), (0,)), ((), ())), preferred_element_type=F32)


def pack_body(*refs):
    out_ref = refs[-1]
    for h in range(4):
        for slot, ref in enumerate(refs[:-1]):
            out_ref[h, :, slot * HD : (slot + 1) * HD] = ref[:, h * HD : (h + 1) * HD]


def pack(*parts):
    return call(pack_body, struct((4, ROWS, len(parts) * HD), BF16), "pack")(*parts)


def unpack_body(x_ref, attended_ref, gq_ref, gk_ref, gv_ref, grads_ref):
    for h in range(4):
        at = slice(h * HD, (h + 1) * HD)
        attended_ref[:, at] = x_ref[h, :ROWS, 0:HD]
        gq_ref[:, at] = x_ref[h, :ROWS, HD : 2 * HD].astype(F32)
        gk_ref[:, at] = x_ref[h, :ROWS, 2 * HD : 3 * HD].astype(F32)
        gv_ref[:, at] = x_ref[h, :ROWS, 3 * HD :].astype(F32)
        for side in range(2):
            high = x_ref[h, ROWS:, side * HD : (side + 1) * HD].astype(F32)
            low = x_ref[h, ROWS:, (side + 2) * HD : (side + 3) * HD].astype(F32)
            grads_ref[h, side * 40 : (side + 1) * 40] = high + low


def unpack(x):
    whole = struct((ROWS, 4 * HD), F32)
    return call(
        unpack_body,
        (struct((ROWS, 4 * HD), BF16), whole, whole, whole, struct((4, 80, HD), F32)),
        "unpack",
    )(x)


def hyena_body(feat_ref, prev_ref, next_ref, up_ref, short_ref, long_ref, *refs):
    (
        mixed_ref, gfeat_ref, glong_ref, gshort_ref,
        x_ref, x1_ref, p_ref, ps_ref, gm_ref, gs_ref, f_ref, gf_ref, wb_ref, gl_ref,
    ) = refs[-14:]
    turn = pl.program_id(0)
    for slot, g in enumerate((0, 2)):
        x_ref[slot, 0:136] = prev_ref[g].astype(F32)
        x_ref[slot, 136:280] = feat_ref[g].astype(F32)
        x_ref[slot, 280:288] = next_ref[272 + 8 * slot : 280 + 8 * slot].astype(F32)
    x1_ref[0:136] = prev_ref[1].astype(F32)
    x1_ref[136:280] = feat_ref[1].astype(F32)
    x1_ref[280:416] = next_ref[0:136].astype(F32)
    taps = [[short_ref[g, s : s + 1, :] for s in range(7)] for g in range(3)]

    def featured(read, g):
        total = taps[g][0] * read(0)
        for s in range(1, 7):
            total = total + taps[g][s] * read(s)
        return total

    f0 = featured(lambda s: x_ref[0, 8 - s : 288 - s], 0)
    f2 = featured(lambda s: x_ref[1, 8 - s : 288 - s], 2)
    p_ref[8:288] = f0 * f2
    f_ref[0] = f0[128:280]
    f_ref[2] = f2[128:280]
    f1 = featured(lambda s: x1_ref[136 - s : 416 - s], 1)
    f_ref[1] = f1[0:152]
    gm_ref[0:144] = up_ref[...].astype(F32) * f1[0:144]
    gm_ref[144:280] = next_ref[136:272].astype(F32) * f1[144:280]
    for b in range(8):
        ps_ref[b, 16:288] = p_ref[16 - b : 288 - b]
        gs_ref[b] = gm_ref[b : 272 + b]
    wb_ref[...] = jnp.broadcast_to(long_ref[...][:, None, :], (128, 8, 128))

    def forward(a, total):
        base = pl.multiple_of(136 - 8 * a, 8)
        for b in range(8):
            tap = 8 * a + b
            x = ps_ref[b, pl.ds(base, 152), :].reshape(19, 8, 128)
            total = total + wb_ref[tap][None] * x
            gm = gm_ref[0:144].reshape(18, 8, 128)
            gl_ref[tap] = jnp.sum(gm * x[:18], axis=0)
        return total

    memory = lax.fori_loop(0, 16, forward, jnp.zeros((19, 8, 128), F32)).reshape(152, 128)
    mixed_ref[...] = (f_ref[1, 0:144] * memory[0:144]).astype(BF16)
    gf_ref[1, 0:144] = up_ref[...].astype(F32) * memory[0:144]
    gf_ref[1, 144:152] = next_ref[136:144].astype(F32) * memory[144:152]

    def backward(a, total):
        base = pl.multiple_of(8 * a, 8)
        for b in range(8):
            y = gs_ref[b, pl.ds(base, 152), :].reshape(19, 8, 128)
            total = total + wb_ref[8 * a + b][None] * y
        return total

    gp = lax.fori_loop(0, 16, backward, jnp.zeros((19, 8, 128), F32)).reshape(152, 128)
    gf_ref[0] = gp * f_ref[2]
    gf_ref[2] = gp * f_ref[0]
    glong = jnp.sum(gl_ref[...], axis=1)

    @pl.when(turn == 0)
    def _():
        glong_ref[...] = glong
        gshort_ref[...] = jnp.zeros_like(gshort_ref)

    @pl.when(turn != 0)
    def _():
        glong_ref[...] += glong

    for g in range(3):
        total = taps[g][0] * gf_ref[g, 0:144]
        for s in range(1, 7):
            total = total + taps[g][s] * gf_ref[g, s : 144 + s]
        gfeat_ref[g] = total
        own = gf_ref[g, 0:144]
        for s in range(7):
            if g == 1:
                x = x1_ref[136 - s : 280 - s]
            else:
                x = x_ref[g // 2, 136 - s : 280 - s]
            column = jnp.sum((own * x).reshape(18, 8, 128), axis=0)
            gshort_ref[g, s : s + 1, :] += jnp.sum(column, axis=0, keepdims=True)


def hyena(side, feat, prev, nxt, up, short8, long_taps, earlier):
    def cols(*lead):
        return pl.BlockSpec(lead + (128,), lambda k: (0,) * len(lead) + (2 * k + side,))

    def filters(*lead):
        return pl.BlockSpec(lead + (128,), lambda k: (0,) * len(lead) + (side,))

    def sums(*lead):
        return pl.BlockSpec(lead + (128,), lambda k: (0,) * (len(lead) + 1))

    kept = pl.BlockSpec(memory_space=pl.ANY)
    return call(
        hyena_body,
        (
            struct((ROWS, 512), BF16),
            struct((3, ROWS, 512), F32),
            struct((128, 128), F32),
            struct((3, 8, 128), F32),
        ),
        "hyena",
        grid=(2,),
        in_specs=[
            cols(3, ROWS), cols(3, 136), cols(288), cols(ROWS), filters(3, 8), filters(128),
        ] + [kept] * len(earlier),
        out_specs=(cols(ROWS), cols(3, ROWS), sums(128), sums(3, 8)),
        input_output_aliases={6 + i: i for i in range(len(earlier))},
        scratch_shapes=[
            pltpu.VMEM((2, 288, 128), F32),
            pltpu.VMEM((416, 128), F32),
            pltpu.VMEM((288, 128), F32),
            pltpu.VMEM((8, 288, 128), F32),
            pltpu.VMEM((280, 128), F32),
            pltpu.VMEM((8, 272, 128), F32),
            pltpu.VMEM((3, 152, 128), F32),
            pltpu.VMEM((3, 152, 128), F32),
            pltpu.VMEM((128, 8, 128), F32),
            pltpu.VMEM((128, 8, 128), F32),
        ],
    )(feat, prev, nxt, up, short8, long_taps, *earlier)


def assemble(where_ref, pieces, out_ref, step):
    for t, piece in enumerate(pieces):
        block = where_ref[0] + step * t

        @pl.when((block >= 0) & (block < len(pieces)))
        def _():
            out_ref[pl.ds(pl.multiple_of(block * GROUP, 64), GROUP), :] = piece[...]

    spare = where_ref[0] - step

    @pl.when((spare >= 0) & (spare < len(pieces)))
    def _():
        out_ref[pl.ds(pl.multiple_of(spare * GROUP, 64), GROUP), :] = jnp.zeros(
            (GROUP, 2 * HD), BF16
        )


def lane_max(x):
    best = x[:, 0:128]
    for j in range(1, CHUNK // 128):
        best = jnp.maximum(best, x[:, j * 128 : (j + 1) * 128])
    return best


def lane_sum(x):
    total = x[:, 0:128]
    for j in range(1, CHUNK // 128):
        total = total + x[:, j * 128 : (j + 1) * 128]
    return total


def query_body(where_ref, own_ref, *refs):
    out_ref, stat_ref, s_ref, mx_ref, l_ref, o_ref, st_ref, kv_ref = refs[8:]
    assemble(where_ref, refs[:8], kv_ref, -1)
    first = where_ref[0] * GROUP
    clear = first // CHUNK
    total = (first + GROUP + CHUNK - 1) // CHUNK
    mx_ref[...] = jnp.full_like(mx_ref, -jnp.inf)
    l_ref[...] = jnp.zeros_like(l_ref)
    o_ref[...] = jnp.zeros_like(o_ref)

    def rows_of(c):
        return pl.ds(pl.multiple_of(c * CHUNK, CHUNK), CHUNK)

    def scores(c, masked):
        s = nt(own_ref[:, :HD], kv_ref[rows_of(c), :HD]) * (SCALE * LOG2E)
        if masked:
            q = first + lax.broadcasted_iota(jnp.int32, (GROUP, CHUNK), 0)
            k = c * CHUNK + lax.broadcasted_iota(jnp.int32, (GROUP, CHUNK), 1)
            s = jnp.where(q >= k, s, -jnp.inf)
        s_ref[c] = s
        mx_ref[...] = jnp.maximum(mx_ref[...], lane_max(s))

    @pl.loop(0, clear)
    def _(c):
        scores(c, False)

    @pl.loop(clear, total)
    def _(c):
        scores(c, True)

    peak = jnp.max(mx_ref[...], axis=1, keepdims=True)

    @pl.loop(0, total)
    def _(c):
        p = jnp.exp2(s_ref[c] - peak)
        s_ref[c] = p
        l_ref[...] += lane_sum(p)
        o_ref[...] += nn(p.astype(BF16), kv_ref[rows_of(c), HD:])

    norm = jnp.sum(l_ref[...], axis=1, keepdims=True)
    inverse = 1.0 / norm
    attended = (o_ref[...] * inverse).astype(BF16)
    out_ref[:, :HD] = attended
    delta = jnp.sum(
        own_ref[:, HD:].astype(F32) * attended.astype(F32), axis=1, keepdims=True
    )
    o_ref[...] = jnp.zeros_like(o_ref)

    @pl.loop(0, total)
    def _(c):
        rows = rows_of(c)
        gw = nt(own_ref[:, HD:], kv_ref[rows, HD:])
        gs = (s_ref[c] * (gw - delta)).astype(BF16)
        o_ref[...] += nn(gs, kv_ref[rows, :HD])

    out_ref[:, HD:] = (o_ref[...] * (inverse * SCALE)).astype(BF16)
    lane = lax.broadcasted_iota(jnp.int32, (GROUP, HD), 1)
    st_ref[0:GROUP] = jnp.where(lane == 0, peak + jnp.log2(norm), delta)
    st_ref[GROUP:640] = jnp.zeros((640 - GROUP, HD), F32)
    stat_ref[...] = st_ref[...].T[0:8]


def query_pass(where, own, kv):
    return call(
        query_body,
        (struct((GROUP, 2 * HD), BF16), struct((8, 640), F32)),
        "query_pass",
        in_specs=[pl.BlockSpec(memory_space=pltpu.SMEM)]
        + [pl.BlockSpec(memory_space=pltpu.VMEM)] * 9,
        scratch_shapes=[
            pltpu.VMEM((CHUNKS, GROUP, CHUNK), F32),
            pltpu.VMEM((GROUP, HD), F32),
            pltpu.VMEM((GROUP, HD), F32),
            pltpu.VMEM((GROUP, HD), F32),
            pltpu.VMEM((640, HD), F32),
            pltpu.VMEM((SEQ, 2 * HD), BF16),
        ],
    )(where, own, *kv)


def key_body(where_ref, own_ref, stat_ref, oq_ref, part_ref, *refs):
    out_ref, gk_ref, gv_ref, qd_ref = refs[8:]
    assemble(where_ref, refs[:8], qd_ref, 1)
    first = where_ref[0] * GROUP
    begin = first // CHUNK
    clear = (first + GROUP - 1 + CHUNK - 1) // CHUNK
    gk_ref[...] = jnp.zeros_like(gk_ref)
    gv_ref[...] = jnp.zeros_like(gv_ref)

    def visit(c, masked):
        rows = pl.ds(pl.multiple_of(c * CHUNK, CHUNK), CHUNK)
        log_row = stat_ref[c, 0:1, :]
        delta_row = stat_ref[c, 1:2, :]
        q = qd_ref[rows, :HD]
        d = qd_ref[rows, HD:]
        s = nt(own_ref[:, :HD], q) * (SCALE * LOG2E)
        p = jnp.exp2(s - log_row)
        if masked:
            k_at = first + lax.broadcasted_iota(jnp.int32, (GROUP, CHUNK), 0)
            q_at = c * CHUNK + lax.broadcasted_iota(jnp.int32, (GROUP, CHUNK), 1)
            p = jnp.where(q_at >= k_at, p, 0.0)
        gv_ref[...] += nn(p.astype(BF16), d)
        gw = nt(own_ref[:, HD:], d)
        gs = (p * (gw - delta_row)).astype(BF16)
        gk_ref[...] += nn(gs, q)

    @pl.loop(begin, jnp.minimum(clear, CHUNKS))
    def _(c):
        visit(c, True)

    @pl.loop(clear, CHUNKS)
    def _(c):
        visit(c, False)

    for j in range(4):
        at = slice(j * ROWS, (j + 1) * ROWS)
        out_ref[j, :ROWS, : 2 * HD] = oq_ref[at]
        out_ref[j, :ROWS, 2 * HD : 3 * HD] = (gk_ref[at] * SCALE).astype(BF16)
        out_ref[j, :ROWS, 3 * HD :] = gv_ref[at].astype(BF16)
        for side in range(2):
            value = part_ref[side * 40 : (side + 1) * 40]
            high = value.astype(BF16)
            out_ref[j, ROWS:, side * HD : (side + 1) * HD] = high
            low = (value - high.astype(F32)).astype(BF16)
            out_ref[j, ROWS:, (side + 2) * HD : (side + 3) * HD] = low


def key_pass(where, own, qd, stats, out_q, part):
    return call(
        key_body,
        struct((4, ROWS + 40, 4 * HD), BF16),
        "key_pass",
        in_specs=[pl.BlockSpec(memory_space=pltpu.SMEM)]
        + [pl.BlockSpec(memory_space=pltpu.VMEM)] * 12,
        scratch_shapes=[
            pltpu.VMEM((GROUP, HD), F32),
            pltpu.VMEM((GROUP, HD), F32),
            pltpu.VMEM((SEQ, 2 * HD), BF16),
        ],
    )(where, own, stats, out_q, part, *qd)


def exchange(x, axis):
    return lax.all_to_all(x, axis, 0, 0, tiled=True)


def share(x, axis, count):
    return exchange(jnp.broadcast_to(x[None], (count,) + x.shape), axis)


def body(
    features, short_filter, long_filter_taps, queries, key_vectors, value_vectors,
    grad_mixed, grad_attended,
):
    feat = features.transpose(1, 0, 2)
    prev = lax.ppermute(feat[:, 8:], CTX, [(i, i + 1) for i in range(31)])
    rim = jnp.concatenate([feat[1, :136], grad_mixed[:136], feat[0, :8], feat[2, :8]], 0)
    nxt = lax.ppermute(rim, CTX, [(i + 1, i) for i in range(31)])

    where = lax.axis_index("cz").astype(jnp.int32).reshape(1)
    packed = pack(queries, grad_attended, key_vectors, value_vectors)
    own = exchange(packed, "cy").reshape(GROUP, 4 * HD)
    kv = [own[:, 2 * HD :]]
    qd = [own[:, : 2 * HD]]

    def step():
        t = len(kv)
        kv.append(lax.ppermute(kv[-1], "cz", [(i, i + 1) for i in range(t - 1, 7)]))
        qd.append(lax.ppermute(qd[-1], "cz", [(i, i - 1) for i in range(1, 9 - t)]))

    def order(*values):
        held = lax.optimization_barrier((kv[-1], qd[-1]) + values)
        kv[-1], qd[-1] = held[:2]
        return held[2:]

    short8 = jnp.pad(short_filter, ((0, 0), (0, 1), (0, 0)))
    step()
    prev, nxt = order(prev, nxt)
    step()
    first = hyena(0, feat, prev, nxt, grad_mixed, short8, long_filter_taps, ())
    first = order(*first)
    step()
    second = hyena(1, feat, prev, nxt, grad_mixed, short8, long_filter_taps, first[:2])
    mixed, gfeat, glong, gshort = order(*second)
    glong = jnp.concatenate([first[2], glong], 1)
    gshort = jnp.concatenate([first[3], gshort], 2).reshape(24, 256)
    grads = jnp.concatenate([glong, gshort, jnp.zeros((8, 256), F32)], 0)
    step()
    part = jnp.sum(exchange(grads.reshape(32, 10, HD), YFT), axis=0)
    (part,) = order(part)
    step()
    part = jnp.sum(share(part, "cz", 8), axis=0)
    (part,) = order(part)
    step()
    part = share(part, FT, 8)
    (part,) = order(part)
    step()

    out_q, stats = query_pass(where, qd[0], kv)
    stats = share(stats[:2, :GROUP], "cz", 8).transpose(1, 0, 2)
    stats = stats.reshape(2, CHUNKS, CHUNK).transpose(1, 0, 2)
    result = key_pass(where, kv[0], qd, stats, out_q, part.reshape(80, HD))
    attended, grad_queries, grad_keys, grad_values, grads = unpack(exchange(result, "cy"))
    grads = grads.reshape(160, 256)
    grad_long = grads[:128]
    grad_short = grads[128:152].reshape(3, 8, 256)[:, :7]
    return (
        mixed, attended, gfeat.transpose(1, 0, 2), grad_short, grad_long,
        grad_queries, grad_keys, grad_values,
    )


def solution(mesh):
    fine = Mesh(np.asarray(mesh.devices).reshape(8, 4, 4, 2), ("cz", "cy", "fsdp", "tp"))
    rows = P(CTX, FT)
    wide = P(CTX, None, FT)
    return jax.shard_map(
        body,
        mesh=fine,
        in_specs=(wide, P(), P(), rows, rows, rows, rows, rows),
        out_specs=(rows, rows, wide, P(), P(), rows, rows, rows),
        check_vma=False,
    )
```

```python
import jax
import jax.numpy as jnp
import numpy as np
from jax import lax
from jax.experimental import pallas as pl
from jax.experimental.pallas import tpu as pltpu
from jax.sharding import Mesh, PartitionSpec as P

HD = 128
ROWS = 144
GROUP = 576
SEQ = 4608
CHUNK = 512
CHUNKS = SEQ // CHUNK
LOG2E = 1.4426950408889634
SCALE = HD ** -0.5
VMEM_BYTES = 56 * 1024 * 1024
F32 = jnp.float32
BF16 = jnp.bfloat16
CTX = ("cz", "cy")
FT = ("fsdp", "tp")
YFT = ("cy", "fsdp", "tp")


def after(value, *others):
    return lax.optimization_barrier((value,) + others)[0]


def call(body, out_shape, name, **options):
    return pl.pallas_call(
        body,
        out_shape=out_shape,
        name=name,
        compiler_params=pltpu.CompilerParams(vmem_limit_bytes=VMEM_BYTES),
        **options,
    )


def struct(shape, dtype):
    return jax.ShapeDtypeStruct(shape, dtype)


def nt(a, b):
    return lax.dot_general(a, b, (((1,), (1,)), ((), ())), preferred_element_type=F32)


def nn(a, b):
    return lax.dot_general(a, b, (((1,), (0,)), ((), ())), preferred_element_type=F32)


def pack_body(*refs):
    out_ref = refs[-1]
    for h in range(4):
        for slot, ref in enumerate(refs[:-1]):
            out_ref[h, :, slot * HD : (slot + 1) * HD] = ref[:, h * HD : (h + 1) * HD]


def pack(*parts):
    return call(pack_body, struct((4, ROWS, len(parts) * HD), BF16), "pack")(*parts)


def unpack_body(x_ref, attended_ref, gq_ref, gk_ref, gv_ref, grads_ref):
    for h in range(4):
        at = slice(h * HD, (h + 1) * HD)
        attended_ref[:, at] = x_ref[h, :ROWS, 0:HD]
        gq_ref[:, at] = x_ref[h, :ROWS, HD : 2 * HD].astype(F32)
        gk_ref[:, at] = x_ref[h, :ROWS, 2 * HD : 3 * HD].astype(F32)
        gv_ref[:, at] = x_ref[h, :ROWS, 3 * HD :].astype(F32)
        for side in range(2):
            high = x_ref[h, ROWS:, side * HD : (side + 1) * HD].astype(F32)
            low = x_ref[h, ROWS:, (side + 2) * HD : (side + 3) * HD].astype(F32)
            grads_ref[h, side * 40 : (side + 1) * 40] = high + low


def unpack(x):
    whole = struct((ROWS, 4 * HD), F32)
    return call(
        unpack_body,
        (struct((ROWS, 4 * HD), BF16), whole, whole, whole, struct((4, 80, HD), F32)),
        "unpack",
    )(x)


def hyena_body(feat_ref, prev_ref, next_ref, up_ref, short_ref, long_ref, *refs):
    (
        mixed_ref, gfeat_ref, glong_ref, gshort_ref,
        x_ref, x1_ref, p_ref, ps_ref, gm_ref, gs_ref, f_ref, gf_ref, wb_ref, gl_ref,
    ) = refs[-14:]
    for slot, g in enumerate((0, 2)):
        x_ref[slot, 0:136] = prev_ref[g].astype(F32)
        x_ref[slot, 136:280] = feat_ref[g].astype(F32)
        x_ref[slot, 280:288] = next_ref[272 + 8 * slot : 280 + 8 * slot].astype(F32)
    x1_ref[0:136] = prev_ref[1].astype(F32)
    x1_ref[136:280] = feat_ref[1].astype(F32)
    x1_ref[280:416] = next_ref[0:136].astype(F32)
    taps = [[short_ref[g, s : s + 1, :] for s in range(7)] for g in range(3)]

    def featured(read, g):
        total = taps[g][0] * read(0)
        for s in range(1, 7):
            total = total + taps[g][s] * read(s)
        return total

    f0 = featured(lambda s: x_ref[0, 8 - s : 288 - s], 0)
    f2 = featured(lambda s: x_ref[1, 8 - s : 288 - s], 2)
    p_ref[8:288] = f0 * f2
    f_ref[0] = f0[128:280]
    f_ref[2] = f2[128:280]
    f1 = featured(lambda s: x1_ref[136 - s : 416 - s], 1)
    f_ref[1] = f1[0:152]
    gm_ref[0:144] = up_ref[...].astype(F32) * f1[0:144]
    gm_ref[144:280] = next_ref[136:272].astype(F32) * f1[144:280]
    for b in range(8):
        ps_ref[b, 16:288] = p_ref[16 - b : 288 - b]
        gs_ref[b] = gm_ref[b : 272 + b]
    wb_ref[...] = jnp.broadcast_to(long_ref[...][:, None, :], (128, 8, 128))

    def forward(a, total):
        base = pl.multiple_of(136 - 8 * a, 8)
        for b in range(8):
            tap = 8 * a + b
            x = ps_ref[b, pl.ds(base, 152), :].reshape(19, 8, 128)
            total = total + wb_ref[tap][None] * x
            gm = gm_ref[0:144].reshape(18, 8, 128)
            gl_ref[tap] = jnp.sum(gm * x[:18], axis=0)
        return total

    memory = lax.fori_loop(0, 16, forward, jnp.zeros((19, 8, 128), F32)).reshape(152, 128)
    mixed_ref[...] = (f_ref[1, 0:144] * memory[0:144]).astype(BF16)
    gf_ref[1, 0:144] = up_ref[...].astype(F32) * memory[0:144]
    gf_ref[1, 144:152] = next_ref[136:144].astype(F32) * memory[144:152]

    def backward(a, total):
        base = pl.multiple_of(8 * a, 8)
        for b in range(8):
            y = gs_ref[b, pl.ds(base, 152), :].reshape(19, 8, 128)
            total = total + wb_ref[8 * a + b][None] * y
        return total

    gp = lax.fori_loop(0, 16, backward, jnp.zeros((19, 8, 128), F32)).reshape(152, 128)
    gf_ref[0] = gp * f_ref[2]
    gf_ref[2] = gp * f_ref[0]
    glong_ref[...] = jnp.sum(gl_ref[...], axis=1)
    gshort_ref[...] = jnp.zeros_like(gshort_ref)
    for g in range(3):
        total = taps[g][0] * gf_ref[g, 0:144]
        for s in range(1, 7):
            total = total + taps[g][s] * gf_ref[g, s : 144 + s]
        gfeat_ref[g] = total
        own = gf_ref[g, 0:144]
        for s in range(7):
            if g == 1:
                x = x1_ref[136 - s : 280 - s]
            else:
                x = x_ref[g // 2, 136 - s : 280 - s]
            column = jnp.sum((own * x).reshape(18, 8, 128), axis=0)
            gshort_ref[g, s : s + 1, :] = jnp.sum(column, axis=0, keepdims=True)


def hyena(tile, feat, prev, nxt, up, short8, long_taps, earlier):
    def cols(*lead):
        return pl.BlockSpec(lead + (128,), lambda k: (0,) * len(lead) + (tile,))

    def filters(*lead):
        return pl.BlockSpec(lead + (128,), lambda k: (0,) * len(lead) + (tile % 2,))

    def sums(*lead):
        return pl.BlockSpec(lead + (128,), lambda k: (0,) * (len(lead) + 1))

    kept = pl.BlockSpec(memory_space=pl.ANY)
    return call(
        hyena_body,
        (
            struct((ROWS, 512), BF16),
            struct((3, ROWS, 512), F32),
            struct((128, 128), F32),
            struct((3, 8, 128), F32),
        ),
        "hyena",
        grid=(1,),
        in_specs=[
            cols(3, ROWS), cols(3, 136), cols(288), cols(ROWS), filters(3, 8), filters(128),
        ] + [kept] * len(earlier),
        out_specs=(cols(ROWS), cols(3, ROWS), sums(128), sums(3, 8)),
        input_output_aliases={6 + i: i for i in range(len(earlier))},
        scratch_shapes=[
            pltpu.VMEM((2, 288, 128), F32),
            pltpu.VMEM((416, 128), F32),
            pltpu.VMEM((288, 128), F32),
            pltpu.VMEM((8, 288, 128), F32),
            pltpu.VMEM((280, 128), F32),
            pltpu.VMEM((8, 272, 128), F32),
            pltpu.VMEM((3, 152, 128), F32),
            pltpu.VMEM((3, 152, 128), F32),
            pltpu.VMEM((128, 8, 128), F32),
            pltpu.VMEM((128, 8, 128), F32),
        ],
    )(feat, prev, nxt, up, short8, long_taps, *earlier)


def assemble(where_ref, pieces, out_ref, step):
    for t, piece in enumerate(pieces):
        block = where_ref[0] + step * t

        @pl.when((block >= 0) & (block < len(pieces)))
        def _():
            out_ref[pl.ds(pl.multiple_of(block * GROUP, 64), GROUP), :] = piece[...]

    spare = where_ref[0] - step

    @pl.when((spare >= 0) & (spare < len(pieces)))
    def _():
        out_ref[pl.ds(pl.multiple_of(spare * GROUP, 64), GROUP), :] = jnp.zeros(
            (GROUP, 2 * HD), BF16
        )


def lane_max(x):
    best = x[:, 0:128]
    for j in range(1, CHUNK // 128):
        best = jnp.maximum(best, x[:, j * 128 : (j + 1) * 128])
    return best


def lane_sum(x):
    total = x[:, 0:128]
    for j in range(1, CHUNK // 128):
        total = total + x[:, j * 128 : (j + 1) * 128]
    return total


def query_body(where_ref, own_ref, *refs):
    out_ref, stat_ref, s_ref, mx_ref, l_ref, o_ref, st_ref, kv_ref = refs[8:]
    assemble(where_ref, refs[:8], kv_ref, -1)
    first = where_ref[0] * GROUP
    clear = first // CHUNK
    total = (first + GROUP + CHUNK - 1) // CHUNK
    mx_ref[...] = jnp.full_like(mx_ref, -jnp.inf)
    l_ref[...] = jnp.zeros_like(l_ref)
    o_ref[...] = jnp.zeros_like(o_ref)

    def rows_of(c):
        return pl.ds(pl.multiple_of(c * CHUNK, CHUNK), CHUNK)

    def scores(c, masked):
        s = nt(own_ref[:, :HD], kv_ref[rows_of(c), :HD]) * (SCALE * LOG2E)
        if masked:
            q = first + lax.broadcasted_iota(jnp.int32, (GROUP, CHUNK), 0)
            k = c * CHUNK + lax.broadcasted_iota(jnp.int32, (GROUP, CHUNK), 1)
            s = jnp.where(q >= k, s, -jnp.inf)
        s_ref[c] = s
        mx_ref[...] = jnp.maximum(mx_ref[...], lane_max(s))

    @pl.loop(0, clear)
    def _(c):
        scores(c, False)

    @pl.loop(clear, total)
    def _(c):
        scores(c, True)

    peak = jnp.max(mx_ref[...], axis=1, keepdims=True)

    @pl.loop(0, total)
    def _(c):
        p = jnp.exp2(s_ref[c] - peak)
        s_ref[c] = p
        l_ref[...] += lane_sum(p)
        o_ref[...] += nn(p.astype(BF16), kv_ref[rows_of(c), HD:])

    norm = jnp.sum(l_ref[...], axis=1, keepdims=True)
    inverse = 1.0 / norm
    attended = (o_ref[...] * inverse).astype(BF16)
    out_ref[:, :HD] = attended
    delta = jnp.sum(
        own_ref[:, HD:].astype(F32) * attended.astype(F32), axis=1, keepdims=True
    )
    o_ref[...] = jnp.zeros_like(o_ref)

    @pl.loop(0, total)
    def _(c):
        rows = rows_of(c)
        gw = nt(own_ref[:, HD:], kv_ref[rows, HD:])
        gs = (s_ref[c] * (gw - delta)).astype(BF16)
        o_ref[...] += nn(gs, kv_ref[rows, :HD])

    out_ref[:, HD:] = (o_ref[...] * (inverse * SCALE)).astype(BF16)
    lane = lax.broadcasted_iota(jnp.int32, (GROUP, HD), 1)
    st_ref[0:GROUP] = jnp.where(lane == 0, peak + jnp.log2(norm), delta)
    st_ref[GROUP:640] = jnp.zeros((640 - GROUP, HD), F32)
    stat_ref[...] = st_ref[...].T[0:8]


def query_pass(where, own, kv):
    return call(
        query_body,
        (struct((GROUP, 2 * HD), BF16), struct((8, 640), F32)),
        "query_pass",
        in_specs=[pl.BlockSpec(memory_space=pltpu.SMEM)]
        + [pl.BlockSpec(memory_space=pltpu.VMEM)] * 9,
        scratch_shapes=[
            pltpu.VMEM((CHUNKS, GROUP, CHUNK), F32),
            pltpu.VMEM((GROUP, HD), F32),
            pltpu.VMEM((GROUP, HD), F32),
            pltpu.VMEM((GROUP, HD), F32),
            pltpu.VMEM((640, HD), F32),
            pltpu.VMEM((SEQ, 2 * HD), BF16),
        ],
    )(where, own, *kv)


def key_body(where_ref, own_ref, stat_ref, *refs):
    out_ref, gk_ref, gv_ref, qd_ref = refs[8:]
    assemble(where_ref, refs[:8], qd_ref, 1)
    first = where_ref[0] * GROUP
    begin = first // CHUNK
    clear = (first + GROUP - 1 + CHUNK - 1) // CHUNK
    gk_ref[...] = jnp.zeros_like(gk_ref)
    gv_ref[...] = jnp.zeros_like(gv_ref)

    def visit(c, masked):
        rows = pl.ds(pl.multiple_of(c * CHUNK, CHUNK), CHUNK)
        log_row = stat_ref[c, 0:1, :]
        delta_row = stat_ref[c, 1:2, :]
        q = qd_ref[rows, :HD]
        d = qd_ref[rows, HD:]
        s = nt(own_ref[:, :HD], q) * (SCALE * LOG2E)
        p = jnp.exp2(s - log_row)
        if masked:
            k_at = first + lax.broadcasted_iota(jnp.int32, (GROUP, CHUNK), 0)
            q_at = c * CHUNK + lax.broadcasted_iota(jnp.int32, (GROUP, CHUNK), 1)
            p = jnp.where(q_at >= k_at, p, 0.0)
        gv_ref[...] += nn(p.astype(BF16), d)
        gw = nt(own_ref[:, HD:], d)
        gs = (p * (gw - delta_row)).astype(BF16)
        gk_ref[...] += nn(gs, q)

    @pl.loop(begin, jnp.minimum(clear, CHUNKS))
    def _(c):
        visit(c, True)

    @pl.loop(clear, CHUNKS)
    def _(c):
        visit(c, False)

    out_ref[:, :HD] = (gk_ref[...] * SCALE).astype(BF16)
    out_ref[:, HD:] = gv_ref[...].astype(BF16)


def join_body(oq_ref, ok_ref, part_ref, out_ref):
    for j in range(4):
        at = slice(j * ROWS, (j + 1) * ROWS)
        out_ref[j, :ROWS, : 2 * HD] = oq_ref[at]
        out_ref[j, :ROWS, 2 * HD :] = ok_ref[at]
        for side in range(2):
            value = part_ref[side * 40 : (side + 1) * 40]
            high = value.astype(BF16)
            out_ref[j, ROWS:, side * HD : (side + 1) * HD] = high
            low = (value - high.astype(F32)).astype(BF16)
            out_ref[j, ROWS:, (side + 2) * HD : (side + 3) * HD] = low


def join(out_q, out_k, part):
    return call(join_body, struct((4, ROWS + 40, 4 * HD), BF16), "join")(out_q, out_k, part)


def key_pass(where, own, qd, stats):
    return call(
        key_body,
        struct((GROUP, 2 * HD), BF16),
        "key_pass",
        in_specs=[pl.BlockSpec(memory_space=pltpu.SMEM)]
        + [pl.BlockSpec(memory_space=pltpu.VMEM)] * 10,
        scratch_shapes=[
            pltpu.VMEM((GROUP, HD), F32),
            pltpu.VMEM((GROUP, HD), F32),
            pltpu.VMEM((SEQ, 2 * HD), BF16),
        ],
    )(where, own, stats, *qd)


def exchange(x, axis):
    return lax.all_to_all(x, axis, 0, 0, tiled=True)


def share(x, axis, count):
    return exchange(jnp.broadcast_to(x[None], (count,) + x.shape), axis)


def body(
    features, short_filter, long_filter_taps, queries, key_vectors, value_vectors,
    grad_mixed, grad_attended,
):
    where = lax.axis_index("cz").astype(jnp.int32).reshape(1)
    packed = pack(queries, grad_attended, key_vectors, value_vectors)
    own = exchange(packed, "cy").reshape(GROUP, 4 * HD)
    kv = [own[:, 2 * HD :]]
    qd = [own[:, : 2 * HD]]

    features, upstream = after(features, own), after(grad_mixed, own)
    feat = features.transpose(1, 0, 2)
    prev = lax.ppermute(feat[:, 8:], CTX, [(i, i + 1) for i in range(31)])
    rim = jnp.concatenate([feat[1, :136], upstream[:136], feat[0, :8], feat[2, :8]], 0)
    nxt = lax.ppermute(rim, CTX, [(i + 1, i) for i in range(31)])

    def step():
        t = len(kv)
        kv.append(lax.ppermute(kv[-1], "cz", [(i, i + 1) for i in range(t - 1, 7)]))
        qd.append(lax.ppermute(qd[-1], "cz", [(i, i - 1) for i in range(1, 9 - t)]))

    def order(*values):
        held = lax.optimization_barrier((kv[-1], qd[-1]) + values)
        kv[-1], qd[-1] = held[:2]
        return held[2:]

    short8 = jnp.pad(short_filter, ((0, 0), (0, 1), (0, 0)))
    step()
    prev, nxt = order(prev, nxt)
    kept = ()
    glong, gshort = [], []
    for tile in range(4):
        step()
        done = hyena(tile, feat, prev, nxt, upstream, short8, long_filter_taps, kept)
        done = order(*done)
        kept = done[:2]
        glong.append(done[2])
        gshort.append(done[3].reshape(24, HD))
    mixed, gfeat = kept
    grads = jnp.concatenate(
        [
            jnp.concatenate([glong[0] + glong[2], glong[1] + glong[3]], 1),
            jnp.concatenate([gshort[0] + gshort[2], gshort[1] + gshort[3]], 1),
            jnp.zeros((8, 256), F32),
        ],
        0,
    )
    part = jnp.sum(exchange(grads.reshape(32, 10, HD), YFT), axis=0)
    step()
    order()
    step()
    order()

    out_q, stats = query_pass(where, qd[0], kv)
    small = jnp.concatenate([stats[:2].reshape(10, HD), part], 0)
    small = share(small, "cz", 8)
    part = share(jnp.sum(small[:, 10:], axis=0), FT, 8)
    stats = small[:, :10].reshape(8, 2, 640)[:, :, :GROUP].transpose(1, 0, 2)
    stats = stats.reshape(2, CHUNKS, CHUNK).transpose(1, 0, 2)
    out_k = key_pass(where, kv[0], qd, stats)
    result = join(out_q, out_k, part.reshape(80, HD))
    attended, grad_queries, grad_keys, grad_values, grads = unpack(exchange(result, "cy"))
    grads = grads.reshape(160, 256)
    grad_long = grads[:128]
    grad_short = grads[128:152].reshape(3, 8, 256)[:, :7]
    return (
        mixed, attended, gfeat.transpose(1, 0, 2), grad_short, grad_long,
        grad_queries, grad_keys, grad_values,
    )


def solution(mesh):
    fine = Mesh(np.asarray(mesh.devices).reshape(8, 4, 4, 2), ("cz", "cy", "fsdp", "tp"))
    rows = P(CTX, FT)
    wide = P(CTX, None, FT)
    return jax.shard_map(
        body,
        mesh=fine,
        in_specs=(wide, P(), P(), rows, rows, rows, rows, rows),
        out_specs=(rows, rows, wide, P(), P(), rows, rows, rows),
        check_vma=False,
    )
```

```python
import jax
import jax.numpy as jnp
import numpy as np
from jax import lax
from jax.experimental import pallas as pl
from jax.experimental.pallas import tpu as pltpu
from jax.sharding import Mesh, PartitionSpec as P

HD = 128
ROWS = 144
GROUP = 576
SEQ = 4608
CHUNK = 512
CHUNKS = SEQ // CHUNK
LOG2E = 1.4426950408889634
SCALE = HD ** -0.5
VMEM_BYTES = 56 * 1024 * 1024
F32 = jnp.float32
BF16 = jnp.bfloat16
CTX = ("cz", "cy")
FT = ("fsdp", "tp")
YFT = ("cy", "fsdp", "tp")


def after(value, *others):
    return lax.optimization_barrier((value,) + others)[0]


def call(body, out_shape, name, **options):
    return pl.pallas_call(
        body,
        out_shape=out_shape,
        name=name,
        compiler_params=pltpu.CompilerParams(vmem_limit_bytes=VMEM_BYTES),
        **options,
    )


def struct(shape, dtype):
    return jax.ShapeDtypeStruct(shape, dtype)


def nt(a, b):
    return lax.dot_general(a, b, (((1,), (1,)), ((), ())), preferred_element_type=F32)


def nn(a, b):
    return lax.dot_general(a, b, (((1,), (0,)), ((), ())), preferred_element_type=F32)


def pack_body(*refs):
    out_ref = refs[-1]
    for h in range(4):
        for slot, ref in enumerate(refs[:-1]):
            out_ref[h, :, slot * HD : (slot + 1) * HD] = ref[:, h * HD : (h + 1) * HD]


def pack(*parts):
    return call(pack_body, struct((4, ROWS, len(parts) * HD), BF16), "pack")(*parts)


def unpack_body(x_ref, attended_ref, gq_ref, gk_ref, gv_ref, grads_ref):
    for h in range(4):
        at = slice(h * HD, (h + 1) * HD)
        attended_ref[:, at] = x_ref[h, :ROWS, 0:HD]
        gq_ref[:, at] = x_ref[h, :ROWS, HD : 2 * HD].astype(F32)
        gk_ref[:, at] = x_ref[h, :ROWS, 2 * HD : 3 * HD].astype(F32)
        gv_ref[:, at] = x_ref[h, :ROWS, 3 * HD :].astype(F32)
        for side in range(2):
            high = x_ref[h, ROWS:, side * HD : (side + 1) * HD].astype(F32)
            low = x_ref[h, ROWS:, (side + 2) * HD : (side + 3) * HD].astype(F32)
            grads_ref[h, side * 40 : (side + 1) * 40] = high + low


def unpack(x):
    whole = struct((ROWS, 4 * HD), F32)
    return call(
        unpack_body,
        (struct((ROWS, 4 * HD), BF16), whole, whole, whole, struct((4, 80, HD), F32)),
        "unpack",
    )(x)


def hyena_body(feat_ref, prev_ref, next_ref, up_ref, short_ref, long_ref, *refs):
    (
        mixed_ref, gfeat_ref, glong_ref, gshort_ref,
        x_ref, x1_ref, p_ref, ps_ref, gm_ref, gs_ref, f_ref, gf_ref, wb_ref, gl_ref,
    ) = refs[-14:]
    turn = pl.program_id(0)
    for slot, g in enumerate((0, 2)):
        x_ref[slot, 0:136] = prev_ref[g].astype(F32)
        x_ref[slot, 136:280] = feat_ref[g].astype(F32)
        x_ref[slot, 280:288] = next_ref[272 + 8 * slot : 280 + 8 * slot].astype(F32)
    x1_ref[0:136] = prev_ref[1].astype(F32)
    x1_ref[136:280] = feat_ref[1].astype(F32)
    x1_ref[280:416] = next_ref[0:136].astype(F32)
    taps = [[short_ref[g, s : s + 1, :] for s in range(7)] for g in range(3)]

    def featured(read, g):
        total = taps[g][0] * read(0)
        for s in range(1, 7):
            total = total + taps[g][s] * read(s)
        return total

    f0 = featured(lambda s: x_ref[0, 8 - s : 288 - s], 0)
    f2 = featured(lambda s: x_ref[1, 8 - s : 288 - s], 2)
    p_ref[8:288] = f0 * f2
    f_ref[0] = f0[128:280]
    f_ref[2] = f2[128:280]
    f1 = featured(lambda s: x1_ref[136 - s : 416 - s], 1)
    f_ref[1] = f1[0:152]
    gm_ref[0:144] = up_ref[...].astype(F32) * f1[0:144]
    gm_ref[144:280] = next_ref[136:272].astype(F32) * f1[144:280]
    for b in range(8):
        ps_ref[b, 16:288] = p_ref[16 - b : 288 - b]
        gs_ref[b] = gm_ref[b : 272 + b]
    wb_ref[...] = jnp.broadcast_to(long_ref[...][:, None, :], (128, 8, 128))

    def forward(a, total):
        base = pl.multiple_of(136 - 8 * a, 8)
        for b in range(8):
            tap = 8 * a + b
            x = ps_ref[b, pl.ds(base, 152), :].reshape(19, 8, 128)
            total = total + wb_ref[tap][None] * x
            gm = gm_ref[0:144].reshape(18, 8, 128)
            gl_ref[tap] = jnp.sum(gm * x[:18], axis=0)
        return total

    memory = lax.fori_loop(0, 16, forward, jnp.zeros((19, 8, 128), F32)).reshape(152, 128)
    mixed_ref[...] = (f_ref[1, 0:144] * memory[0:144]).astype(BF16)
    gf_ref[1, 0:144] = up_ref[...].astype(F32) * memory[0:144]
    gf_ref[1, 144:152] = next_ref[136:144].astype(F32) * memory[144:152]

    def backward(a, total):
        base = pl.multiple_of(8 * a, 8)
        for b in range(8):
            y = gs_ref[b, pl.ds(base, 152), :].reshape(19, 8, 128)
            total = total + wb_ref[8 * a + b][None] * y
        return total

    gp = lax.fori_loop(0, 16, backward, jnp.zeros((19, 8, 128), F32)).reshape(152, 128)
    gf_ref[0] = gp * f_ref[2]
    gf_ref[2] = gp * f_ref[0]
    glong = jnp.sum(gl_ref[...], axis=1)

    @pl.when(turn == 0)
    def _():
        glong_ref[...] = glong
        gshort_ref[...] = jnp.zeros_like(gshort_ref)

    @pl.when(turn != 0)
    def _():
        glong_ref[...] += glong

    for g in range(3):
        total = taps[g][0] * gf_ref[g, 0:144]
        for s in range(1, 7):
            total = total + taps[g][s] * gf_ref[g, s : 144 + s]
        gfeat_ref[g] = total
        own = gf_ref[g, 0:144]
        for s in range(7):
            if g == 1:
                x = x1_ref[136 - s : 280 - s]
            else:
                x = x_ref[g // 2, 136 - s : 280 - s]
            column = jnp.sum((own * x).reshape(18, 8, 128), axis=0)
            gshort_ref[g, s : s + 1, :] += jnp.sum(column, axis=0, keepdims=True)


def hyena(side, feat, prev, nxt, up, short8, long_taps, earlier):
    def cols(*lead):
        return pl.BlockSpec(lead + (128,), lambda k: (0,) * len(lead) + (2 * k + side,))

    def filters(*lead):
        return pl.BlockSpec(lead + (128,), lambda k: (0,) * len(lead) + (side,))

    def sums(*lead):
        return pl.BlockSpec(lead + (128,), lambda k: (0,) * (len(lead) + 1))

    kept = pl.BlockSpec(memory_space=pl.ANY)
    return call(
        hyena_body,
        (
            struct((ROWS, 512), BF16),
            struct((3, ROWS, 512), F32),
            struct((128, 128), F32),
            struct((3, 8, 128), F32),
        ),
        "hyena",
        grid=(2,),
        in_specs=[
            cols(3, ROWS), cols(3, 136), cols(288), cols(ROWS), filters(3, 8), filters(128),
        ] + [kept] * len(earlier),
        out_specs=(cols(ROWS), cols(3, ROWS), sums(128), sums(3, 8)),
        input_output_aliases={6 + i: i for i in range(len(earlier))},
        scratch_shapes=[
            pltpu.VMEM((2, 288, 128), F32),
            pltpu.VMEM((416, 128), F32),
            pltpu.VMEM((288, 128), F32),
            pltpu.VMEM((8, 288, 128), F32),
            pltpu.VMEM((280, 128), F32),
            pltpu.VMEM((8, 272, 128), F32),
            pltpu.VMEM((3, 152, 128), F32),
            pltpu.VMEM((3, 152, 128), F32),
            pltpu.VMEM((128, 8, 128), F32),
            pltpu.VMEM((128, 8, 128), F32),
        ],
    )(feat, prev, nxt, up, short8, long_taps, *earlier)


PLACES = (0, -1, -2, -3, 1, 2, 3, 4)


def part_of(side):
    return pl.BlockSpec((GROUP, 2 * HD), lambda i: (0, side))


def assemble(where_ref, pieces, out_ref, below):
    z = where_ref[0]
    for place, piece in zip(PLACES, pieces):
        block = (z + place + 8) % 8
        needed = (block <= z) if below else (block >= z)

        @pl.when(needed)
        def _():
            out_ref[pl.ds(pl.multiple_of(block * GROUP, 64), GROUP), :] = piece[...]

    spare = z + 1 if below else z - 1

    @pl.when((spare >= 0) & (spare < 8))
    def _():
        out_ref[pl.ds(pl.multiple_of(spare * GROUP, 64), GROUP), :] = jnp.zeros(
            (GROUP, 2 * HD), BF16
        )


def lane_max(x):
    best = x[:, 0:128]
    for j in range(1, CHUNK // 128):
        best = jnp.maximum(best, x[:, j * 128 : (j + 1) * 128])
    return best


def lane_sum(x):
    total = x[:, 0:128]
    for j in range(1, CHUNK // 128):
        total = total + x[:, j * 128 : (j + 1) * 128]
    return total


def query_body(where_ref, own_ref, *refs):
    out_ref, stat_ref, s_ref, mx_ref, l_ref, o_ref, st_ref, kv_ref = refs[8:]
    assemble(where_ref, refs[:8], kv_ref, True)
    first = where_ref[0] * GROUP
    clear = first // CHUNK
    total = (first + GROUP + CHUNK - 1) // CHUNK
    mx_ref[...] = jnp.full_like(mx_ref, -jnp.inf)
    l_ref[...] = jnp.zeros_like(l_ref)
    o_ref[...] = jnp.zeros_like(o_ref)

    def rows_of(c):
        return pl.ds(pl.multiple_of(c * CHUNK, CHUNK), CHUNK)

    def scores(c, masked):
        s = nt(own_ref[:, :HD], kv_ref[rows_of(c), :HD]) * (SCALE * LOG2E)
        if masked:
            q = first + lax.broadcasted_iota(jnp.int32, (GROUP, CHUNK), 0)
            k = c * CHUNK + lax.broadcasted_iota(jnp.int32, (GROUP, CHUNK), 1)
            s = jnp.where(q >= k, s, -jnp.inf)
        s_ref[c] = s
        mx_ref[...] = jnp.maximum(mx_ref[...], lane_max(s))

    @pl.loop(0, clear)
    def _(c):
        scores(c, False)

    @pl.loop(clear, total)
    def _(c):
        scores(c, True)

    peak = jnp.max(mx_ref[...], axis=1, keepdims=True)

    @pl.loop(0, total)
    def _(c):
        p = jnp.exp2(s_ref[c] - peak)
        s_ref[c] = p
        l_ref[...] += lane_sum(p)
        o_ref[...] += nn(p.astype(BF16), kv_ref[rows_of(c), HD:])

    norm = jnp.sum(l_ref[...], axis=1, keepdims=True)
    inverse = 1.0 / norm
    attended = (o_ref[...] * inverse).astype(BF16)
    out_ref[:, :HD] = attended
    delta = jnp.sum(
        own_ref[:, HD:].astype(F32) * attended.astype(F32), axis=1, keepdims=True
    )
    o_ref[...] = jnp.zeros_like(o_ref)

    @pl.loop(0, total)
    def _(c):
        rows = rows_of(c)
        gw = nt(own_ref[:, HD:], kv_ref[rows, HD:])
        gs = (s_ref[c] * (gw - delta)).astype(BF16)
        o_ref[...] += nn(gs, kv_ref[rows, :HD])

    out_ref[:, HD:] = (o_ref[...] * (inverse * SCALE)).astype(BF16)
    lane = lax.broadcasted_iota(jnp.int32, (GROUP, HD), 1)
    st_ref[0:GROUP] = jnp.where(lane == 0, peak + jnp.log2(norm), delta)
    st_ref[GROUP:640] = jnp.zeros((640 - GROUP, HD), F32)
    stat_ref[...] = st_ref[...].T[0:8]


def query_pass(where, own, kv):
    return call(
        query_body,
        (struct((GROUP, 2 * HD), BF16), struct((8, 640), F32)),
        "query_pass",
        grid=(1,),
        in_specs=[pl.BlockSpec(memory_space=pltpu.SMEM)]
        + [part_of(0)]
        + [part_of(1)] * 7
        + [part_of(0)],
        scratch_shapes=[
            pltpu.VMEM((CHUNKS, GROUP, CHUNK), F32),
            pltpu.VMEM((GROUP, HD), F32),
            pltpu.VMEM((GROUP, HD), F32),
            pltpu.VMEM((GROUP, HD), F32),
            pltpu.VMEM((640, HD), F32),
            pltpu.VMEM((SEQ, 2 * HD), BF16),
        ],
    )(where, own, *kv)


def key_body(where_ref, own_ref, stat_ref, *refs):
    out_ref, gk_ref, gv_ref, qd_ref = refs[8:]
    assemble(where_ref, refs[:8], qd_ref, False)
    first = where_ref[0] * GROUP
    begin = first // CHUNK
    clear = (first + GROUP - 1 + CHUNK - 1) // CHUNK
    gk_ref[...] = jnp.zeros_like(gk_ref)
    gv_ref[...] = jnp.zeros_like(gv_ref)

    def visit(c, masked):
        rows = pl.ds(pl.multiple_of(c * CHUNK, CHUNK), CHUNK)
        log_row = stat_ref[c, 0:1, :]
        delta_row = stat_ref[c, 1:2, :]
        q = qd_ref[rows, :HD]
        d = qd_ref[rows, HD:]
        s = nt(own_ref[:, :HD], q) * (SCALE * LOG2E)
        p = jnp.exp2(s - log_row)
        if masked:
            k_at = first + lax.broadcasted_iota(jnp.int32, (GROUP, CHUNK), 0)
            q_at = c * CHUNK + lax.broadcasted_iota(jnp.int32, (GROUP, CHUNK), 1)
            p = jnp.where(q_at >= k_at, p, 0.0)
        gv_ref[...] += nn(p.astype(BF16), d)
        gw = nt(own_ref[:, HD:], d)
        gs = (p * (gw - delta_row)).astype(BF16)
        gk_ref[...] += nn(gs, q)

    @pl.loop(begin, jnp.minimum(clear, CHUNKS))
    def _(c):
        visit(c, True)

    @pl.loop(clear, CHUNKS)
    def _(c):
        visit(c, False)

    out_ref[:, :HD] = (gk_ref[...] * SCALE).astype(BF16)
    out_ref[:, HD:] = gv_ref[...].astype(BF16)


def join_body(oq_ref, ok_ref, part_ref, out_ref):
    for j in range(4):
        at = slice(j * ROWS, (j + 1) * ROWS)
        out_ref[j, :ROWS, : 2 * HD] = oq_ref[at]
        out_ref[j, :ROWS, 2 * HD :] = ok_ref[at]
        for side in range(2):
            value = part_ref[side * 40 : (side + 1) * 40]
            high = value.astype(BF16)
            out_ref[j, ROWS:, side * HD : (side + 1) * HD] = high
            low = (value - high.astype(F32)).astype(BF16)
            out_ref[j, ROWS:, (side + 2) * HD : (side + 3) * HD] = low


def join(out_q, out_k, part):
    return call(join_body, struct((4, ROWS + 40, 4 * HD), BF16), "join")(out_q, out_k, part)


def key_pass(where, own, qd, stats):
    return call(
        key_body,
        struct((GROUP, 2 * HD), BF16),
        "key_pass",
        grid=(1,),
        in_specs=[pl.BlockSpec(memory_space=pltpu.SMEM)]
        + [part_of(1)]
        + [pl.BlockSpec(memory_space=pltpu.VMEM)]
        + [part_of(0)] * 8,
        scratch_shapes=[
            pltpu.VMEM((GROUP, HD), F32),
            pltpu.VMEM((GROUP, HD), F32),
            pltpu.VMEM((SEQ, 2 * HD), BF16),
        ],
    )(where, own, stats, *qd)


def exchange(x, axis):
    return lax.all_to_all(x, axis, 0, 0, tiled=True)


def share(x, axis, count):
    return exchange(jnp.broadcast_to(x[None], (count,) + x.shape), axis)


def body(
    features, short_filter, long_filter_taps, queries, key_vectors, value_vectors,
    grad_mixed, grad_attended,
):
    where = lax.axis_index("cz").astype(jnp.int32).reshape(1)
    packed = pack(queries, grad_attended, key_vectors, value_vectors)
    own = exchange(packed, "cy").reshape(GROUP, 4 * HD)
    features, upstream = after(features, own), after(grad_mixed, own)
    feat = features.transpose(1, 0, 2)
    prev = lax.ppermute(feat[:, 8:], CTX, [(i, i + 1) for i in range(31)])
    rim = jnp.concatenate([feat[1, :136], upstream[:136], feat[0, :8], feat[2, :8]], 0)
    nxt = lax.ppermute(rim, CTX, [(i + 1, i) for i in range(31)])

    rising, falling = [own], [own]

    def shift(x, by):
        return lax.ppermute(x, "cz", [(i, (i + by) % 8) for i in range(8)])

    def step():
        rising.append(shift(rising[-1], 1))
        falling.append(shift(falling[-1], -1))

    def order(*values):
        held = lax.optimization_barrier((rising[-1], falling[-1]) + values)
        rising[-1], falling[-1] = held[:2]
        return held[2:]

    short8 = jnp.pad(short_filter, ((0, 0), (0, 1), (0, 0)))
    step()
    prev, nxt = order(prev, nxt)
    step()
    first = hyena(0, feat, prev, nxt, upstream, short8, long_filter_taps, ())
    first = order(*first)
    step()
    second = hyena(1, feat, prev, nxt, upstream, short8, long_filter_taps, first[:2])
    mixed, gfeat, glong, gshort = order(*second)
    glong = jnp.concatenate([first[2], glong], 1)
    gshort = jnp.concatenate([first[3], gshort], 2).reshape(24, 256)
    grads = jnp.concatenate([glong, gshort, jnp.zeros((8, 256), F32)], 0)
    far_kv = shift(rising[-1][:, 2 * HD :], 1)
    far_qd = shift(falling[-1][:, : 2 * HD], -1)
    part = jnp.sum(exchange(grads.reshape(32, 10, HD), YFT), axis=0)
    far_kv, far_qd, own = lax.optimization_barrier((far_kv, far_qd, own))
    pieces = [own] + rising[1:] + falling[1:]

    out_q, stats = query_pass(where, own, pieces + [far_kv])
    small = jnp.concatenate([stats[:2].reshape(10, HD), part], 0)
    small = share(small, "cz", 8)
    part = share(jnp.sum(small[:, 10:], axis=0), FT, 8)
    stats = small[:, :10].reshape(8, 2, 640)[:, :, :GROUP].transpose(1, 0, 2)
    stats = stats.reshape(2, CHUNKS, CHUNK).transpose(1, 0, 2)
    out_k = key_pass(where, own, pieces + [far_qd], stats)
    result = join(out_q, out_k, part.reshape(80, HD))
    attended, grad_queries, grad_keys, grad_values, grads = unpack(exchange(result, "cy"))
    grads = grads.reshape(160, 256)
    grad_long = grads[:128]
    grad_short = grads[128:152].reshape(3, 8, 256)[:, :7]
    return (
        mixed, attended, gfeat.transpose(1, 0, 2), grad_short, grad_long,
        grad_queries, grad_keys, grad_values,
    )


def solution(mesh):
    fine = Mesh(np.asarray(mesh.devices).reshape(8, 4, 4, 2), ("cz", "cy", "fsdp", "tp"))
    rows = P(CTX, FT)
    wide = P(CTX, None, FT)
    return jax.shard_map(
        body,
        mesh=fine,
        in_specs=(wide, P(), P(), rows, rows, rows, rows, rows),
        out_specs=(rows, rows, wide, P(), P(), rows, rows, rows),
        check_vma=False,
    )
```

```python
import jax
import jax.numpy as jnp
import numpy as np
from jax import lax
from jax.experimental import pallas as pl
from jax.experimental.pallas import tpu as pltpu
from jax.sharding import Mesh, PartitionSpec as P

HD = 128
ROWS = 144
GROUP = 576
SEQ = 4608
CHUNK = 512
CHUNKS = SEQ // CHUNK
LOG2E = 1.4426950408889634
SCALE = HD ** -0.5
VMEM_BYTES = 56 * 1024 * 1024
F32 = jnp.float32
BF16 = jnp.bfloat16
CTX = ("cz", "cy")
FT = ("fsdp", "tp")
YFT = ("cy", "fsdp", "tp")


def after(value, *others):
    return lax.optimization_barrier((value,) + others)[0]


def call(body, out_shape, name, **options):
    return pl.pallas_call(
        body,
        out_shape=out_shape,
        name=name,
        compiler_params=pltpu.CompilerParams(vmem_limit_bytes=VMEM_BYTES),
        **options,
    )


def struct(shape, dtype):
    return jax.ShapeDtypeStruct(shape, dtype)


def nt(a, b):
    return lax.dot_general(a, b, (((1,), (1,)), ((), ())), preferred_element_type=F32)


def nn(a, b):
    return lax.dot_general(a, b, (((1,), (0,)), ((), ())), preferred_element_type=F32)


def pack_body(q_ref, d_ref, k_ref, v_ref, feat_ref, up_ref, out_ref, tail_ref, rim_ref):
    for h in range(4):
        for slot, ref in enumerate((q_ref, d_ref, k_ref, v_ref)):
            out_ref[h, :, slot * HD : (slot + 1) * HD] = ref[:, h * HD : (h + 1) * HD]
    tail_ref[...] = feat_ref[:, 8:]
    rim_ref[0:136] = feat_ref[1, 0:136]
    rim_ref[136:272] = up_ref[0:136]
    rim_ref[272:280] = feat_ref[0, 0:8]
    rim_ref[280:288] = feat_ref[2, 0:8]


def pack(*parts):
    return call(
        pack_body,
        (
            struct((4, ROWS, 4 * HD), BF16),
            struct((3, 136, 4 * HD), BF16),
            struct((288, 4 * HD), BF16),
        ),
        "pack",
    )(*parts)


def unpack_body(x_ref, attended_ref, gq_ref, gk_ref, gv_ref, grads_ref):
    for h in range(4):
        at = slice(h * HD, (h + 1) * HD)
        attended_ref[:, at] = x_ref[h, :ROWS, 0:HD]
        gq_ref[:, at] = x_ref[h, :ROWS, HD : 2 * HD].astype(F32)
        gk_ref[:, at] = x_ref[h, :ROWS, 2 * HD : 3 * HD].astype(F32)
        gv_ref[:, at] = x_ref[h, :ROWS, 3 * HD :].astype(F32)
        for side in range(2):
            high = x_ref[h, ROWS:, side * HD : (side + 1) * HD].astype(F32)
            low = x_ref[h, ROWS:, (side + 2) * HD : (side + 3) * HD].astype(F32)
            grads_ref[h, side * 40 : (side + 1) * 40] = high + low


def unpack(x):
    whole = struct((ROWS, 4 * HD), F32)
    return call(
        unpack_body,
        (struct((ROWS, 4 * HD), BF16), whole, whole, whole, struct((4, 80, HD), F32)),
        "unpack",
    )(x)


def hyena_body(feat_ref, prev_ref, next_ref, up_ref, short_ref, long_ref, *refs):
    (
        mixed_ref, gfeat_ref, glong_ref, gshort_ref,
        x_ref, x1_ref, p_ref, ps_ref, gm_ref, gs_ref, f_ref, gf_ref, wb_ref, gl_ref,
    ) = refs[-14:]
    turn = pl.program_id(0)
    for slot, g in enumerate((0, 2)):
        x_ref[slot, 0:136] = prev_ref[g].astype(F32)
        x_ref[slot, 136:280] = feat_ref[g].astype(F32)
        x_ref[slot, 280:288] = next_ref[272 + 8 * slot : 280 + 8 * slot].astype(F32)
    x1_ref[0:136] = prev_ref[1].astype(F32)
    x1_ref[136:280] = feat_ref[1].astype(F32)
    x1_ref[280:416] = next_ref[0:136].astype(F32)
    taps = [[short_ref[g, s : s + 1, :] for s in range(7)] for g in range(3)]

    def featured(read, g):
        total = taps[g][0] * read(0)
        for s in range(1, 7):
            total = total + taps[g][s] * read(s)
        return total

    f0 = featured(lambda s: x_ref[0, 8 - s : 288 - s], 0)
    f2 = featured(lambda s: x_ref[1, 8 - s : 288 - s], 2)
    p_ref[8:288] = f0 * f2
    f_ref[0] = f0[128:280]
    f_ref[2] = f2[128:280]
    f1 = featured(lambda s: x1_ref[136 - s : 416 - s], 1)
    f_ref[1] = f1[0:152]
    gm_ref[0:144] = up_ref[...].astype(F32) * f1[0:144]
    gm_ref[144:280] = next_ref[136:272].astype(F32) * f1[144:280]
    for b in range(8):
        ps_ref[b, 16:288] = p_ref[16 - b : 288 - b]
        gs_ref[b] = gm_ref[b : 272 + b]
    wb_ref[...] = jnp.broadcast_to(long_ref[...][:, None, :], (128, 8, 128))

    def forward(a, total):
        base = pl.multiple_of(136 - 8 * a, 8)
        for b in range(8):
            tap = 8 * a + b
            x = ps_ref[b, pl.ds(base, 152), :].reshape(19, 8, 128)
            total = total + wb_ref[tap][None] * x
            gm = gm_ref[0:144].reshape(18, 8, 128)
            gl_ref[tap] = jnp.sum(gm * x[:18], axis=0)
        return total

    memory = lax.fori_loop(0, 16, forward, jnp.zeros((19, 8, 128), F32)).reshape(152, 128)
    mixed_ref[...] = (f_ref[1, 0:144] * memory[0:144]).astype(BF16)
    gf_ref[1, 0:144] = up_ref[...].astype(F32) * memory[0:144]
    gf_ref[1, 144:152] = next_ref[136:144].astype(F32) * memory[144:152]

    def backward(a, total):
        base = pl.multiple_of(8 * a, 8)
        for b in range(8):
            y = gs_ref[b, pl.ds(base, 152), :].reshape(19, 8, 128)
            total = total + wb_ref[8 * a + b][None] * y
        return total

    gp = lax.fori_loop(0, 16, backward, jnp.zeros((19, 8, 128), F32)).reshape(152, 128)
    gf_ref[0] = gp * f_ref[2]
    gf_ref[2] = gp * f_ref[0]
    glong = jnp.sum(gl_ref[...], axis=1)

    @pl.when(turn == 0)
    def _():
        glong_ref[...] = glong
        gshort_ref[...] = jnp.zeros_like(gshort_ref)

    @pl.when(turn != 0)
    def _():
        glong_ref[...] += glong

    for g in range(3):
        total = taps[g][0] * gf_ref[g, 0:144]
        for s in range(1, 7):
            total = total + taps[g][s] * gf_ref[g, s : 144 + s]
        gfeat_ref[g] = total
        own = gf_ref[g, 0:144]
        for s in range(7):
            if g == 1:
                x = x1_ref[136 - s : 280 - s]
            else:
                x = x_ref[g // 2, 136 - s : 280 - s]
            column = jnp.sum((own * x).reshape(18, 8, 128), axis=0)
            gshort_ref[g, s : s + 1, :] += jnp.sum(column, axis=0, keepdims=True)


def hyena(side, feat, prev, nxt, up, short8, long_taps, earlier):
    def cols(*lead):
        return pl.BlockSpec(lead + (128,), lambda k: (0,) * len(lead) + (2 * k + side,))

    def filters(*lead):
        return pl.BlockSpec(lead + (128,), lambda k: (0,) * len(lead) + (side,))

    def sums(*lead):
        return pl.BlockSpec(lead + (128,), lambda k: (0,) * (len(lead) + 1))

    kept = pl.BlockSpec(memory_space=pl.ANY)
    return call(
        hyena_body,
        (
            struct((ROWS, 512), BF16),
            struct((3, ROWS, 512), F32),
            struct((128, 128), F32),
            struct((3, 8, 128), F32),
        ),
        "hyena",
        grid=(2,),
        in_specs=[
            cols(3, ROWS), cols(3, 136), cols(288), cols(ROWS), filters(3, 8), filters(128),
        ] + [kept] * len(earlier),
        out_specs=(cols(ROWS), cols(3, ROWS), sums(128), sums(3, 8)),
        input_output_aliases={6 + i: i for i in range(len(earlier))},
        scratch_shapes=[
            pltpu.VMEM((2, 288, 128), F32),
            pltpu.VMEM((416, 128), F32),
            pltpu.VMEM((288, 128), F32),
            pltpu.VMEM((8, 288, 128), F32),
            pltpu.VMEM((280, 128), F32),
            pltpu.VMEM((8, 272, 128), F32),
            pltpu.VMEM((3, 152, 128), F32),
            pltpu.VMEM((3, 152, 128), F32),
            pltpu.VMEM((128, 8, 128), F32),
            pltpu.VMEM((128, 8, 128), F32),
        ],
    )(feat, prev, nxt, up, short8, long_taps, *earlier)


PLACES = (0, -1, -2, -3, 1, 2, 3, 4)


def part_of(side):
    return pl.BlockSpec((GROUP, 2 * HD), lambda i: (0, side))


def assemble(where_ref, pieces, out_ref, below):
    z = where_ref[0]
    for place, piece in zip(PLACES, pieces):
        block = (z + place + 8) % 8
        needed = (block <= z) if below else (block >= z)

        @pl.when(needed)
        def _():
            out_ref[pl.ds(pl.multiple_of(block * GROUP, 64), GROUP), :] = piece[...]

    spare = z + 1 if below else z - 1

    @pl.when((spare >= 0) & (spare < 8))
    def _():
        out_ref[pl.ds(pl.multiple_of(spare * GROUP, 64), GROUP), :] = jnp.zeros(
            (GROUP, 2 * HD), BF16
        )


def lane_max(x):
    best = x[:, 0:128]
    for j in range(1, CHUNK // 128):
        best = jnp.maximum(best, x[:, j * 128 : (j + 1) * 128])
    return best


def lane_sum(x):
    total = x[:, 0:128]
    for j in range(1, CHUNK // 128):
        total = total + x[:, j * 128 : (j + 1) * 128]
    return total


def query_body(where_ref, own_ref, *refs):
    out_ref, stat_ref, s_ref, mx_ref, l_ref, o_ref, st_ref, kv_ref = refs[8:]
    assemble(where_ref, refs[:8], kv_ref, True)
    first = where_ref[0] * GROUP
    clear = first // CHUNK
    total = (first + GROUP + CHUNK - 1) // CHUNK
    mx_ref[...] = jnp.full_like(mx_ref, -jnp.inf)
    l_ref[...] = jnp.zeros_like(l_ref)
    o_ref[...] = jnp.zeros_like(o_ref)

    def rows_of(c):
        return pl.ds(pl.multiple_of(c * CHUNK, CHUNK), CHUNK)

    def scores(c, masked):
        s = nt(own_ref[:, :HD], kv_ref[rows_of(c), :HD]) * (SCALE * LOG2E)
        if masked:
            q = first + lax.broadcasted_iota(jnp.int32, (GROUP, CHUNK), 0)
            k = c * CHUNK + lax.broadcasted_iota(jnp.int32, (GROUP, CHUNK), 1)
            s = jnp.where(q >= k, s, -jnp.inf)
        s_ref[c] = s
        mx_ref[...] = jnp.maximum(mx_ref[...], lane_max(s))

    @pl.loop(0, clear)
    def _(c):
        scores(c, False)

    @pl.loop(clear, total)
    def _(c):
        scores(c, True)

    peak = jnp.max(mx_ref[...], axis=1, keepdims=True)

    @pl.loop(0, total)
    def _(c):
        p = jnp.exp2(s_ref[c] - peak)
        s_ref[c] = p
        l_ref[...] += lane_sum(p)
        o_ref[...] += nn(p.astype(BF16), kv_ref[rows_of(c), HD:])

    norm = jnp.sum(l_ref[...], axis=1, keepdims=True)
    inverse = 1.0 / norm
    attended = (o_ref[...] * inverse).astype(BF16)
    out_ref[:, :HD] = attended
    delta = jnp.sum(
        own_ref[:, HD:].astype(F32) * attended.astype(F32), axis=1, keepdims=True
    )
    o_ref[...] = jnp.zeros_like(o_ref)

    @pl.loop(0, total)
    def _(c):
        rows = rows_of(c)
        gw = nt(own_ref[:, HD:], kv_ref[rows, HD:])
        gs = (s_ref[c] * (gw - delta)).astype(BF16)
        o_ref[...] += nn(gs, kv_ref[rows, :HD])

    out_ref[:, HD:] = (o_ref[...] * (inverse * SCALE)).astype(BF16)
    lane = lax.broadcasted_iota(jnp.int32, (GROUP, HD), 1)
    st_ref[0:GROUP] = jnp.where(lane == 0, peak + jnp.log2(norm), delta)
    st_ref[GROUP:640] = jnp.zeros((640 - GROUP, HD), F32)
    stat_ref[...] = st_ref[...].T[0:8]


def query_pass(where, own, kv):
    return call(
        query_body,
        (struct((GROUP, 2 * HD), BF16), struct((8, 640), F32)),
        "query_pass",
        grid=(1,),
        in_specs=[pl.BlockSpec(memory_space=pltpu.SMEM)]
        + [part_of(0)]
        + [part_of(1)] * 7
        + [part_of(0)],
        scratch_shapes=[
            pltpu.VMEM((CHUNKS, GROUP, CHUNK), F32),
            pltpu.VMEM((GROUP, HD), F32),
            pltpu.VMEM((GROUP, HD), F32),
            pltpu.VMEM((GROUP, HD), F32),
            pltpu.VMEM((640, HD), F32),
            pltpu.VMEM((SEQ, 2 * HD), BF16),
        ],
    )(where, own, *kv)


def key_body(where_ref, own_ref, stat_ref, *refs):
    out_ref, gk_ref, gv_ref, qd_ref = refs[8:]
    assemble(where_ref, refs[:8], qd_ref, False)
    first = where_ref[0] * GROUP
    begin = first // CHUNK
    clear = (first + GROUP - 1 + CHUNK - 1) // CHUNK
    gk_ref[...] = jnp.zeros_like(gk_ref)
    gv_ref[...] = jnp.zeros_like(gv_ref)

    def visit(c, masked):
        rows = pl.ds(pl.multiple_of(c * CHUNK, CHUNK), CHUNK)
        log_row = stat_ref[c, 0:1, :]
        delta_row = stat_ref[c, 1:2, :]
        q = qd_ref[rows, :HD]
        d = qd_ref[rows, HD:]
        s = nt(own_ref[:, :HD], q) * (SCALE * LOG2E)
        p = jnp.exp2(s - log_row)
        if masked:
            k_at = first + lax.broadcasted_iota(jnp.int32, (GROUP, CHUNK), 0)
            q_at = c * CHUNK + lax.broadcasted_iota(jnp.int32, (GROUP, CHUNK), 1)
            p = jnp.where(q_at >= k_at, p, 0.0)
        gv_ref[...] += nn(p.astype(BF16), d)
        gw = nt(own_ref[:, HD:], d)
        gs = (p * (gw - delta_row)).astype(BF16)
        gk_ref[...] += nn(gs, q)

    @pl.loop(begin, jnp.minimum(clear, CHUNKS))
    def _(c):
        visit(c, True)

    @pl.loop(clear, CHUNKS)
    def _(c):
        visit(c, False)

    out_ref[:, :HD] = (gk_ref[...] * SCALE).astype(BF16)
    out_ref[:, HD:] = gv_ref[...].astype(BF16)


def join_body(oq_ref, ok_ref, part_ref, out_ref):
    for j in range(4):
        at = slice(j * ROWS, (j + 1) * ROWS)
        out_ref[j, :ROWS, : 2 * HD] = oq_ref[at]
        out_ref[j, :ROWS, 2 * HD :] = ok_ref[at]
        for side in range(2):
            value = part_ref[side * 40 : (side + 1) * 40]
            high = value.astype(BF16)
            out_ref[j, ROWS:, side * HD : (side + 1) * HD] = high
            low = (value - high.astype(F32)).astype(BF16)
            out_ref[j, ROWS:, (side + 2) * HD : (side + 3) * HD] = low


def join(out_q, out_k, part):
    return call(join_body, struct((4, ROWS + 40, 4 * HD), BF16), "join")(out_q, out_k, part)


def key_pass(where, own, qd, stats):
    return call(
        key_body,
        struct((GROUP, 2 * HD), BF16),
        "key_pass",
        grid=(1,),
        in_specs=[pl.BlockSpec(memory_space=pltpu.SMEM)]
        + [part_of(1)]
        + [pl.BlockSpec(memory_space=pltpu.VMEM)]
        + [part_of(0)] * 8,
        scratch_shapes=[
            pltpu.VMEM((GROUP, HD), F32),
            pltpu.VMEM((GROUP, HD), F32),
            pltpu.VMEM((SEQ, 2 * HD), BF16),
        ],
    )(where, own, stats, *qd)


def exchange(x, axis):
    return lax.all_to_all(x, axis, 0, 0, tiled=True)


def share(x, axis, count):
    return exchange(jnp.broadcast_to(x[None], (count,) + x.shape), axis)


def body(
    features, short_filter, long_filter_taps, queries, key_vectors, value_vectors,
    grad_mixed, grad_attended,
):
    feat = features.transpose(1, 0, 2)
    where = lax.axis_index("cz").astype(jnp.int32).reshape(1)
    packed, tail, rim = pack(
        queries, grad_attended, key_vectors, value_vectors, feat, grad_mixed
    )
    prev = lax.ppermute(tail, CTX, [(i, i + 1) for i in range(31)])
    nxt = lax.ppermute(rim, CTX, [(i + 1, i) for i in range(31)])
    own = exchange(packed, "cy").reshape(GROUP, 4 * HD)
    own, prev, nxt = lax.optimization_barrier((own, prev, nxt))
    rising, falling = [own], [own]

    def shift(x, by):
        return lax.ppermute(x, "cz", [(i, (i + by) % 8) for i in range(8)])

    def step():
        rising.append(shift(rising[-1], 1))
        falling.append(shift(falling[-1], -1))

    def order(*values):
        held = lax.optimization_barrier((rising[-1], falling[-1]) + values)
        rising[-1], falling[-1] = held[:2]
        return held[2:]

    short8 = jnp.pad(short_filter, ((0, 0), (0, 1), (0, 0)))
    step()
    first = hyena(0, feat, prev, nxt, grad_mixed, short8, long_filter_taps, ())
    first = order(*first)
    step()
    second = hyena(1, feat, prev, nxt, grad_mixed, short8, long_filter_taps, first[:2])
    mixed, gfeat, glong, gshort = order(*second)
    step()
    glong = jnp.concatenate([first[2], glong], 1)
    gshort = jnp.concatenate([first[3], gshort], 2).reshape(24, 256)
    grads = jnp.concatenate([glong, gshort, jnp.zeros((8, 256), F32)], 0)
    part = jnp.sum(exchange(grads.reshape(32, 10, HD), YFT), axis=0)
    (part,) = order(part)
    far_kv = shift(rising[-1][:, 2 * HD :], 1)
    far_qd = shift(falling[-1][:, : 2 * HD], -1)
    far_kv, far_qd, own = lax.optimization_barrier((far_kv, far_qd, own))
    pieces = [own] + rising[1:] + falling[1:]

    out_q, stats = query_pass(where, own, pieces + [far_kv])
    small = jnp.concatenate([stats[:2].reshape(10, HD), part], 0)
    small = share(small, "cz", 8)
    part = share(jnp.sum(small[:, 10:], axis=0), FT, 8)
    stats = small[:, :10].reshape(8, 2, 640)[:, :, :GROUP].transpose(1, 0, 2)
    stats = stats.reshape(2, CHUNKS, CHUNK).transpose(1, 0, 2)
    out_k = key_pass(where, own, pieces + [far_qd], stats)
    result = join(out_q, out_k, part.reshape(80, HD))
    attended, grad_queries, grad_keys, grad_values, grads = unpack(exchange(result, "cy"))
    grads = grads.reshape(160, 256)
    grad_long = grads[:128]
    grad_short = grads[128:152].reshape(3, 8, 256)[:, :7]
    return (
        mixed, attended, gfeat.transpose(1, 0, 2), grad_short, grad_long,
        grad_queries, grad_keys, grad_values,
    )


def solution(mesh):
    fine = Mesh(np.asarray(mesh.devices).reshape(8, 4, 4, 2), ("cz", "cy", "fsdp", "tp"))
    rows = P(CTX, FT)
    wide = P(CTX, None, FT)
    return jax.shard_map(
        body,
        mesh=fine,
        in_specs=(wide, P(), P(), rows, rows, rows, rows, rows),
        out_specs=(rows, rows, wide, P(), P(), rows, rows, rows),
        check_vma=False,
    )
```

```python
import jax
import jax.numpy as jnp
import numpy as np
from jax import lax
from jax.experimental import pallas as pl
from jax.experimental.pallas import tpu as pltpu
from jax.sharding import Mesh, PartitionSpec as P

HD = 128
ROWS = 144
GROUP = 576
SEQ = 4608
CHUNK = 512
CHUNKS = SEQ // CHUNK
LOG2E = 1.4426950408889634
SCALE = HD ** -0.5
VMEM_BYTES = 56 * 1024 * 1024
F32 = jnp.float32
BF16 = jnp.bfloat16
CTX = ("cz", "cy")
FT = ("fsdp", "tp")
YFT = ("cy", "fsdp", "tp")


def after(value, *others):
    return lax.optimization_barrier((value,) + others)[0]


def call(body, out_shape, name, **options):
    return pl.pallas_call(
        body,
        out_shape=out_shape,
        name=name,
        compiler_params=pltpu.CompilerParams(vmem_limit_bytes=VMEM_BYTES),
        **options,
    )


def struct(shape, dtype):
    return jax.ShapeDtypeStruct(shape, dtype)


def nt(a, b):
    return lax.dot_general(a, b, (((1,), (1,)), ((), ())), preferred_element_type=F32)


def nn(a, b):
    return lax.dot_general(a, b, (((1,), (0,)), ((), ())), preferred_element_type=F32)


def pack_body(q_ref, d_ref, k_ref, v_ref, feat_ref, up_ref, out_ref, tail_ref, rim_ref):
    for h in range(4):
        for slot, ref in enumerate((q_ref, d_ref, k_ref, v_ref)):
            out_ref[h, :, slot * HD : (slot + 1) * HD] = ref[:, h * HD : (h + 1) * HD]
    tail_ref[0:136] = feat_ref[0, 8:]
    tail_ref[136:272] = feat_ref[2, 8:]
    tail_ref[272:280] = feat_ref[1, 136:]
    rim_ref[0:136] = feat_ref[1, 0:136]
    rim_ref[136:272] = up_ref[0:136]
    rim_ref[272:280] = feat_ref[0, 0:8]
    rim_ref[280:288] = feat_ref[2, 0:8]


def pack(*parts):
    return call(
        pack_body,
        (
            struct((4, ROWS, 4 * HD), BF16),
            struct((280, 4 * HD), BF16),
            struct((288, 4 * HD), BF16),
        ),
        "pack",
    )(*parts)


def unpack_body(x_ref, attended_ref, gq_ref, gk_ref, gv_ref, glong_ref, gshort_ref, grads_ref):
    for h in range(4):
        at = slice(h * HD, (h + 1) * HD)
        attended_ref[:, at] = x_ref[h, :ROWS, 0:HD]
        gq_ref[:, at] = x_ref[h, :ROWS, HD : 2 * HD].astype(F32)
        gk_ref[:, at] = x_ref[h, :ROWS, 2 * HD : 3 * HD].astype(F32)
        gv_ref[:, at] = x_ref[h, :ROWS, 3 * HD :].astype(F32)
        for side in range(2):
            high = x_ref[h, ROWS:, side * HD : (side + 1) * HD].astype(F32)
            low = x_ref[h, ROWS:, (side + 2) * HD : (side + 3) * HD].astype(F32)
            first = 80 * h + 40 * side
            grads_ref[first : first + 40] = high + low
    for side in range(2):
        at = slice(side * HD, (side + 1) * HD)
        glong_ref[:, at] = grads_ref[128 * side : 128 * (side + 1)]
        for g in range(3):
            first = 256 + 24 * side + 8 * g
            gshort_ref[g, :, at] = grads_ref[first : first + 7]


def unpack(x):
    whole = struct((ROWS, 4 * HD), F32)
    return call(
        unpack_body,
        (
            struct((ROWS, 4 * HD), BF16), whole, whole, whole,
            struct((128, 256), F32), struct((3, 7, 256), F32),
        ),
        "unpack",
        scratch_shapes=[pltpu.VMEM((320, HD), F32)],
    )(x)


def hyena_body(feat_ref, prev_ref, next_ref, up_ref, short_ref, long_ref, *refs):
    (
        mixed_ref, gfeat_ref, glong_ref, gshort_ref,
        x_ref, x1_ref, p_ref, ps_ref, gm_ref, gs_ref, f_ref, gf_ref, wb_ref, gl_ref,
    ) = refs[-14:]
    turn = pl.program_id(0)
    for slot, g in enumerate((0, 2)):
        x_ref[slot, 0:136] = prev_ref[136 * slot : 136 * (slot + 1)].astype(F32)
        x_ref[slot, 136:280] = feat_ref[g].astype(F32)
        x_ref[slot, 280:288] = next_ref[272 + 8 * slot : 280 + 8 * slot].astype(F32)
    x1_ref[128:136] = prev_ref[272:280].astype(F32)
    x1_ref[136:280] = feat_ref[1].astype(F32)
    x1_ref[280:416] = next_ref[0:136].astype(F32)
    taps = [[short_ref[g, s : s + 1, :] for s in range(7)] for g in range(3)]

    def featured(read, g):
        total = taps[g][0] * read(0)
        for s in range(1, 7):
            total = total + taps[g][s] * read(s)
        return total

    f0 = featured(lambda s: x_ref[0, 8 - s : 288 - s], 0)
    f2 = featured(lambda s: x_ref[1, 8 - s : 288 - s], 2)
    p_ref[8:288] = f0 * f2
    f_ref[0] = f0[128:280]
    f_ref[2] = f2[128:280]
    f1 = featured(lambda s: x1_ref[136 - s : 416 - s], 1)
    f_ref[1] = f1[0:152]
    gm_ref[0:144] = up_ref[...].astype(F32) * f1[0:144]
    gm_ref[144:280] = next_ref[136:272].astype(F32) * f1[144:280]
    for b in range(8):
        ps_ref[b, 16:288] = p_ref[16 - b : 288 - b]
        gs_ref[b] = gm_ref[b : 272 + b]
    wb_ref[...] = jnp.broadcast_to(long_ref[...][:, None, :], (128, 8, 128))

    def forward(a, total):
        base = pl.multiple_of(136 - 8 * a, 8)
        for b in range(8):
            tap = 8 * a + b
            x = ps_ref[b, pl.ds(base, 152), :].reshape(19, 8, 128)
            total = total + wb_ref[tap][None] * x
            gm = gm_ref[0:144].reshape(18, 8, 128)
            gl_ref[tap] = jnp.sum(gm * x[:18], axis=0)
        return total

    memory = lax.fori_loop(0, 16, forward, jnp.zeros((19, 8, 128), F32)).reshape(152, 128)
    mixed_ref[...] = (f_ref[1, 0:144] * memory[0:144]).astype(BF16)
    gf_ref[1, 0:144] = up_ref[...].astype(F32) * memory[0:144]
    gf_ref[1, 144:152] = next_ref[136:144].astype(F32) * memory[144:152]

    def backward(a, total):
        base = pl.multiple_of(8 * a, 8)
        for b in range(8):
            y = gs_ref[b, pl.ds(base, 152), :].reshape(19, 8, 128)
            total = total + wb_ref[8 * a + b][None] * y
        return total

    gp = lax.fori_loop(0, 16, backward, jnp.zeros((19, 8, 128), F32)).reshape(152, 128)
    gf_ref[0] = gp * f_ref[2]
    gf_ref[2] = gp * f_ref[0]
    glong = jnp.sum(gl_ref[...], axis=1)

    @pl.when(turn == 0)
    def _():
        glong_ref[...] = glong
        gshort_ref[...] = jnp.zeros_like(gshort_ref)

    @pl.when(turn != 0)
    def _():
        glong_ref[...] += glong

    for g in range(3):
        total = taps[g][0] * gf_ref[g, 0:144]
        for s in range(1, 7):
            total = total + taps[g][s] * gf_ref[g, s : 144 + s]
        gfeat_ref[g] = total
        own = gf_ref[g, 0:144]
        for s in range(7):
            if g == 1:
                x = x1_ref[136 - s : 280 - s]
            else:
                x = x_ref[g // 2, 136 - s : 280 - s]
            column = jnp.sum((own * x).reshape(18, 8, 128), axis=0)
            gshort_ref[g, s : s + 1, :] += jnp.sum(column, axis=0, keepdims=True)


def hyena(side, feat, prev, nxt, up, short8, long_taps, earlier):
    def cols(*lead):
        return pl.BlockSpec(lead + (128,), lambda k: (0,) * len(lead) + (2 * k + side,))

    def filters(*lead):
        return pl.BlockSpec(lead + (128,), lambda k: (0,) * len(lead) + (side,))

    def sums(*lead):
        return pl.BlockSpec(lead + (128,), lambda k: (0,) * (len(lead) + 1))

    kept = pl.BlockSpec(memory_space=pl.ANY)
    return call(
        hyena_body,
        (
            struct((ROWS, 512), BF16),
            struct((3, ROWS, 512), F32),
            struct((128, 128), F32),
            struct((3, 8, 128), F32),
        ),
        "hyena",
        grid=(2,),
        in_specs=[
            cols(3, ROWS), cols(280), cols(288), cols(ROWS), filters(3, 8), filters(128),
        ] + [kept] * len(earlier),
        out_specs=(cols(ROWS), cols(3, ROWS), sums(128), sums(3, 8)),
        input_output_aliases={6 + i: i for i in range(len(earlier))},
        scratch_shapes=[
            pltpu.VMEM((2, 288, 128), F32),
            pltpu.VMEM((416, 128), F32),
            pltpu.VMEM((288, 128), F32),
            pltpu.VMEM((8, 288, 128), F32),
            pltpu.VMEM((280, 128), F32),
            pltpu.VMEM((8, 272, 128), F32),
            pltpu.VMEM((3, 152, 128), F32),
            pltpu.VMEM((3, 152, 128), F32),
            pltpu.VMEM((128, 8, 128), F32),
            pltpu.VMEM((128, 8, 128), F32),
        ],
    )(feat, prev, nxt, up, short8, long_taps, *earlier)


PLACES = (0, -1, -2, -3, 1, 2, 3, 4)


def part_of(side):
    return pl.BlockSpec((GROUP, 2 * HD), lambda i: (0, side))


def assemble(where_ref, pieces, out_ref, below):
    z = where_ref[0]
    for place, piece in zip(PLACES, pieces):
        block = (z + place + 8) % 8
        needed = (block <= z) if below else (block >= z)

        @pl.when(needed)
        def _():
            out_ref[pl.ds(pl.multiple_of(block * GROUP, 64), GROUP), :] = piece[...]

    spare = z + 1 if below else z - 1

    @pl.when((spare >= 0) & (spare < 8))
    def _():
        out_ref[pl.ds(pl.multiple_of(spare * GROUP, 64), GROUP), :] = jnp.zeros(
            (GROUP, 2 * HD), BF16
        )


def lane_max(x):
    best = x[:, 0:128]
    for j in range(1, CHUNK // 128):
        best = jnp.maximum(best, x[:, j * 128 : (j + 1) * 128])
    return best


def lane_sum(x):
    total = x[:, 0:128]
    for j in range(1, CHUNK // 128):
        total = total + x[:, j * 128 : (j + 1) * 128]
    return total


def query_body(where_ref, part_ref, own_ref, *refs):
    out_ref, small_ref, s_ref, mx_ref, l_ref, o_ref, st_ref, kv_ref = refs[8:]
    assemble(where_ref, refs[:8], kv_ref, True)
    first = where_ref[0] * GROUP
    clear = first // CHUNK
    total = (first + GROUP + CHUNK - 1) // CHUNK
    mx_ref[...] = jnp.full_like(mx_ref, -jnp.inf)
    l_ref[...] = jnp.zeros_like(l_ref)
    o_ref[...] = jnp.zeros_like(o_ref)

    def rows_of(c):
        return pl.ds(pl.multiple_of(c * CHUNK, CHUNK), CHUNK)

    def scores(c, masked):
        s = nt(own_ref[:, :HD], kv_ref[rows_of(c), :HD]) * (SCALE * LOG2E)
        if masked:
            q = first + lax.broadcasted_iota(jnp.int32, (GROUP, CHUNK), 0)
            k = c * CHUNK + lax.broadcasted_iota(jnp.int32, (GROUP, CHUNK), 1)
            s = jnp.where(q >= k, s, -jnp.inf)
        s_ref[c] = s
        mx_ref[...] = jnp.maximum(mx_ref[...], lane_max(s))

    @pl.loop(0, clear)
    def _(c):
        scores(c, False)

    @pl.loop(clear, total)
    def _(c):
        scores(c, True)

    peak = jnp.max(mx_ref[...], axis=1, keepdims=True)

    @pl.loop(0, total)
    def _(c):
        p = jnp.exp2(s_ref[c] - peak)
        s_ref[c] = p
        l_ref[...] += lane_sum(p)
        o_ref[...] += nn(p.astype(BF16), kv_ref[rows_of(c), HD:])

    norm = jnp.sum(l_ref[...], axis=1, keepdims=True)
    inverse = 1.0 / norm
    attended = (o_ref[...] * inverse).astype(BF16)
    out_ref[:, :HD] = attended
    delta = jnp.sum(
        own_ref[:, HD:].astype(F32) * attended.astype(F32), axis=1, keepdims=True
    )
    o_ref[...] = jnp.zeros_like(o_ref)

    @pl.loop(0, total)
    def _(c):
        rows = rows_of(c)
        gw = nt(own_ref[:, HD:], kv_ref[rows, HD:])
        gs = (s_ref[c] * (gw - delta)).astype(BF16)
        o_ref[...] += nn(gs, kv_ref[rows, :HD])

    out_ref[:, HD:] = (o_ref[...] * (inverse * SCALE)).astype(BF16)
    lane = lax.broadcasted_iota(jnp.int32, (GROUP, HD), 1)
    st_ref[0:GROUP] = jnp.where(lane == 0, peak + jnp.log2(norm), delta)
    st_ref[GROUP:640] = jnp.zeros((640 - GROUP, HD), F32)
    rows = st_ref[...].T
    for line in range(2):
        for j in range(5):
            row = rows[line : line + 1, j * 128 : (j + 1) * 128]
            small_ref[:, 5 * line + j : 5 * line + j + 1, :] = jnp.broadcast_to(
                row[None], (8, 1, 128)
            )
    for n in range(8):
        small_ref[n, 10:20] = part_ref[...]


def query_pass(where, part, own, kv):
    return call(
        query_body,
        (struct((GROUP, 2 * HD), BF16), struct((8, 20, HD), F32)),
        "query_pass",
        grid=(1,),
        in_specs=[pl.BlockSpec(memory_space=pltpu.SMEM)]
        + [pl.BlockSpec(memory_space=pltpu.VMEM)]
        + [part_of(side) for side in (0, 1, 1, 1, 0, 1, 1, 0, 0)],
        scratch_shapes=[
            pltpu.VMEM((CHUNKS, GROUP, CHUNK), F32),
            pltpu.VMEM((GROUP, HD), F32),
            pltpu.VMEM((GROUP, HD), F32),
            pltpu.VMEM((GROUP, HD), F32),
            pltpu.VMEM((640, HD), F32),
            pltpu.VMEM((SEQ, 2 * HD), BF16),
        ],
    )(where, part, own, *kv)


def key_body(where_ref, own_ref, stat_ref, *refs):
    out_ref, gk_ref, gv_ref, qd_ref = refs[8:]
    assemble(where_ref, refs[:8], qd_ref, False)
    first = where_ref[0] * GROUP
    begin = first // CHUNK
    clear = (first + GROUP - 1 + CHUNK - 1) // CHUNK
    gk_ref[...] = jnp.zeros_like(gk_ref)
    gv_ref[...] = jnp.zeros_like(gv_ref)

    def visit(c, masked):
        rows = pl.ds(pl.multiple_of(c * CHUNK, CHUNK), CHUNK)
        log_row = stat_ref[c, 0:1, :]
        delta_row = stat_ref[c, 1:2, :]
        q = qd_ref[rows, :HD]
        d = qd_ref[rows, HD:]
        s = nt(own_ref[:, :HD], q) * (SCALE * LOG2E)
        p = jnp.exp2(s - log_row)
        if masked:
            k_at = first + lax.broadcasted_iota(jnp.int32, (GROUP, CHUNK), 0)
            q_at = c * CHUNK + lax.broadcasted_iota(jnp.int32, (GROUP, CHUNK), 1)
            p = jnp.where(q_at >= k_at, p, 0.0)
        gv_ref[...] += nn(p.astype(BF16), d)
        gw = nt(own_ref[:, HD:], d)
        gs = (p * (gw - delta_row)).astype(BF16)
        gk_ref[...] += nn(gs, q)

    @pl.loop(begin, jnp.minimum(clear, CHUNKS))
    def _(c):
        visit(c, True)

    @pl.loop(clear, CHUNKS)
    def _(c):
        visit(c, False)

    out_ref[:, :HD] = (gk_ref[...] * SCALE).astype(BF16)
    out_ref[:, HD:] = gv_ref[...].astype(BF16)


def join_body(oq_ref, ok_ref, slices_ref, out_ref, part_ref):
    for n in range(8):
        part_ref[10 * n : 10 * (n + 1)] = slices_ref[n]
    for j in range(4):
        at = slice(j * ROWS, (j + 1) * ROWS)
        out_ref[j, :ROWS, : 2 * HD] = oq_ref[at]
        out_ref[j, :ROWS, 2 * HD :] = ok_ref[at]
        for side in range(2):
            value = part_ref[side * 40 : (side + 1) * 40]
            high = value.astype(BF16)
            out_ref[j, ROWS:, side * HD : (side + 1) * HD] = high
            low = (value - high.astype(F32)).astype(BF16)
            out_ref[j, ROWS:, (side + 2) * HD : (side + 3) * HD] = low


def join(out_q, out_k, part):
    return call(join_body, struct((4, ROWS + 40, 4 * HD), BF16), "join",
                scratch_shapes=[pltpu.VMEM((80, HD), F32)])(out_q, out_k, part)


def key_pass(where, own, qd, stats):
    return call(
        key_body,
        struct((GROUP, 2 * HD), BF16),
        "key_pass",
        grid=(1,),
        in_specs=[pl.BlockSpec(memory_space=pltpu.SMEM)]
        + [part_of(1)]
        + [pl.BlockSpec(memory_space=pltpu.VMEM)]
        + [part_of(0)] * 8,
        scratch_shapes=[
            pltpu.VMEM((GROUP, HD), F32),
            pltpu.VMEM((GROUP, HD), F32),
            pltpu.VMEM((SEQ, 2 * HD), BF16),
        ],
    )(where, own, stats, *qd)


def exchange(x, axis):
    return lax.all_to_all(x, axis, 0, 0, tiled=True)


def share(x, axis, count):
    return exchange(jnp.broadcast_to(x[None], (count,) + x.shape), axis)


def body(
    features, short_filter, long_filter_taps, queries, key_vectors, value_vectors,
    grad_mixed, grad_attended,
):
    feat = features.transpose(1, 0, 2)
    where = lax.axis_index("cz").astype(jnp.int32).reshape(1)
    packed, tail, rim = pack(
        queries, grad_attended, key_vectors, value_vectors, feat, grad_mixed
    )
    prev = lax.ppermute(tail, CTX, [(i, i + 1) for i in range(31)])
    nxt = lax.ppermute(rim, CTX, [(i + 1, i) for i in range(31)])
    own = exchange(packed, "cy").reshape(GROUP, 4 * HD)
    own, prev, nxt = lax.optimization_barrier((own, prev, nxt))
    rising, falling = [own], [own]

    def shift(x, by):
        return lax.ppermute(x, "cz", [(i, (i + by) % 8) for i in range(8)])

    def step():
        rising.append(shift(rising[-1], 1))
        falling.append(shift(falling[-1], -1))

    def order(*values):
        held = lax.optimization_barrier((rising[-1], falling[-1]) + values)
        rising[-1], falling[-1] = held[:2]
        return held[2:]

    short8 = jnp.pad(short_filter, ((0, 0), (0, 1), (0, 0)))
    step()
    first = hyena(0, feat, prev, nxt, grad_mixed, short8, long_filter_taps, ())
    first = order(*first)
    step()
    second = hyena(1, feat, prev, nxt, grad_mixed, short8, long_filter_taps, first[:2])
    mixed, gfeat, glong, gshort = order(*second)
    z = where[0]
    low, high = 0, 2 * HD
    up_side = jnp.where((z >= 2) & (z <= 6), high, low)
    down_side = jnp.where((z >= 1) & (z <= 5), low, high)
    rising.append(shift(lax.dynamic_slice(rising[2], (0, up_side), (GROUP, 2 * HD)), 1))
    falling.append(shift(lax.dynamic_slice(falling[2], (0, down_side), (GROUP, 2 * HD)), -1))
    grads = jnp.concatenate(
        [first[2], glong, first[3].reshape(24, HD), gshort.reshape(24, HD), jnp.zeros((16, HD), F32)],
        0,
    )
    part = jnp.sum(exchange(grads.reshape(32, 10, HD), YFT), axis=0)
    order()
    far_kv = lax.ppermute(rising[3], "cz", [(i, i + 1) for i in range(3, 7)])
    far_qd = lax.ppermute(falling[3], "cz", [(i, i - 1) for i in range(1, 5)])
    far_kv, far_qd, own = lax.optimization_barrier((far_kv, far_qd, own))
    pieces = [own] + rising[1:] + falling[1:]

    out_q, small = query_pass(where, part, own, pieces + [far_kv])
    small = exchange(small, "cz")
    part = share(jnp.sum(small[:, 10:], axis=0), FT, 8)
    stats = small[:, :10].reshape(8, 2, 640)[:, :, :GROUP].transpose(1, 0, 2)
    stats = stats.reshape(2, CHUNKS, CHUNK).transpose(1, 0, 2)
    out_k = key_pass(where, own, pieces + [far_qd], stats)
    result = join(out_q, out_k, part)
    attended, grad_queries, grad_keys, grad_values, grad_long, grad_short = unpack(
        exchange(result, "cy")
    )
    return (
        mixed, attended, gfeat.transpose(1, 0, 2), grad_short, grad_long,
        grad_queries, grad_keys, grad_values,
    )


def solution(mesh):
    fine = Mesh(np.asarray(mesh.devices).reshape(8, 4, 4, 2), ("cz", "cy", "fsdp", "tp"))
    rows = P(CTX, FT)
    wide = P(CTX, None, FT)
    return jax.shard_map(
        body,
        mesh=fine,
        in_specs=(wide, P(), P(), rows, rows, rows, rows, rows),
        out_specs=(rows, rows, wide, P(), P(), rows, rows, rows),
        check_vma=False,
    )
```

```python
import jax
import jax.numpy as jnp
import numpy as np
from jax import lax
from jax.experimental import pallas as pl
from jax.experimental.pallas import tpu as pltpu
from jax.sharding import Mesh, PartitionSpec as P

HD = 128
ROWS = 144
GROUP = 576
SEQ = 4608
CHUNK = 512
CHUNKS = SEQ // CHUNK
LOG2E = 1.4426950408889634
SCALE = HD ** -0.5
VMEM_BYTES = 56 * 1024 * 1024
F32 = jnp.float32
BF16 = jnp.bfloat16
CTX = ("cz", "cy")
FT = ("fsdp", "tp")
YFT = ("cy", "fsdp", "tp")


def after(value, *others):
    return lax.optimization_barrier((value,) + others)[0]


def call(body, out_shape, name, **options):
    return pl.pallas_call(
        body,
        out_shape=out_shape,
        name=name,
        compiler_params=pltpu.CompilerParams(vmem_limit_bytes=VMEM_BYTES),
        **options,
    )


def struct(shape, dtype):
    return jax.ShapeDtypeStruct(shape, dtype)


def nt(a, b):
    return lax.dot_general(a, b, (((1,), (1,)), ((), ())), preferred_element_type=F32)


def nn(a, b):
    return lax.dot_general(a, b, (((1,), (0,)), ((), ())), preferred_element_type=F32)


def pack_body(q_ref, d_ref, k_ref, v_ref, feat_ref, up_ref, out_ref, tail_ref, rim_ref):
    for h in range(4):
        for slot, ref in enumerate((q_ref, d_ref, k_ref, v_ref)):
            out_ref[h, :, slot * HD : (slot + 1) * HD] = ref[:, h * HD : (h + 1) * HD]
    tail_ref[0:136] = feat_ref[0, 8:]
    tail_ref[136:272] = feat_ref[2, 8:]
    tail_ref[272:280] = feat_ref[1, 136:]
    rim_ref[0:136] = feat_ref[1, 0:136]
    rim_ref[136:272] = up_ref[0:136]
    rim_ref[272:280] = feat_ref[0, 0:8]
    rim_ref[280:288] = feat_ref[2, 0:8]


def pack(*parts):
    return call(
        pack_body,
        (
            struct((4, ROWS, 4 * HD), BF16),
            struct((280, 4 * HD), BF16),
            struct((288, 4 * HD), BF16),
        ),
        "pack",
    )(*parts)


def unpack_body(x_ref, attended_ref, gq_ref, gk_ref, gv_ref, glong_ref, gshort_ref, grads_ref):
    for h in range(4):
        at = slice(h * HD, (h + 1) * HD)
        attended_ref[:, at] = x_ref[h, :ROWS, 0:HD]
        gq_ref[:, at] = x_ref[h, :ROWS, HD : 2 * HD].astype(F32)
        gk_ref[:, at] = x_ref[h, :ROWS, 2 * HD : 3 * HD].astype(F32)
        gv_ref[:, at] = x_ref[h, :ROWS, 3 * HD :].astype(F32)
        for c in range(4):
            first = 80 * h + 20 * c
            piece = x_ref[h, ROWS : ROWS + 20, c * HD : (c + 1) * HD]
            grads_ref[first : first + 20] = piece.astype(F32)
    for side in range(2):
        at = slice(side * HD, (side + 1) * HD)
        glong_ref[:, at] = grads_ref[128 * side : 128 * (side + 1)]
        for g in range(3):
            first = 256 + 24 * side + 8 * g
            gshort_ref[g, :, at] = grads_ref[first : first + 7]


def unpack(x):
    whole = struct((ROWS, 4 * HD), F32)
    return call(
        unpack_body,
        (
            struct((ROWS, 4 * HD), BF16), whole, whole, whole,
            struct((128, 256), F32), struct((3, 7, 256), F32),
        ),
        "unpack",
        scratch_shapes=[pltpu.VMEM((320, HD), F32)],
    )(x)


def hyena_body(feat_ref, prev_ref, next_ref, up_ref, short_ref, long_ref, *refs):
    (
        mixed_ref, gfeat_ref, glong_ref, gshort_ref,
        x_ref, x1_ref, p_ref, ps_ref, gm_ref, gs_ref, f_ref, gf_ref, wb_ref, gl_ref,
    ) = refs[-14:]
    turn = pl.program_id(0)
    for slot, g in enumerate((0, 2)):
        x_ref[slot, 0:136] = prev_ref[136 * slot : 136 * (slot + 1)].astype(F32)
        x_ref[slot, 136:280] = feat_ref[g].astype(F32)
        x_ref[slot, 280:288] = next_ref[272 + 8 * slot : 280 + 8 * slot].astype(F32)
    x1_ref[128:136] = prev_ref[272:280].astype(F32)
    x1_ref[136:280] = feat_ref[1].astype(F32)
    x1_ref[280:416] = next_ref[0:136].astype(F32)
    taps = [[short_ref[g, s : s + 1, :] for s in range(7)] for g in range(3)]

    def featured(read, g):
        total = taps[g][0] * read(0)
        for s in range(1, 7):
            total = total + taps[g][s] * read(s)
        return total

    f0 = featured(lambda s: x_ref[0, 8 - s : 288 - s], 0)
    f2 = featured(lambda s: x_ref[1, 8 - s : 288 - s], 2)
    p_ref[8:288] = f0 * f2
    f_ref[0] = f0[128:280]
    f_ref[2] = f2[128:280]
    f1 = featured(lambda s: x1_ref[136 - s : 416 - s], 1)
    f_ref[1] = f1[0:152]
    gm_ref[0:144] = up_ref[...].astype(F32) * f1[0:144]
    gm_ref[144:280] = next_ref[136:272].astype(F32) * f1[144:280]
    for b in range(8):
        ps_ref[b, 16:288] = p_ref[16 - b : 288 - b]
        gs_ref[b] = gm_ref[b : 272 + b]
    wb_ref[...] = jnp.broadcast_to(long_ref[...][:, None, :], (128, 8, 128))

    def forward(a, total):
        base = pl.multiple_of(136 - 8 * a, 8)
        for b in range(8):
            tap = 8 * a + b
            x = ps_ref[b, pl.ds(base, 152), :].reshape(19, 8, 128)
            total = total + wb_ref[tap][None] * x
            gm = gm_ref[0:144].reshape(18, 8, 128)
            gl_ref[tap] = jnp.sum(gm * x[:18], axis=0)
        return total

    memory = lax.fori_loop(0, 16, forward, jnp.zeros((19, 8, 128), F32)).reshape(152, 128)
    mixed_ref[...] = (f_ref[1, 0:144] * memory[0:144]).astype(BF16)
    gf_ref[1, 0:144] = up_ref[...].astype(F32) * memory[0:144]
    gf_ref[1, 144:152] = next_ref[136:144].astype(F32) * memory[144:152]

    def backward(a, total):
        base = pl.multiple_of(8 * a, 8)
        for b in range(8):
            y = gs_ref[b, pl.ds(base, 152), :].reshape(19, 8, 128)
            total = total + wb_ref[8 * a + b][None] * y
        return total

    gp = lax.fori_loop(0, 16, backward, jnp.zeros((19, 8, 128), F32)).reshape(152, 128)
    gf_ref[0] = gp * f_ref[2]
    gf_ref[2] = gp * f_ref[0]
    glong = jnp.sum(gl_ref[...], axis=1)

    @pl.when(turn == 0)
    def _():
        glong_ref[...] = glong
        gshort_ref[...] = jnp.zeros_like(gshort_ref)

    @pl.when(turn != 0)
    def _():
        glong_ref[...] += glong

    for g in range(3):
        total = taps[g][0] * gf_ref[g, 0:144]
        for s in range(1, 7):
            total = total + taps[g][s] * gf_ref[g, s : 144 + s]
        gfeat_ref[g] = total
        own = gf_ref[g, 0:144]
        for s in range(7):
            if g == 1:
                x = x1_ref[136 - s : 280 - s]
            else:
                x = x_ref[g // 2, 136 - s : 280 - s]
            column = jnp.sum((own * x).reshape(18, 8, 128), axis=0)
            gshort_ref[g, s : s + 1, :] += jnp.sum(column, axis=0, keepdims=True)


def hyena(side, feat, prev, nxt, up, short8, long_taps, earlier):
    def cols(*lead):
        return pl.BlockSpec(lead + (128,), lambda k: (0,) * len(lead) + (2 * k + side,))

    def filters(*lead):
        return pl.BlockSpec(lead + (128,), lambda k: (0,) * len(lead) + (side,))

    def sums(*lead):
        return pl.BlockSpec(lead + (128,), lambda k: (0,) * (len(lead) + 1))

    kept = pl.BlockSpec(memory_space=pl.ANY)
    return call(
        hyena_body,
        (
            struct((ROWS, 512), BF16),
            struct((3, ROWS, 512), F32),
            struct((128, 128), F32),
            struct((3, 8, 128), F32),
        ),
        "hyena",
        grid=(2,),
        in_specs=[
            cols(3, ROWS), cols(280), cols(288), cols(ROWS), filters(3, 8), filters(128),
        ] + [kept] * len(earlier),
        out_specs=(cols(ROWS), cols(3, ROWS), sums(128), sums(3, 8)),
        input_output_aliases={6 + i: i for i in range(len(earlier))},
        scratch_shapes=[
            pltpu.VMEM((2, 288, 128), F32),
            pltpu.VMEM((416, 128), F32),
            pltpu.VMEM((288, 128), F32),
            pltpu.VMEM((8, 288, 128), F32),
            pltpu.VMEM((280, 128), F32),
            pltpu.VMEM((8, 272, 128), F32),
            pltpu.VMEM((3, 152, 128), F32),
            pltpu.VMEM((3, 152, 128), F32),
            pltpu.VMEM((128, 8, 128), F32),
            pltpu.VMEM((128, 8, 128), F32),
        ],
    )(feat, prev, nxt, up, short8, long_taps, *earlier)


PLACES = (0, -1, -2, -3, 1, 2, 3, 4)


def part_of(side):
    return pl.BlockSpec((GROUP, 2 * HD), lambda i: (0, side))


def assemble(where_ref, pieces, out_ref, below):
    z = where_ref[0]
    for place, piece in zip(PLACES, pieces):
        block = (z + place + 8) % 8
        needed = (block <= z) if below else (block >= z)

        @pl.when(needed)
        def _():
            out_ref[pl.ds(pl.multiple_of(block * GROUP, 64), GROUP), :] = piece[...]

    spare = z + 1 if below else z - 1

    @pl.when((spare >= 0) & (spare < 8))
    def _():
        out_ref[pl.ds(pl.multiple_of(spare * GROUP, 64), GROUP), :] = jnp.zeros(
            (GROUP, 2 * HD), BF16
        )


def lane_max(x):
    best = x[:, 0:128]
    for j in range(1, CHUNK // 128):
        best = jnp.maximum(best, x[:, j * 128 : (j + 1) * 128])
    return best


def lane_sum(x):
    total = x[:, 0:128]
    for j in range(1, CHUNK // 128):
        total = total + x[:, j * 128 : (j + 1) * 128]
    return total


def query_body(where_ref, own_ref, *refs):
    out_ref, small_ref, s_ref, mx_ref, l_ref, o_ref, st_ref, kv_ref = refs[8:]
    assemble(where_ref, refs[:8], kv_ref, True)
    first = where_ref[0] * GROUP
    clear = first // CHUNK
    total = (first + GROUP + CHUNK - 1) // CHUNK
    mx_ref[...] = jnp.full_like(mx_ref, -jnp.inf)
    l_ref[...] = jnp.zeros_like(l_ref)
    o_ref[...] = jnp.zeros_like(o_ref)

    def rows_of(c):
        return pl.ds(pl.multiple_of(c * CHUNK, CHUNK), CHUNK)

    def scores(c, masked):
        s = nt(own_ref[:, :HD], kv_ref[rows_of(c), :HD]) * (SCALE * LOG2E)
        if masked:
            q = first + lax.broadcasted_iota(jnp.int32, (GROUP, CHUNK), 0)
            k = c * CHUNK + lax.broadcasted_iota(jnp.int32, (GROUP, CHUNK), 1)
            s = jnp.where(q >= k, s, -jnp.inf)
        s_ref[c] = s
        mx_ref[...] = jnp.maximum(mx_ref[...], lane_max(s))

    @pl.loop(0, clear)
    def _(c):
        scores(c, False)

    @pl.loop(clear, total)
    def _(c):
        scores(c, True)

    peak = jnp.max(mx_ref[...], axis=1, keepdims=True)

    @pl.loop(0, total)
    def _(c):
        p = jnp.exp2(s_ref[c] - peak)
        s_ref[c] = p
        l_ref[...] += lane_sum(p)
        o_ref[...] += nn(p.astype(BF16), kv_ref[rows_of(c), HD:])

    norm = jnp.sum(l_ref[...], axis=1, keepdims=True)
    inverse = 1.0 / norm
    attended = (o_ref[...] * inverse).astype(BF16)
    out_ref[:, :HD] = attended
    delta = jnp.sum(
        own_ref[:, HD:].astype(F32) * attended.astype(F32), axis=1, keepdims=True
    )
    o_ref[...] = jnp.zeros_like(o_ref)

    @pl.loop(0, total)
    def _(c):
        rows = rows_of(c)
        gw = nt(own_ref[:, HD:], kv_ref[rows, HD:])
        gs = (s_ref[c] * (gw - delta)).astype(BF16)
        o_ref[...] += nn(gs, kv_ref[rows, :HD])

    out_ref[:, HD:] = (o_ref[...] * (inverse * SCALE)).astype(BF16)
    lane = lax.broadcasted_iota(jnp.int32, (GROUP, HD), 1)
    st_ref[0:GROUP] = jnp.where(lane == 0, peak + jnp.log2(norm), delta)
    st_ref[GROUP:640] = jnp.zeros((640 - GROUP, HD), F32)
    rows = st_ref[...].T
    for line in range(2):
        for j in range(5):
            row = rows[line : line + 1, j * 128 : (j + 1) * 128]
            small_ref[:, 5 * line + j : 5 * line + j + 1, :] = jnp.broadcast_to(
                row[None], (8, 1, 128)
            )


def query_pass(where, own, kv):
    return call(
        query_body,
        (struct((GROUP, 2 * HD), BF16), struct((8, 10, HD), F32)),
        "query_pass",
        grid=(1,),
        in_specs=[pl.BlockSpec(memory_space=pltpu.SMEM)]
        + [part_of(side) for side in (0, 1, 1, 1, 0, 1, 1, 0, 0)],
        scratch_shapes=[
            pltpu.VMEM((CHUNKS, GROUP, CHUNK), F32),
            pltpu.VMEM((GROUP, HD), F32),
            pltpu.VMEM((GROUP, HD), F32),
            pltpu.VMEM((GROUP, HD), F32),
            pltpu.VMEM((640, HD), F32),
            pltpu.VMEM((SEQ, 2 * HD), BF16),
        ],
    )(where, own, *kv)


def key_body(where_ref, own_ref, stat_ref, *refs):
    out_ref, gk_ref, gv_ref, qd_ref = refs[8:]
    assemble(where_ref, refs[:8], qd_ref, False)
    first = where_ref[0] * GROUP
    begin = first // CHUNK
    clear = (first + GROUP - 1 + CHUNK - 1) // CHUNK
    gk_ref[...] = jnp.zeros_like(gk_ref)
    gv_ref[...] = jnp.zeros_like(gv_ref)

    def visit(c, masked):
        rows = pl.ds(pl.multiple_of(c * CHUNK, CHUNK), CHUNK)
        log_row = stat_ref[c, 0:1, :]
        delta_row = stat_ref[c, 1:2, :]
        q = qd_ref[rows, :HD]
        d = qd_ref[rows, HD:]
        s = nt(own_ref[:, :HD], q) * (SCALE * LOG2E)
        p = jnp.exp2(s - log_row)
        if masked:
            k_at = first + lax.broadcasted_iota(jnp.int32, (GROUP, CHUNK), 0)
            q_at = c * CHUNK + lax.broadcasted_iota(jnp.int32, (GROUP, CHUNK), 1)
            p = jnp.where(q_at >= k_at, p, 0.0)
        gv_ref[...] += nn(p.astype(BF16), d)
        gw = nt(own_ref[:, HD:], d)
        gs = (p * (gw - delta_row)).astype(BF16)
        gk_ref[...] += nn(gs, q)

    @pl.loop(begin, jnp.minimum(clear, CHUNKS))
    def _(c):
        visit(c, True)

    @pl.loop(clear, CHUNKS)
    def _(c):
        visit(c, False)

    out_ref[:, :HD] = (gk_ref[...] * SCALE).astype(BF16)
    out_ref[:, HD:] = gv_ref[...].astype(BF16)


def join_body(oq_ref, ok_ref, slices_ref, out_ref, part_ref):
    for n in range(8):
        part_ref[10 * n : 10 * (n + 1)] = slices_ref[n]
    for j in range(4):
        at = slice(j * ROWS, (j + 1) * ROWS)
        out_ref[j, :ROWS, : 2 * HD] = oq_ref[at]
        out_ref[j, :ROWS, 2 * HD :] = ok_ref[at]
        for c in range(4):
            value = part_ref[20 * c : 20 * (c + 1)].astype(BF16)
            out_ref[j, ROWS : ROWS + 20, c * HD : (c + 1) * HD] = value
        out_ref[j, ROWS + 20 :] = jnp.zeros((4, 4 * HD), BF16)


def join(out_q, out_k, part):
    return call(join_body, struct((4, ROWS + 24, 4 * HD), BF16), "join",
                scratch_shapes=[pltpu.VMEM((80, HD), F32)])(out_q, out_k, part)


def key_pass(where, own, qd, stats):
    return call(
        key_body,
        struct((GROUP, 2 * HD), BF16),
        "key_pass",
        grid=(1,),
        in_specs=[pl.BlockSpec(memory_space=pltpu.SMEM)]
        + [part_of(1)]
        + [pl.BlockSpec(memory_space=pltpu.VMEM)]
        + [part_of(0)] * 8,
        scratch_shapes=[
            pltpu.VMEM((GROUP, HD), F32),
            pltpu.VMEM((GROUP, HD), F32),
            pltpu.VMEM((SEQ, 2 * HD), BF16),
        ],
    )(where, own, stats, *qd)


def exchange(x, axis):
    return lax.all_to_all(x, axis, 0, 0, tiled=True)


def share(x, axis, count):
    return exchange(jnp.broadcast_to(x[None], (count,) + x.shape), axis)


def body(
    features, short_filter, long_filter_taps, queries, key_vectors, value_vectors,
    grad_mixed, grad_attended,
):
    feat = features.transpose(1, 0, 2)
    where = lax.axis_index("cz").astype(jnp.int32).reshape(1)
    packed, tail, rim = pack(
        queries, grad_attended, key_vectors, value_vectors, feat, grad_mixed
    )
    prev = lax.ppermute(tail, CTX, [(i, i + 1) for i in range(31)])
    nxt = lax.ppermute(rim, CTX, [(i + 1, i) for i in range(31)])
    own = exchange(packed, "cy").reshape(GROUP, 4 * HD)
    own, prev, nxt = lax.optimization_barrier((own, prev, nxt))
    rising, falling = [own], [own]

    def shift(x, by):
        return lax.ppermute(x, "cz", [(i, (i + by) % 8) for i in range(8)])

    def step():
        rising.append(shift(rising[-1], 1))
        falling.append(shift(falling[-1], -1))

    def order(*values):
        held = lax.optimization_barrier((rising[-1], falling[-1]) + values)
        rising[-1], falling[-1] = held[:2]
        return held[2:]

    short8 = jnp.pad(short_filter, ((0, 0), (0, 1), (0, 0)))
    step()
    first = hyena(0, feat, prev, nxt, grad_mixed, short8, long_filter_taps, ())
    first = order(*first)
    step()
    second = hyena(1, feat, prev, nxt, grad_mixed, short8, long_filter_taps, first[:2])
    mixed, gfeat, glong, gshort = order(*second)
    z = where[0]
    low, high = 0, 2 * HD
    up_side = jnp.where((z >= 2) & (z <= 6), high, low)
    down_side = jnp.where((z >= 1) & (z <= 5), low, high)
    rising.append(shift(lax.dynamic_slice(rising[2], (0, up_side), (GROUP, 2 * HD)), 1))
    falling.append(shift(lax.dynamic_slice(falling[2], (0, down_side), (GROUP, 2 * HD)), -1))
    grads = jnp.concatenate(
        [first[2], glong, first[3].reshape(24, HD), gshort.reshape(24, HD), jnp.zeros((16, HD), F32)],
        0,
    )
    order()
    far_kv = lax.ppermute(rising[3], "cz", [(i, i + 1) for i in range(3, 7)])
    far_qd = lax.ppermute(falling[3], "cz", [(i, i - 1) for i in range(1, 5)])
    far_kv, far_qd, own = lax.optimization_barrier((far_kv, far_qd, own))
    pieces = [own] + rising[1:] + falling[1:]

    received = exchange(after(grads, own).reshape(32, 10, HD), YFT)
    out_q, small = query_pass(where, own, pieces + [far_kv])
    part = jnp.sum(received, axis=0)
    small = jnp.concatenate([small, jnp.broadcast_to(part[None], (8, 10, HD))], 1)
    small = exchange(small, "cz")
    part = share(jnp.sum(small[:, 10:], axis=0), FT, 8)
    stats = small[:, :10].reshape(8, 2, 640)[:, :, :GROUP].transpose(1, 0, 2)
    stats = stats.reshape(2, CHUNKS, CHUNK).transpose(1, 0, 2)
    out_k = key_pass(where, own, pieces + [far_qd], stats)
    result = join(out_q, out_k, part)
    attended, grad_queries, grad_keys, grad_values, grad_long, grad_short = unpack(
        exchange(result, "cy")
    )
    return (
        mixed, attended, gfeat.transpose(1, 0, 2), grad_short, grad_long,
        grad_queries, grad_keys, grad_values,
    )


def solution(mesh):
    fine = Mesh(np.asarray(mesh.devices).reshape(8, 4, 4, 2), ("cz", "cy", "fsdp", "tp"))
    rows = P(CTX, FT)
    wide = P(CTX, None, FT)
    return jax.shard_map(
        body,
        mesh=fine,
        in_specs=(wide, P(), P(), rows, rows, rows, rows, rows),
        out_specs=(rows, rows, wide, P(), P(), rows, rows, rows),
        check_vma=False,
    )
```

```python
import jax
import jax.numpy as jnp
import numpy as np
from jax import lax
from jax.experimental import pallas as pl
from jax.experimental.pallas import tpu as pltpu
from jax.sharding import Mesh, PartitionSpec as P

HD = 128
ROWS = 144
GROUP = 576
SEQ = 4608
CHUNK = 1536
CHUNKS = SEQ // CHUNK
LOG2E = 1.4426950408889634
SCALE = HD ** -0.5
VMEM_BYTES = 56 * 1024 * 1024
F32 = jnp.float32
BF16 = jnp.bfloat16
CTX = ("cz", "cy")
FT = ("fsdp", "tp")
YFT = ("cy", "fsdp", "tp")


def after(value, *others):
    return lax.optimization_barrier((value,) + others)[0]


def call(body, out_shape, name, **options):
    return pl.pallas_call(
        body,
        out_shape=out_shape,
        name=name,
        compiler_params=pltpu.CompilerParams(vmem_limit_bytes=VMEM_BYTES),
        **options,
    )


def struct(shape, dtype):
    return jax.ShapeDtypeStruct(shape, dtype)


def nt(a, b):
    return lax.dot_general(a, b, (((1,), (1,)), ((), ())), preferred_element_type=F32)


def nn(a, b):
    return lax.dot_general(a, b, (((1,), (0,)), ((), ())), preferred_element_type=F32)


def pack_body(q_ref, d_ref, k_ref, v_ref, feat_ref, up_ref, out_ref, tail_ref, rim_ref):
    for h in range(4):
        for slot, ref in enumerate((q_ref, d_ref, k_ref, v_ref)):
            out_ref[h, :, slot * HD : (slot + 1) * HD] = ref[:, h * HD : (h + 1) * HD]
    tail_ref[0:136] = feat_ref[0, 8:]
    tail_ref[136:272] = feat_ref[2, 8:]
    tail_ref[272:280] = feat_ref[1, 136:]
    rim_ref[0:136] = feat_ref[1, 0:136]
    rim_ref[136:272] = up_ref[0:136]
    rim_ref[272:280] = feat_ref[0, 0:8]
    rim_ref[280:288] = feat_ref[2, 0:8]


def pack(*parts):
    return call(
        pack_body,
        (
            struct((4, ROWS, 4 * HD), BF16),
            struct((280, 4 * HD), BF16),
            struct((288, 4 * HD), BF16),
        ),
        "pack",
    )(*parts)


def unpack_body(x_ref, attended_ref, gq_ref, gk_ref, gv_ref, glong_ref, gshort_ref, grads_ref):
    for h in range(4):
        at = slice(h * HD, (h + 1) * HD)
        attended_ref[:, at] = x_ref[h, :ROWS, 0:HD]
        gq_ref[:, at] = x_ref[h, :ROWS, HD : 2 * HD].astype(F32)
        gk_ref[:, at] = x_ref[h, :ROWS, 2 * HD : 3 * HD].astype(F32)
        gv_ref[:, at] = x_ref[h, :ROWS, 3 * HD :].astype(F32)
        for c in range(4):
            first = 80 * h + 20 * c
            piece = x_ref[h, ROWS : ROWS + 20, c * HD : (c + 1) * HD]
            grads_ref[first : first + 20] = piece.astype(F32)
    for side in range(2):
        at = slice(side * HD, (side + 1) * HD)
        glong_ref[:, at] = grads_ref[128 * side : 128 * (side + 1)]
        for g in range(3):
            first = 256 + 24 * side + 8 * g
            gshort_ref[g, :, at] = grads_ref[first : first + 7]


def unpack(x):
    whole = struct((ROWS, 4 * HD), F32)
    return call(
        unpack_body,
        (
            struct((ROWS, 4 * HD), BF16), whole, whole, whole,
            struct((128, 256), F32), struct((3, 7, 256), F32),
        ),
        "unpack",
        scratch_shapes=[pltpu.VMEM((320, HD), F32)],
    )(x)


def hyena_body(feat_ref, prev_ref, next_ref, up_ref, short_ref, long_ref, *refs):
    (
        mixed_ref, gfeat_ref, glong_ref, gshort_ref,
        x_ref, x1_ref, p_ref, ps_ref, gm_ref, gs_ref, f_ref, gf_ref, wb_ref, gl_ref,
    ) = refs[-14:]
    turn = pl.program_id(0)
    for slot, g in enumerate((0, 2)):
        x_ref[slot, 0:136] = prev_ref[136 * slot : 136 * (slot + 1)].astype(F32)
        x_ref[slot, 136:280] = feat_ref[g].astype(F32)
        x_ref[slot, 280:288] = next_ref[272 + 8 * slot : 280 + 8 * slot].astype(F32)
    x1_ref[128:136] = prev_ref[272:280].astype(F32)
    x1_ref[136:280] = feat_ref[1].astype(F32)
    x1_ref[280:416] = next_ref[0:136].astype(F32)
    taps = [[short_ref[g, s : s + 1, :] for s in range(7)] for g in range(3)]

    def featured(read, g):
        total = taps[g][0] * read(0)
        for s in range(1, 7):
            total = total + taps[g][s] * read(s)
        return total

    f0 = featured(lambda s: x_ref[0, 8 - s : 288 - s], 0)
    f2 = featured(lambda s: x_ref[1, 8 - s : 288 - s], 2)
    p_ref[8:288] = f0 * f2
    f_ref[0] = f0[128:280]
    f_ref[2] = f2[128:280]
    f1 = featured(lambda s: x1_ref[136 - s : 416 - s], 1)
    f_ref[1] = f1[0:152]
    gm_ref[0:144] = up_ref[...].astype(F32) * f1[0:144]
    gm_ref[144:280] = next_ref[136:272].astype(F32) * f1[144:280]
    for b in range(8):
        ps_ref[b, 16:288] = p_ref[16 - b : 288 - b]
        gs_ref[b] = gm_ref[b : 272 + b]
    wb_ref[...] = jnp.broadcast_to(long_ref[...][:, None, :], (128, 8, 128))

    def forward(a, total):
        base = pl.multiple_of(136 - 8 * a, 8)
        for b in range(8):
            tap = 8 * a + b
            x = ps_ref[b, pl.ds(base, 152), :].reshape(19, 8, 128)
            total = total + wb_ref[tap][None] * x
            gm = gm_ref[0:144].reshape(18, 8, 128)
            gl_ref[tap] = jnp.sum(gm * x[:18], axis=0)
        return total

    memory = lax.fori_loop(0, 16, forward, jnp.zeros((19, 8, 128), F32)).reshape(152, 128)
    mixed_ref[...] = (f_ref[1, 0:144] * memory[0:144]).astype(BF16)
    gf_ref[1, 0:144] = up_ref[...].astype(F32) * memory[0:144]
    gf_ref[1, 144:152] = next_ref[136:144].astype(F32) * memory[144:152]

    def backward(a, total):
        base = pl.multiple_of(8 * a, 8)
        for b in range(8):
            y = gs_ref[b, pl.ds(base, 152), :].reshape(19, 8, 128)
            total = total + wb_ref[8 * a + b][None] * y
        return total

    gp = lax.fori_loop(0, 16, backward, jnp.zeros((19, 8, 128), F32)).reshape(152, 128)
    gf_ref[0] = gp * f_ref[2]
    gf_ref[2] = gp * f_ref[0]
    glong = jnp.sum(gl_ref[...], axis=1)

    @pl.when(turn == 0)
    def _():
        glong_ref[...] = glong
        gshort_ref[...] = jnp.zeros_like(gshort_ref)

    @pl.when(turn != 0)
    def _():
        glong_ref[...] += glong

    for g in range(3):
        total = taps[g][0] * gf_ref[g, 0:144]
        for s in range(1, 7):
            total = total + taps[g][s] * gf_ref[g, s : 144 + s]
        gfeat_ref[g] = total
        own = gf_ref[g, 0:144]
        for s in range(7):
            if g == 1:
                x = x1_ref[136 - s : 280 - s]
            else:
                x = x_ref[g // 2, 136 - s : 280 - s]
            column = jnp.sum((own * x).reshape(18, 8, 128), axis=0)
            gshort_ref[g, s : s + 1, :] += jnp.sum(column, axis=0, keepdims=True)


def hyena(side, feat, prev, nxt, up, short8, long_taps, earlier):
    def cols(*lead):
        return pl.BlockSpec(lead + (128,), lambda k: (0,) * len(lead) + (2 * k + side,))

    def filters(*lead):
        return pl.BlockSpec(lead + (128,), lambda k: (0,) * len(lead) + (side,))

    def sums(*lead):
        return pl.BlockSpec(lead + (128,), lambda k: (0,) * (len(lead) + 1))

    kept = pl.BlockSpec(memory_space=pl.ANY)
    return call(
        hyena_body,
        (
            struct((ROWS, 512), BF16),
            struct((3, ROWS, 512), F32),
            struct((128, 128), F32),
            struct((3, 8, 128), F32),
        ),
        "hyena",
        grid=(2,),
        in_specs=[
            cols(3, ROWS), cols(280), cols(288), cols(ROWS), filters(3, 8), filters(128),
        ] + [kept] * len(earlier),
        out_specs=(cols(ROWS), cols(3, ROWS), sums(128), sums(3, 8)),
        input_output_aliases={6 + i: i for i in range(len(earlier))},
        scratch_shapes=[
            pltpu.VMEM((2, 288, 128), F32),
            pltpu.VMEM((416, 128), F32),
            pltpu.VMEM((288, 128), F32),
            pltpu.VMEM((8, 288, 128), F32),
            pltpu.VMEM((280, 128), F32),
            pltpu.VMEM((8, 272, 128), F32),
            pltpu.VMEM((3, 152, 128), F32),
            pltpu.VMEM((3, 152, 128), F32),
            pltpu.VMEM((128, 8, 128), F32),
            pltpu.VMEM((128, 8, 128), F32),
        ],
    )(feat, prev, nxt, up, short8, long_taps, *earlier)


PLACES = (0, -1, -2, -3, 1, 2, 3, 4)


def part_of(side):
    return pl.BlockSpec((GROUP, 2 * HD), lambda i: (0, side))


def assemble(where_ref, pieces, out_ref, below):
    z = where_ref[0]
    for place, piece in zip(PLACES, pieces):
        block = (z + place + 8) % 8
        needed = (block <= z) if below else (block >= z)

        at = pl.ds(pl.multiple_of(block * GROUP, 64), GROUP)

        @pl.when(needed)
        def _():
            out_ref[at, :] = piece[...]

        @pl.when(jnp.logical_not(needed))
        def _():
            out_ref[at, :] = jnp.zeros((GROUP, 2 * HD), BF16)


def lane_max(x):
    best = x[:, 0:128]
    for j in range(1, CHUNK // 128):
        best = jnp.maximum(best, x[:, j * 128 : (j + 1) * 128])
    return best


def lane_sum(x):
    total = x[:, 0:128]
    for j in range(1, CHUNK // 128):
        total = total + x[:, j * 128 : (j + 1) * 128]
    return total


def query_body(where_ref, own_ref, *refs):
    out_ref, small_ref, s_ref, mx_ref, l_ref, o_ref, st_ref, kv_ref = refs[8:]
    assemble(where_ref, refs[:8], kv_ref, True)
    first = where_ref[0] * GROUP
    clear = first // CHUNK
    total = (first + GROUP + CHUNK - 1) // CHUNK
    mx_ref[...] = jnp.full_like(mx_ref, -jnp.inf)
    l_ref[...] = jnp.zeros_like(l_ref)
    o_ref[...] = jnp.zeros_like(o_ref)

    def rows_of(c):
        return pl.ds(pl.multiple_of(c * CHUNK, CHUNK), CHUNK)

    def scores(c, masked):
        s = nt(own_ref[:, :HD], kv_ref[rows_of(c), :HD]) * (SCALE * LOG2E)
        if masked:
            q = first + lax.broadcasted_iota(jnp.int32, (GROUP, CHUNK), 0)
            k = c * CHUNK + lax.broadcasted_iota(jnp.int32, (GROUP, CHUNK), 1)
            s = jnp.where(q >= k, s, -jnp.inf)
        s_ref[c] = s
        mx_ref[...] = jnp.maximum(mx_ref[...], lane_max(s))

    @pl.loop(0, clear)
    def _(c):
        scores(c, False)

    @pl.loop(clear, total)
    def _(c):
        scores(c, True)

    peak = jnp.max(mx_ref[...], axis=1, keepdims=True)

    @pl.loop(0, total)
    def _(c):
        p = jnp.exp2(s_ref[c] - peak)
        s_ref[c] = p
        l_ref[...] += lane_sum(p)
        o_ref[...] += nn(p.astype(BF16), kv_ref[rows_of(c), HD:])

    norm = jnp.sum(l_ref[...], axis=1, keepdims=True)
    inverse = 1.0 / norm
    attended = (o_ref[...] * inverse).astype(BF16)
    out_ref[:, :HD] = attended
    delta = jnp.sum(
        own_ref[:, HD:].astype(F32) * attended.astype(F32), axis=1, keepdims=True
    )
    o_ref[...] = jnp.zeros_like(o_ref)

    @pl.loop(0, total)
    def _(c):
        rows = rows_of(c)
        gw = nt(own_ref[:, HD:], kv_ref[rows, HD:])
        gs = (s_ref[c] * (gw - delta)).astype(BF16)
        o_ref[...] += nn(gs, kv_ref[rows, :HD])

    out_ref[:, HD:] = (o_ref[...] * (inverse * SCALE)).astype(BF16)
    lane = lax.broadcasted_iota(jnp.int32, (GROUP, HD), 1)
    st_ref[0:GROUP] = jnp.where(lane == 0, peak + jnp.log2(norm), delta)
    st_ref[GROUP:640] = jnp.zeros((640 - GROUP, HD), F32)
    rows = st_ref[...].T
    for line in range(2):
        for j in range(5):
            row = rows[line : line + 1, j * 128 : (j + 1) * 128]
            small_ref[:, 5 * line + j : 5 * line + j + 1, :] = jnp.broadcast_to(
                row[None], (8, 1, 128)
            )


def query_pass(where, own, kv):
    return call(
        query_body,
        (struct((GROUP, 2 * HD), BF16), struct((8, 10, HD), F32)),
        "query_pass",
        grid=(1,),
        in_specs=[pl.BlockSpec(memory_space=pltpu.SMEM)]
        + [part_of(side) for side in (0, 1, 1, 1, 0, 1, 1, 0, 0)],
        scratch_shapes=[
            pltpu.VMEM((CHUNKS, GROUP, CHUNK), F32),
            pltpu.VMEM((GROUP, HD), F32),
            pltpu.VMEM((GROUP, HD), F32),
            pltpu.VMEM((GROUP, HD), F32),
            pltpu.VMEM((640, HD), F32),
            pltpu.VMEM((SEQ, 2 * HD), BF16),
        ],
    )(where, own, *kv)


def key_body(where_ref, own_ref, stat_ref, *refs):
    out_ref, gk_ref, gv_ref, qd_ref = refs[8:]
    assemble(where_ref, refs[:8], qd_ref, False)
    first = where_ref[0] * GROUP
    begin = first // CHUNK
    clear = (first + GROUP - 1 + CHUNK - 1) // CHUNK
    gk_ref[...] = jnp.zeros_like(gk_ref)
    gv_ref[...] = jnp.zeros_like(gv_ref)

    def visit(c, masked):
        rows = pl.ds(pl.multiple_of(c * CHUNK, CHUNK), CHUNK)
        log_row = stat_ref[c, 0:1, :]
        delta_row = stat_ref[c, 1:2, :]
        q = qd_ref[rows, :HD]
        d = qd_ref[rows, HD:]
        s = nt(own_ref[:, :HD], q) * (SCALE * LOG2E)
        p = jnp.exp2(s - log_row)
        if masked:
            k_at = first + lax.broadcasted_iota(jnp.int32, (GROUP, CHUNK), 0)
            q_at = c * CHUNK + lax.broadcasted_iota(jnp.int32, (GROUP, CHUNK), 1)
            p = jnp.where(q_at >= k_at, p, 0.0)
        gv_ref[...] += nn(p.astype(BF16), d)
        gw = nt(own_ref[:, HD:], d)
        gs = (p * (gw - delta_row)).astype(BF16)
        gk_ref[...] += nn(gs, q)

    @pl.loop(begin, jnp.minimum(clear, CHUNKS))
    def _(c):
        visit(c, True)

    @pl.loop(clear, CHUNKS)
    def _(c):
        visit(c, False)

    out_ref[:, :HD] = (gk_ref[...] * SCALE).astype(BF16)
    out_ref[:, HD:] = gv_ref[...].astype(BF16)


def join_body(oq_ref, ok_ref, slices_ref, out_ref, part_ref):
    for n in range(8):
        part_ref[10 * n : 10 * (n + 1)] = slices_ref[n]
    for j in range(4):
        at = slice(j * ROWS, (j + 1) * ROWS)
        out_ref[j, :ROWS, : 2 * HD] = oq_ref[at]
        out_ref[j, :ROWS, 2 * HD :] = ok_ref[at]
        for c in range(4):
            value = part_ref[20 * c : 20 * (c + 1)].astype(BF16)
            out_ref[j, ROWS : ROWS + 20, c * HD : (c + 1) * HD] = value
        out_ref[j, ROWS + 20 :] = jnp.zeros((4, 4 * HD), BF16)


def join(out_q, out_k, part):
    return call(join_body, struct((4, ROWS + 24, 4 * HD), BF16), "join",
                scratch_shapes=[pltpu.VMEM((80, HD), F32)])(out_q, out_k, part)


def key_pass(where, own, qd, stats):
    return call(
        key_body,
        struct((GROUP, 2 * HD), BF16),
        "key_pass",
        grid=(1,),
        in_specs=[pl.BlockSpec(memory_space=pltpu.SMEM)]
        + [part_of(1)]
        + [pl.BlockSpec(memory_space=pltpu.VMEM)]
        + [part_of(0)] * 8,
        scratch_shapes=[
            pltpu.VMEM((GROUP, HD), F32),
            pltpu.VMEM((GROUP, HD), F32),
            pltpu.VMEM((SEQ, 2 * HD), BF16),
        ],
    )(where, own, stats, *qd)


def exchange(x, axis):
    return lax.all_to_all(x, axis, 0, 0, tiled=True)


def share(x, axis, count):
    return exchange(jnp.broadcast_to(x[None], (count,) + x.shape), axis)


def body(
    features, short_filter, long_filter_taps, queries, key_vectors, value_vectors,
    grad_mixed, grad_attended,
):
    feat = features.transpose(1, 0, 2)
    where = lax.axis_index("cz").astype(jnp.int32).reshape(1)
    packed, tail, rim = pack(
        queries, grad_attended, key_vectors, value_vectors, feat, grad_mixed
    )
    prev = lax.ppermute(tail, CTX, [(i, i + 1) for i in range(31)])
    nxt = lax.ppermute(rim, CTX, [(i + 1, i) for i in range(31)])
    own = exchange(packed, "cy").reshape(GROUP, 4 * HD)
    own, prev, nxt = lax.optimization_barrier((own, prev, nxt))
    rising, falling = [own], [own]

    def shift(x, by):
        return lax.ppermute(x, "cz", [(i, (i + by) % 8) for i in range(8)])

    def step():
        rising.append(shift(rising[-1], 1))
        falling.append(shift(falling[-1], -1))

    def order(*values):
        held = lax.optimization_barrier((rising[-1], falling[-1]) + values)
        rising[-1], falling[-1] = held[:2]
        return held[2:]

    short8 = jnp.pad(short_filter, ((0, 0), (0, 1), (0, 0)))
    step()
    first = hyena(0, feat, prev, nxt, grad_mixed, short8, long_filter_taps, ())
    first = order(*first)
    step()
    second = hyena(1, feat, prev, nxt, grad_mixed, short8, long_filter_taps, first[:2])
    mixed, gfeat, glong, gshort = order(*second)
    z = where[0]
    low, high = 0, 2 * HD
    up_side = jnp.where((z >= 2) & (z <= 6), high, low)
    down_side = jnp.where((z >= 1) & (z <= 5), low, high)
    rising.append(shift(lax.dynamic_slice(rising[2], (0, up_side), (GROUP, 2 * HD)), 1))
    falling.append(shift(lax.dynamic_slice(falling[2], (0, down_side), (GROUP, 2 * HD)), -1))
    grads = jnp.concatenate(
        [first[2], glong, first[3].reshape(24, HD), gshort.reshape(24, HD), jnp.zeros((16, HD), F32)],
        0,
    )
    order()
    far_kv = lax.ppermute(rising[3], "cz", [(i, i + 1) for i in range(3, 7)])
    far_qd = lax.ppermute(falling[3], "cz", [(i, i - 1) for i in range(1, 5)])
    far_kv, far_qd, own = lax.optimization_barrier((far_kv, far_qd, own))
    pieces = [own] + rising[1:] + falling[1:]

    received = exchange(after(grads, own).reshape(32, 10, HD), YFT)
    out_q, small = query_pass(where, own, pieces + [far_kv])
    part = jnp.sum(received, axis=0)
    small = jnp.concatenate([small, jnp.broadcast_to(part[None], (8, 10, HD))], 1)
    small = lax.all_to_all(
        small, "cz", 0, 0, tiled=True, axis_index_groups=[[7, 6, 5, 4, 3, 2, 1, 0]]
    )[::-1]
    part = share(jnp.sum(small[:, 10:], axis=0), FT, 8)
    stats = small[:, :10].reshape(8, 2, 640)[:, :, :GROUP].transpose(1, 0, 2)
    stats = stats.reshape(2, CHUNKS, CHUNK).transpose(1, 0, 2)
    out_k = key_pass(where, own, pieces + [far_qd], stats)
    result = join(out_q, out_k, part)
    attended, grad_queries, grad_keys, grad_values, grad_long, grad_short = unpack(
        exchange(result, "cy")
    )
    return (
        mixed, attended, gfeat.transpose(1, 0, 2), grad_short, grad_long,
        grad_queries, grad_keys, grad_values,
    )


def solution(mesh):
    fine = Mesh(np.asarray(mesh.devices).reshape(8, 4, 4, 2), ("cz", "cy", "fsdp", "tp"))
    rows = P(CTX, FT)
    wide = P(CTX, None, FT)
    return jax.shard_map(
        body,
        mesh=fine,
        in_specs=(wide, P(), P(), rows, rows, rows, rows, rows),
        out_specs=(rows, rows, wide, P(), P(), rows, rows, rows),
        check_vma=False,
    )
```

```python
import jax
import jax.numpy as jnp
import numpy as np
from jax import lax
from jax.experimental import pallas as pl
from jax.experimental.pallas import tpu as pltpu
from jax.sharding import Mesh, PartitionSpec as P

HD = 128
ROWS = 144
GROUP = 576
SEQ = 4608
CHUNK = 1536
CHUNKS = SEQ // CHUNK
LOG2E = 1.4426950408889634
SCALE = HD ** -0.5
VMEM_BYTES = 56 * 1024 * 1024
F32 = jnp.float32
BF16 = jnp.bfloat16
CTX = ("cz", "cy")
FT = ("fsdp", "tp")
YFT = ("cy", "fsdp", "tp")


def after(value, *others):
    return lax.optimization_barrier((value,) + others)[0]


def call(body, out_shape, name, **options):
    return pl.pallas_call(
        body,
        out_shape=out_shape,
        name=name,
        compiler_params=pltpu.CompilerParams(vmem_limit_bytes=VMEM_BYTES),
        **options,
    )


def struct(shape, dtype):
    return jax.ShapeDtypeStruct(shape, dtype)


def nt(a, b):
    return lax.dot_general(a, b, (((1,), (1,)), ((), ())), preferred_element_type=F32)


def nn(a, b):
    return lax.dot_general(a, b, (((1,), (0,)), ((), ())), preferred_element_type=F32)


def pack_body(q_ref, d_ref, k_ref, v_ref, feat_ref, up_ref, out_ref, tail_ref, rim_ref):
    for h in range(4):
        for slot, ref in enumerate((q_ref, d_ref, k_ref, v_ref)):
            out_ref[h, :, slot * HD : (slot + 1) * HD] = ref[:, h * HD : (h + 1) * HD]
    tail_ref[0:136] = feat_ref[0, 8:]
    tail_ref[136:272] = feat_ref[2, 8:]
    tail_ref[272:280] = feat_ref[1, 136:]
    rim_ref[0:136] = feat_ref[1, 0:136]
    rim_ref[136:272] = up_ref[0:136]
    rim_ref[272:280] = feat_ref[0, 0:8]
    rim_ref[280:288] = feat_ref[2, 0:8]


def pack(*parts):
    return call(
        pack_body,
        (
            struct((4, ROWS, 4 * HD), BF16),
            struct((280, 4 * HD), BF16),
            struct((288, 4 * HD), BF16),
        ),
        "pack",
    )(*parts)


def unpack_body(x_ref, attended_ref, gq_ref, gk_ref, gv_ref, glong_ref, gshort_ref, grads_ref):
    for h in range(4):
        at = slice(h * HD, (h + 1) * HD)
        attended_ref[:, at] = x_ref[h, :ROWS, 0:HD]
        gq_ref[:, at] = x_ref[h, :ROWS, HD : 2 * HD].astype(F32)
        gk_ref[:, at] = x_ref[h, :ROWS, 2 * HD : 3 * HD].astype(F32)
        gv_ref[:, at] = x_ref[h, :ROWS, 3 * HD :].astype(F32)
        for c in range(4):
            first = 80 * h + 20 * c
            piece = x_ref[h, ROWS : ROWS + 20, c * HD : (c + 1) * HD]
            grads_ref[first : first + 20] = piece.astype(F32)
    for side in range(2):
        at = slice(side * HD, (side + 1) * HD)
        glong_ref[:, at] = grads_ref[128 * side : 128 * (side + 1)]
        for g in range(3):
            first = 256 + 24 * side + 8 * g
            gshort_ref[g, :, at] = grads_ref[first : first + 7]


def unpack(x):
    whole = struct((ROWS, 4 * HD), F32)
    return call(
        unpack_body,
        (
            struct((ROWS, 4 * HD), BF16), whole, whole, whole,
            struct((128, 256), F32), struct((3, 7, 256), F32),
        ),
        "unpack",
        scratch_shapes=[pltpu.VMEM((320, HD), F32)],
    )(x)


def hyena_body(feat_ref, prev_ref, next_ref, up_ref, short_ref, long_ref, *refs):
    (
        mixed_ref, gfeat_ref, glong_ref, gshort_ref,
        x_ref, x1_ref, p_ref, ps_ref, gm_ref, gs_ref, f_ref, gf_ref, wb_ref, gl_ref,
    ) = refs[-14:]
    turn = pl.program_id(0)
    for slot, g in enumerate((0, 2)):
        x_ref[slot, 0:136] = prev_ref[136 * slot : 136 * (slot + 1)].astype(F32)
        x_ref[slot, 136:280] = feat_ref[g].astype(F32)
        x_ref[slot, 280:288] = next_ref[272 + 8 * slot : 280 + 8 * slot].astype(F32)
    x1_ref[128:136] = prev_ref[272:280].astype(F32)
    x1_ref[136:280] = feat_ref[1].astype(F32)
    x1_ref[280:416] = next_ref[0:136].astype(F32)
    taps = [[short_ref[g, s : s + 1, :] for s in range(7)] for g in range(3)]

    def featured(read, g):
        total = taps[g][0] * read(0)
        for s in range(1, 7):
            total = total + taps[g][s] * read(s)
        return total

    f0 = featured(lambda s: x_ref[0, 8 - s : 288 - s], 0)
    f2 = featured(lambda s: x_ref[1, 8 - s : 288 - s], 2)
    p_ref[8:288] = f0 * f2
    f_ref[0] = f0[128:280]
    f_ref[2] = f2[128:280]
    f1 = featured(lambda s: x1_ref[136 - s : 416 - s], 1)
    f_ref[1] = f1[0:152]
    gm_ref[0:144] = up_ref[...].astype(F32) * f1[0:144]
    gm_ref[144:280] = next_ref[136:272].astype(F32) * f1[144:280]
    for b in range(8):
        ps_ref[b, 16:288] = p_ref[16 - b : 288 - b]
        gs_ref[b] = gm_ref[b : 272 + b]
    wb_ref[...] = jnp.broadcast_to(long_ref[...][:, None, :], (128, 8, 128))

    def forward(a, total):
        base = pl.multiple_of(136 - 8 * a, 8)
        for b in range(8):
            tap = 8 * a + b
            x = ps_ref[b, pl.ds(base, 152), :].reshape(19, 8, 128)
            total = total + wb_ref[tap][None] * x
            gm = gm_ref[0:144].reshape(18, 8, 128)
            gl_ref[tap] = jnp.sum(gm * x[:18], axis=0)
        return total

    memory = lax.fori_loop(0, 16, forward, jnp.zeros((19, 8, 128), F32)).reshape(152, 128)
    mixed_ref[...] = (f_ref[1, 0:144] * memory[0:144]).astype(BF16)
    gf_ref[1, 0:144] = up_ref[...].astype(F32) * memory[0:144]
    gf_ref[1, 144:152] = next_ref[136:144].astype(F32) * memory[144:152]

    def backward(a, total):
        base = pl.multiple_of(8 * a, 8)
        for b in range(8):
            y = gs_ref[b, pl.ds(base, 152), :].reshape(19, 8, 128)
            total = total + wb_ref[8 * a + b][None] * y
        return total

    gp = lax.fori_loop(0, 16, backward, jnp.zeros((19, 8, 128), F32)).reshape(152, 128)
    gf_ref[0] = gp * f_ref[2]
    gf_ref[2] = gp * f_ref[0]
    glong = jnp.sum(gl_ref[...], axis=1)

    @pl.when(turn == 0)
    def _():
        glong_ref[...] = glong
        gshort_ref[...] = jnp.zeros_like(gshort_ref)

    @pl.when(turn != 0)
    def _():
        glong_ref[...] += glong

    for g in range(3):
        total = taps[g][0] * gf_ref[g, 0:144]
        for s in range(1, 7):
            total = total + taps[g][s] * gf_ref[g, s : 144 + s]
        gfeat_ref[g] = total
        own = gf_ref[g, 0:144]
        for s in range(7):
            if g == 1:
                x = x1_ref[136 - s : 280 - s]
            else:
                x = x_ref[g // 2, 136 - s : 280 - s]
            column = jnp.sum((own * x).reshape(18, 8, 128), axis=0)
            gshort_ref[g, s : s + 1, :] += jnp.sum(column, axis=0, keepdims=True)


def hyena(side, feat, prev, nxt, up, short8, long_taps, earlier):
    def cols(*lead):
        return pl.BlockSpec(lead + (128,), lambda k: (0,) * len(lead) + (2 * k + side,))

    def filters(*lead):
        return pl.BlockSpec(lead + (128,), lambda k: (0,) * len(lead) + (side,))

    def sums(*lead):
        return pl.BlockSpec(lead + (128,), lambda k: (0,) * (len(lead) + 1))

    kept = pl.BlockSpec(memory_space=pl.ANY)
    return call(
        hyena_body,
        (
            struct((ROWS, 512), BF16),
            struct((3, ROWS, 512), F32),
            struct((128, 128), F32),
            struct((3, 8, 128), F32),
        ),
        "hyena",
        grid=(2,),
        in_specs=[
            cols(3, ROWS), cols(280), cols(288), cols(ROWS), filters(3, 8), filters(128),
        ] + [kept] * len(earlier),
        out_specs=(cols(ROWS), cols(3, ROWS), sums(128), sums(3, 8)),
        input_output_aliases={6 + i: i for i in range(len(earlier))},
        scratch_shapes=[
            pltpu.VMEM((2, 288, 128), F32),
            pltpu.VMEM((416, 128), F32),
            pltpu.VMEM((288, 128), F32),
            pltpu.VMEM((8, 288, 128), F32),
            pltpu.VMEM((280, 128), F32),
            pltpu.VMEM((8, 272, 128), F32),
            pltpu.VMEM((3, 152, 128), F32),
            pltpu.VMEM((3, 152, 128), F32),
            pltpu.VMEM((128, 8, 128), F32),
            pltpu.VMEM((128, 8, 128), F32),
        ],
    )(feat, prev, nxt, up, short8, long_taps, *earlier)


PLACES = (0, -1, -2, -3, 1, 2, 3, 4)


def part_of(side):
    return pl.BlockSpec((GROUP, 2 * HD), lambda i: (0, side))


def assemble(where_ref, pieces, out_ref, below):
    z = where_ref[0]
    for place, piece in zip(PLACES, pieces):
        block = (z + place + 8) % 8
        needed = (block <= z) if below else (block >= z)

        at = pl.ds(pl.multiple_of(block * GROUP, 64), GROUP)

        @pl.when(needed)
        def _():
            out_ref[at, :] = piece[...]

        @pl.when(jnp.logical_not(needed))
        def _():
            out_ref[at, :] = jnp.zeros((GROUP, 2 * HD), BF16)


def lane_max(x):
    best = x[:, 0:128]
    for j in range(1, CHUNK // 128):
        best = jnp.maximum(best, x[:, j * 128 : (j + 1) * 128])
    return best


def lane_sum(x):
    total = x[:, 0:128]
    for j in range(1, CHUNK // 128):
        total = total + x[:, j * 128 : (j + 1) * 128]
    return total


def query_body(where_ref, own_ref, *refs):
    out_ref, small_ref, s_ref, mx_ref, l_ref, o_ref, st_ref, kv_ref = refs[8:]
    assemble(where_ref, refs[:8], kv_ref, True)
    first = where_ref[0] * GROUP
    clear = first // CHUNK
    total = (first + GROUP + CHUNK - 1) // CHUNK
    mx_ref[...] = jnp.full_like(mx_ref, -jnp.inf)
    l_ref[...] = jnp.zeros_like(l_ref)
    o_ref[...] = jnp.zeros_like(o_ref)

    def rows_of(c):
        return pl.ds(pl.multiple_of(c * CHUNK, CHUNK), CHUNK)

    def scores(c, masked):
        s = nt(own_ref[:, :HD], kv_ref[rows_of(c), :HD]) * (SCALE * LOG2E)
        if masked:
            q = first + lax.broadcasted_iota(jnp.int32, (GROUP, CHUNK), 0)
            k = c * CHUNK + lax.broadcasted_iota(jnp.int32, (GROUP, CHUNK), 1)
            s = jnp.where(q >= k, s, -jnp.inf)
        s_ref[c] = s
        mx_ref[...] = jnp.maximum(mx_ref[...], lane_max(s))

    @pl.loop(0, clear)
    def _(c):
        scores(c, False)

    @pl.loop(clear, total)
    def _(c):
        scores(c, True)

    peak = jnp.max(mx_ref[...], axis=1, keepdims=True)

    @pl.loop(0, total)
    def _(c):
        p = jnp.exp2(s_ref[c] - peak)
        s_ref[c] = p
        l_ref[...] += lane_sum(p)
        o_ref[...] += nn(p.astype(BF16), kv_ref[rows_of(c), HD:])

    norm = jnp.sum(l_ref[...], axis=1, keepdims=True)
    inverse = 1.0 / norm
    attended = (o_ref[...] * inverse).astype(BF16)
    out_ref[:, :HD] = attended
    delta = jnp.sum(
        own_ref[:, HD:].astype(F32) * attended.astype(F32), axis=1, keepdims=True
    )
    o_ref[...] = jnp.zeros_like(o_ref)

    @pl.loop(0, total)
    def _(c):
        rows = rows_of(c)
        gw = nt(own_ref[:, HD:], kv_ref[rows, HD:])
        gs = (s_ref[c] * (gw - delta)).astype(BF16)
        o_ref[...] += nn(gs, kv_ref[rows, :HD])

    out_ref[:, HD:] = (o_ref[...] * (inverse * SCALE)).astype(BF16)
    lane = lax.broadcasted_iota(jnp.int32, (GROUP, HD), 1)
    st_ref[0:GROUP] = jnp.where(lane == 0, peak + jnp.log2(norm), delta)
    st_ref[GROUP:640] = jnp.zeros((640 - GROUP, HD), F32)
    rows = st_ref[...].T
    for line in range(2):
        for j in range(5):
            row = rows[line : line + 1, j * 128 : (j + 1) * 128]
            small_ref[:, 5 * line + j : 5 * line + j + 1, :] = jnp.broadcast_to(
                row[None], (8, 1, 128)
            )


def query_pass(where, own, kv):
    return call(
        query_body,
        (struct((GROUP, 2 * HD), BF16), struct((8, 10, HD), F32)),
        "query_pass",
        grid=(1,),
        in_specs=[pl.BlockSpec(memory_space=pltpu.SMEM)]
        + [part_of(side) for side in (0, 1, 1, 1, 0, 1, 1, 0, 0)],
        scratch_shapes=[
            pltpu.VMEM((CHUNKS, GROUP, CHUNK), F32),
            pltpu.VMEM((GROUP, HD), F32),
            pltpu.VMEM((GROUP, HD), F32),
            pltpu.VMEM((GROUP, HD), F32),
            pltpu.VMEM((640, HD), F32),
            pltpu.VMEM((SEQ, 2 * HD), BF16),
        ],
    )(where, own, *kv)


def key_body(where_ref, own_ref, stat_ref, oq_ref, *refs):
    out_ref, gk_ref, gv_ref, qd_ref = refs[8:]
    assemble(where_ref, refs[:8], qd_ref, False)
    first = where_ref[0] * GROUP
    begin = first // CHUNK
    clear = (first + GROUP - 1 + CHUNK - 1) // CHUNK
    gk_ref[...] = jnp.zeros_like(gk_ref)
    gv_ref[...] = jnp.zeros_like(gv_ref)

    def visit(c, masked):
        rows = pl.ds(pl.multiple_of(c * CHUNK, CHUNK), CHUNK)
        log_row = stat_ref[c, 0:1, :]
        delta_row = stat_ref[c, 1:2, :]
        q = qd_ref[rows, :HD]
        d = qd_ref[rows, HD:]
        s = nt(own_ref[:, :HD], q) * (SCALE * LOG2E)
        p = jnp.exp2(s - log_row)
        if masked:
            k_at = first + lax.broadcasted_iota(jnp.int32, (GROUP, CHUNK), 0)
            q_at = c * CHUNK + lax.broadcasted_iota(jnp.int32, (GROUP, CHUNK), 1)
            p = jnp.where(q_at >= k_at, p, 0.0)
        gv_ref[...] += nn(p.astype(BF16), d)
        gw = nt(own_ref[:, HD:], d)
        gs = (p * (gw - delta_row)).astype(BF16)
        gk_ref[...] += nn(gs, q)

    @pl.loop(begin, jnp.minimum(clear, CHUNKS))
    def _(c):
        visit(c, True)

    @pl.loop(clear, CHUNKS)
    def _(c):
        visit(c, False)

    for j in range(4):
        at = slice(j * ROWS, (j + 1) * ROWS)
        out_ref[j, :ROWS, : 2 * HD] = oq_ref[at]
        out_ref[j, :ROWS, 2 * HD : 3 * HD] = (gk_ref[at] * SCALE).astype(BF16)
        out_ref[j, :ROWS, 3 * HD :] = gv_ref[at].astype(BF16)
        out_ref[j, ROWS:] = jnp.zeros((24, 4 * HD), BF16)


def join_body(slices_ref, kept_ref, out_ref, part_ref):
    for n in range(8):
        part_ref[10 * n : 10 * (n + 1)] = slices_ref[n]
    for j in range(4):
        for c in range(4):
            value = part_ref[20 * c : 20 * (c + 1)].astype(BF16)
            out_ref[j, 0:20, c * HD : (c + 1) * HD] = value
        out_ref[j, 20:] = jnp.zeros((4, 4 * HD), BF16)


def join(result, part):
    return call(
        join_body,
        struct((4, ROWS + 24, 4 * HD), BF16),
        "join",
        grid=(1,),
        in_specs=[
            pl.BlockSpec((8, 10, HD), lambda i: (0, 0, 0)),
            pl.BlockSpec(memory_space=pl.ANY),
        ],
        out_specs=pl.BlockSpec((4, 24, 4 * HD), lambda i: (0, 6, 0)),
        input_output_aliases={1: 0},
        scratch_shapes=[pltpu.VMEM((80, HD), F32)],
    )(part, result)


def key_pass(where, own, qd, stats, out_q):
    return call(
        key_body,
        struct((4, ROWS + 24, 4 * HD), BF16),
        "key_pass",
        grid=(1,),
        in_specs=[pl.BlockSpec(memory_space=pltpu.SMEM)]
        + [part_of(1)]
        + [pl.BlockSpec(memory_space=pltpu.VMEM)] * 2
        + [part_of(0)] * 8,
        scratch_shapes=[
            pltpu.VMEM((GROUP, HD), F32),
            pltpu.VMEM((GROUP, HD), F32),
            pltpu.VMEM((SEQ, 2 * HD), BF16),
        ],
    )(where, own, stats, out_q, *qd)


def exchange(x, axis):
    return lax.all_to_all(x, axis, 0, 0, tiled=True)


def share(x, axis, count):
    return exchange(jnp.broadcast_to(x[None], (count,) + x.shape), axis)


def body(
    features, short_filter, long_filter_taps, queries, key_vectors, value_vectors,
    grad_mixed, grad_attended,
):
    feat = features.transpose(1, 0, 2)
    where = lax.axis_index("cz").astype(jnp.int32).reshape(1)
    packed, tail, rim = pack(
        queries, grad_attended, key_vectors, value_vectors, feat, grad_mixed
    )
    prev = lax.ppermute(tail, CTX, [(i, i + 1) for i in range(31)])
    nxt = lax.ppermute(rim, CTX, [(i + 1, i) for i in range(31)])
    own = exchange(packed, "cy").reshape(GROUP, 4 * HD)
    own, prev, nxt = lax.optimization_barrier((own, prev, nxt))
    rising, falling = [own], [own]

    def shift(x, by):
        return lax.ppermute(x, "cz", [(i, (i + by) % 8) for i in range(8)])

    def step():
        rising.append(shift(rising[-1], 1))
        falling.append(shift(falling[-1], -1))

    def order(*values):
        held = lax.optimization_barrier((rising[-1], falling[-1]) + values)
        rising[-1], falling[-1] = held[:2]
        return held[2:]

    short8 = jnp.pad(short_filter, ((0, 0), (0, 1), (0, 0)))
    step()
    first = hyena(0, feat, prev, nxt, grad_mixed, short8, long_filter_taps, ())
    first = order(*first)
    step()
    second = hyena(1, feat, prev, nxt, grad_mixed, short8, long_filter_taps, first[:2])
    mixed, gfeat, glong, gshort = order(*second)
    z = where[0]
    low, high = 0, 2 * HD
    up_side = jnp.where((z >= 2) & (z <= 6), high, low)
    down_side = jnp.where((z >= 1) & (z <= 5), low, high)
    rising.append(shift(lax.dynamic_slice(rising[2], (0, up_side), (GROUP, 2 * HD)), 1))
    falling.append(shift(lax.dynamic_slice(falling[2], (0, down_side), (GROUP, 2 * HD)), -1))
    grads = jnp.concatenate(
        [first[2], glong, first[3].reshape(24, HD), gshort.reshape(24, HD), jnp.zeros((16, HD), F32)],
        0,
    )
    order()
    far_kv = lax.ppermute(rising[3], "cz", [(i, i + 1) for i in range(3, 7)])
    far_qd = lax.ppermute(falling[3], "cz", [(i, i - 1) for i in range(1, 5)])
    far_kv, far_qd, own = lax.optimization_barrier((far_kv, far_qd, own))
    pieces = [own] + rising[1:] + falling[1:]

    received = exchange(after(grads, own).reshape(32, 10, HD), YFT)
    out_q, small = query_pass(where, own, pieces + [far_kv])
    part = jnp.sum(received, axis=0)
    small = jnp.concatenate([small, jnp.broadcast_to(part[None], (8, 10, HD))], 1)
    small = lax.all_to_all(
        small, "cz", 0, 0, tiled=True, axis_index_groups=[[7, 6, 5, 4, 3, 2, 1, 0]]
    )[::-1]
    part = share(jnp.sum(small[:, 10:], axis=0), FT, 8)
    stats = small[:, :10].reshape(8, 2, 640)[:, :, :GROUP].transpose(1, 0, 2)
    stats = stats.reshape(2, CHUNKS, CHUNK).transpose(1, 0, 2)
    result = key_pass(where, own, pieces + [far_qd], stats, out_q)
    result = join(result, part)
    attended, grad_queries, grad_keys, grad_values, grad_long, grad_short = unpack(
        exchange(result, "cy")
    )
    return (
        mixed, attended, gfeat.transpose(1, 0, 2), grad_short, grad_long,
        grad_queries, grad_keys, grad_values,
    )


def solution(mesh):
    fine = Mesh(np.asarray(mesh.devices).reshape(8, 4, 4, 2), ("cz", "cy", "fsdp", "tp"))
    rows = P(CTX, FT)
    wide = P(CTX, None, FT)
    return jax.shard_map(
        body,
        mesh=fine,
        in_specs=(wide, P(), P(), rows, rows, rows, rows, rows),
        out_specs=(rows, rows, wide, P(), P(), rows, rows, rows),
        check_vma=False,
    )
```

```python
import jax
import jax.numpy as jnp
import numpy as np
from jax import lax
from jax.experimental import pallas as pl
from jax.experimental.pallas import tpu as pltpu
from jax.sharding import Mesh, PartitionSpec as P

HD = 128
ROWS = 144
GROUP = 576
SEQ = 4608
CHUNK = 2304
CHUNKS = SEQ // CHUNK
LOG2E = 1.4426950408889634
SCALE = HD ** -0.5
VMEM_BYTES = 56 * 1024 * 1024
F32 = jnp.float32
BF16 = jnp.bfloat16
CTX = ("cz", "cy")
FT = ("fsdp", "tp")
YFT = ("cy", "fsdp", "tp")


def after(value, *others):
    return lax.optimization_barrier((value,) + others)[0]


def call(body, out_shape, name, **options):
    return pl.pallas_call(
        body,
        out_shape=out_shape,
        name=name,
        compiler_params=pltpu.CompilerParams(vmem_limit_bytes=VMEM_BYTES),
        **options,
    )


def struct(shape, dtype):
    return jax.ShapeDtypeStruct(shape, dtype)


def nt(a, b):
    return lax.dot_general(a, b, (((1,), (1,)), ((), ())), preferred_element_type=F32)


def nn(a, b):
    return lax.dot_general(a, b, (((1,), (0,)), ((), ())), preferred_element_type=F32)


def pack_body(q_ref, d_ref, k_ref, v_ref, feat_ref, up_ref, out_ref, tail_ref, rim_ref):
    for h in range(4):
        for slot, ref in enumerate((q_ref, d_ref, k_ref, v_ref)):
            out_ref[h, :, slot * HD : (slot + 1) * HD] = ref[:, h * HD : (h + 1) * HD]
    tail_ref[0:136] = feat_ref[0, 8:]
    tail_ref[136:272] = feat_ref[2, 8:]
    tail_ref[272:280] = feat_ref[1, 136:]
    rim_ref[0:136] = feat_ref[1, 0:136]
    rim_ref[136:272] = up_ref[0:136]
    rim_ref[272:280] = feat_ref[0, 0:8]
    rim_ref[280:288] = feat_ref[2, 0:8]


def pack(*parts):
    return call(
        pack_body,
        (
            struct((4, ROWS, 4 * HD), BF16),
            struct((280, 4 * HD), BF16),
            struct((288, 4 * HD), BF16),
        ),
        "pack",
    )(*parts)


def unpack_body(x_ref, attended_ref, gq_ref, gk_ref, gv_ref, glong_ref, gshort_ref, grads_ref):
    for h in range(4):
        at = slice(h * HD, (h + 1) * HD)
        attended_ref[:, at] = x_ref[h, :ROWS, 0:HD]
        gq_ref[:, at] = x_ref[h, :ROWS, HD : 2 * HD].astype(F32)
        gk_ref[:, at] = x_ref[h, :ROWS, 2 * HD : 3 * HD].astype(F32)
        gv_ref[:, at] = x_ref[h, :ROWS, 3 * HD :].astype(F32)
        for c in range(4):
            first = 80 * h + 20 * c
            piece = x_ref[h, ROWS : ROWS + 20, c * HD : (c + 1) * HD]
            grads_ref[first : first + 20] = piece.astype(F32)
    for side in range(2):
        at = slice(side * HD, (side + 1) * HD)
        glong_ref[:, at] = grads_ref[128 * side : 128 * (side + 1)]
        for g in range(3):
            first = 256 + 24 * side + 8 * g
            gshort_ref[g, :, at] = grads_ref[first : first + 7]


def unpack(x):
    whole = struct((ROWS, 4 * HD), F32)
    return call(
        unpack_body,
        (
            struct((ROWS, 4 * HD), BF16), whole, whole, whole,
            struct((128, 256), F32), struct((3, 7, 256), F32),
        ),
        "unpack",
        scratch_shapes=[pltpu.VMEM((320, HD), F32)],
    )(x)


def hyena_body(feat_ref, prev_ref, next_ref, up_ref, short_ref, long_ref, *refs):
    (
        mixed_ref, gfeat_ref, glong_ref, gshort_ref,
        x_ref, x1_ref, p_ref, ps_ref, gm_ref, gs_ref, f_ref, gf_ref, wb_ref, gl_ref,
    ) = refs[-14:]
    turn = pl.program_id(0)
    for slot, g in enumerate((0, 2)):
        x_ref[slot, 0:136] = prev_ref[136 * slot : 136 * (slot + 1)].astype(F32)
        x_ref[slot, 136:280] = feat_ref[g].astype(F32)
        x_ref[slot, 280:288] = next_ref[272 + 8 * slot : 280 + 8 * slot].astype(F32)
    x1_ref[128:136] = prev_ref[272:280].astype(F32)
    x1_ref[136:280] = feat_ref[1].astype(F32)
    x1_ref[280:416] = next_ref[0:136].astype(F32)
    taps = [[short_ref[g, s : s + 1, :] for s in range(7)] for g in range(3)]

    def featured(read, g):
        total = taps[g][0] * read(0)
        for s in range(1, 7):
            total = total + taps[g][s] * read(s)
        return total

    f0 = featured(lambda s: x_ref[0, 8 - s : 288 - s], 0)
    f2 = featured(lambda s: x_ref[1, 8 - s : 288 - s], 2)
    p_ref[8:288] = f0 * f2
    f_ref[0] = f0[128:280]
    f_ref[2] = f2[128:280]
    f1 = featured(lambda s: x1_ref[136 - s : 416 - s], 1)
    f_ref[1] = f1[0:152]
    gm_ref[0:144] = up_ref[...].astype(F32) * f1[0:144]
    gm_ref[144:280] = next_ref[136:272].astype(F32) * f1[144:280]
    for b in range(8):
        ps_ref[b, 16:288] = p_ref[16 - b : 288 - b]
        gs_ref[b] = gm_ref[b : 272 + b]
    wb_ref[...] = jnp.broadcast_to(long_ref[...][:, None, :], (128, 8, 128))

    def forward(a, total):
        base = pl.multiple_of(136 - 8 * a, 8)
        for b in range(8):
            tap = 8 * a + b
            x = ps_ref[b, pl.ds(base, 152), :].reshape(19, 8, 128)
            total = total + wb_ref[tap][None] * x
            gm = gm_ref[0:144].reshape(18, 8, 128)
            gl_ref[tap] = jnp.sum(gm * x[:18], axis=0)
        return total

    memory = lax.fori_loop(0, 16, forward, jnp.zeros((19, 8, 128), F32)).reshape(152, 128)
    mixed_ref[...] = (f_ref[1, 0:144] * memory[0:144]).astype(BF16)
    gf_ref[1, 0:144] = up_ref[...].astype(F32) * memory[0:144]
    gf_ref[1, 144:152] = next_ref[136:144].astype(F32) * memory[144:152]

    def backward(a, total):
        base = pl.multiple_of(8 * a, 8)
        for b in range(8):
            y = gs_ref[b, pl.ds(base, 152), :].reshape(19, 8, 128)
            total = total + wb_ref[8 * a + b][None] * y
        return total

    gp = lax.fori_loop(0, 16, backward, jnp.zeros((19, 8, 128), F32)).reshape(152, 128)
    gf_ref[0] = gp * f_ref[2]
    gf_ref[2] = gp * f_ref[0]
    glong = jnp.sum(gl_ref[...], axis=1)

    @pl.when(turn == 0)
    def _():
        glong_ref[...] = glong
        gshort_ref[...] = jnp.zeros_like(gshort_ref)

    @pl.when(turn != 0)
    def _():
        glong_ref[...] += glong

    for g in range(3):
        total = taps[g][0] * gf_ref[g, 0:144]
        for s in range(1, 7):
            total = total + taps[g][s] * gf_ref[g, s : 144 + s]
        gfeat_ref[g] = total
        own = gf_ref[g, 0:144]
        for s in range(7):
            if g == 1:
                x = x1_ref[136 - s : 280 - s]
            else:
                x = x_ref[g // 2, 136 - s : 280 - s]
            column = jnp.sum((own * x).reshape(18, 8, 128), axis=0)
            gshort_ref[g, s : s + 1, :] += jnp.sum(column, axis=0, keepdims=True)


def hyena(side, feat, prev, nxt, up, short8, long_taps, earlier):
    def cols(*lead):
        return pl.BlockSpec(lead + (128,), lambda k: (0,) * len(lead) + (2 * k + side,))

    def filters(*lead):
        return pl.BlockSpec(lead + (128,), lambda k: (0,) * len(lead) + (side,))

    def sums(*lead):
        return pl.BlockSpec(lead + (128,), lambda k: (0,) * (len(lead) + 1))

    kept = pl.BlockSpec(memory_space=pl.ANY)
    return call(
        hyena_body,
        (
            struct((ROWS, 512), BF16),
            struct((3, ROWS, 512), F32),
            struct((128, 128), F32),
            struct((3, 8, 128), F32),
        ),
        "hyena",
        grid=(2,),
        in_specs=[
            cols(3, ROWS), cols(280), cols(288), cols(ROWS), filters(3, 8), filters(128),
        ] + [kept] * len(earlier),
        out_specs=(cols(ROWS), cols(3, ROWS), sums(128), sums(3, 8)),
        input_output_aliases={6 + i: i for i in range(len(earlier))},
        scratch_shapes=[
            pltpu.VMEM((2, 288, 128), F32),
            pltpu.VMEM((416, 128), F32),
            pltpu.VMEM((288, 128), F32),
            pltpu.VMEM((8, 288, 128), F32),
            pltpu.VMEM((280, 128), F32),
            pltpu.VMEM((8, 272, 128), F32),
            pltpu.VMEM((3, 152, 128), F32),
            pltpu.VMEM((3, 152, 128), F32),
            pltpu.VMEM((128, 8, 128), F32),
            pltpu.VMEM((128, 8, 128), F32),
        ],
    )(feat, prev, nxt, up, short8, long_taps, *earlier)


PLACES = (0, -1, -2, -3, 1, 2, 3, 4)


def part_of(side):
    return pl.BlockSpec((GROUP, 2 * HD), lambda i: (0, side))


def assemble(where_ref, pieces, out_ref, below):
    z = where_ref[0]
    for place, piece in zip(PLACES, pieces):
        block = (z + place + 8) % 8
        needed = (block <= z) if below else (block >= z)

        at = pl.ds(pl.multiple_of(block * GROUP, 64), GROUP)

        @pl.when(needed)
        def _():
            out_ref[at, :] = piece[...]

        @pl.when(jnp.logical_not(needed))
        def _():
            out_ref[at, :] = jnp.zeros((GROUP, 2 * HD), BF16)


def lane_max(x):
    best = x[:, 0:128]
    for j in range(1, CHUNK // 128):
        best = jnp.maximum(best, x[:, j * 128 : (j + 1) * 128])
    return best


def lane_sum(x):
    total = x[:, 0:128]
    for j in range(1, CHUNK // 128):
        total = total + x[:, j * 128 : (j + 1) * 128]
    return total


def query_body(where_ref, own_ref, *refs):
    out_ref, small_ref, s_ref, mx_ref, l_ref, o_ref, st_ref, kv_ref = refs[8:]
    assemble(where_ref, refs[:8], kv_ref, True)
    first = where_ref[0] * GROUP
    clear = first // CHUNK
    total = (first + GROUP + CHUNK - 1) // CHUNK
    mx_ref[...] = jnp.full_like(mx_ref, -jnp.inf)
    l_ref[...] = jnp.zeros_like(l_ref)
    o_ref[...] = jnp.zeros_like(o_ref)

    def rows_of(c):
        return pl.ds(pl.multiple_of(c * CHUNK, CHUNK), CHUNK)

    def scores(c, masked):
        s = nt(own_ref[:, :HD], kv_ref[rows_of(c), :HD]) * (SCALE * LOG2E)
        if masked:
            q = first + lax.broadcasted_iota(jnp.int32, (GROUP, CHUNK), 0)
            k = c * CHUNK + lax.broadcasted_iota(jnp.int32, (GROUP, CHUNK), 1)
            s = jnp.where(q >= k, s, -jnp.inf)
        s_ref[c] = s
        mx_ref[...] = jnp.maximum(mx_ref[...], lane_max(s))

    @pl.loop(0, clear)
    def _(c):
        scores(c, False)

    @pl.loop(clear, total)
    def _(c):
        scores(c, True)

    peak = jnp.max(mx_ref[...], axis=1, keepdims=True)

    @pl.loop(0, total)
    def _(c):
        p = jnp.exp2(s_ref[c] - peak)
        s_ref[c] = p
        l_ref[...] += lane_sum(p)
        o_ref[...] += nn(p.astype(BF16), kv_ref[rows_of(c), HD:])

    norm = jnp.sum(l_ref[...], axis=1, keepdims=True)
    inverse = 1.0 / norm
    attended = (o_ref[...] * inverse).astype(BF16)
    out_ref[:, :HD] = attended
    delta = jnp.sum(
        own_ref[:, HD:].astype(F32) * attended.astype(F32), axis=1, keepdims=True
    )
    o_ref[...] = jnp.zeros_like(o_ref)

    @pl.loop(0, total)
    def _(c):
        rows = rows_of(c)
        gw = nt(own_ref[:, HD:], kv_ref[rows, HD:])
        gs = (s_ref[c] * (gw - delta)).astype(BF16)
        o_ref[...] += nn(gs, kv_ref[rows, :HD])

    out_ref[:, HD:] = (o_ref[...] * (inverse * SCALE)).astype(BF16)
    lane = lax.broadcasted_iota(jnp.int32, (GROUP, HD), 1)
    st_ref[0:GROUP] = jnp.where(lane == 0, peak + jnp.log2(norm), delta)
    st_ref[GROUP:640] = jnp.zeros((640 - GROUP, HD), F32)
    rows = st_ref[...].T
    for line in range(2):
        for j in range(5):
            row = rows[line : line + 1, j * 128 : (j + 1) * 128]
            small_ref[:, 5 * line + j : 5 * line + j + 1, :] = jnp.broadcast_to(
                row[None], (8, 1, 128)
            )


def query_pass(where, own, kv):
    return call(
        query_body,
        (struct((GROUP, 2 * HD), BF16), struct((8, 10, HD), F32)),
        "query_pass",
        grid=(1,),
        in_specs=[pl.BlockSpec(memory_space=pltpu.SMEM)]
        + [part_of(side) for side in (0, 1, 1, 1, 0, 1, 1, 0, 0)],
        scratch_shapes=[
            pltpu.VMEM((CHUNKS, GROUP, CHUNK), F32),
            pltpu.VMEM((GROUP, HD), F32),
            pltpu.VMEM((GROUP, HD), F32),
            pltpu.VMEM((GROUP, HD), F32),
            pltpu.VMEM((640, HD), F32),
            pltpu.VMEM((SEQ, 2 * HD), BF16),
        ],
    )(where, own, *kv)


def key_body(where_ref, own_ref, stat_ref, oq_ref, *refs):
    out_ref, gk_ref, gv_ref, qd_ref = refs[8:]
    assemble(where_ref, refs[:8], qd_ref, False)
    first = where_ref[0] * GROUP
    begin = first // CHUNK
    clear = (first + GROUP - 1 + CHUNK - 1) // CHUNK
    gk_ref[...] = jnp.zeros_like(gk_ref)
    gv_ref[...] = jnp.zeros_like(gv_ref)

    def visit(c, masked):
        rows = pl.ds(pl.multiple_of(c * CHUNK, CHUNK), CHUNK)
        log_row = stat_ref[c, 0:1, :]
        delta_row = stat_ref[c, 1:2, :]
        q = qd_ref[rows, :HD]
        d = qd_ref[rows, HD:]
        s = nt(own_ref[:, :HD], q) * (SCALE * LOG2E)
        p = jnp.exp2(s - log_row)
        if masked:
            k_at = first + lax.broadcasted_iota(jnp.int32, (GROUP, CHUNK), 0)
            q_at = c * CHUNK + lax.broadcasted_iota(jnp.int32, (GROUP, CHUNK), 1)
            p = jnp.where(q_at >= k_at, p, 0.0)
        gv_ref[...] += nn(p.astype(BF16), d)
        gw = nt(own_ref[:, HD:], d)
        gs = (p * (gw - delta_row)).astype(BF16)
        gk_ref[...] += nn(gs, q)

    @pl.loop(begin, jnp.minimum(clear, CHUNKS))
    def _(c):
        visit(c, True)

    @pl.loop(clear, CHUNKS)
    def _(c):
        visit(c, False)

    for j in range(4):
        at = slice(j * ROWS, (j + 1) * ROWS)
        out_ref[j, :ROWS, : 2 * HD] = oq_ref[at]
        out_ref[j, :ROWS, 2 * HD : 3 * HD] = (gk_ref[at] * SCALE).astype(BF16)
        out_ref[j, :ROWS, 3 * HD :] = gv_ref[at].astype(BF16)
        out_ref[j, ROWS:] = jnp.zeros((24, 4 * HD), BF16)


def join_body(slices_ref, kept_ref, out_ref, part_ref):
    for n in range(8):
        part_ref[10 * n : 10 * (n + 1)] = slices_ref[n]
    for j in range(4):
        for c in range(4):
            value = part_ref[20 * c : 20 * (c + 1)].astype(BF16)
            out_ref[j, 0:20, c * HD : (c + 1) * HD] = value
        out_ref[j, 20:] = jnp.zeros((4, 4 * HD), BF16)


def join(result, part):
    return call(
        join_body,
        struct((4, ROWS + 24, 4 * HD), BF16),
        "join",
        grid=(1,),
        in_specs=[
            pl.BlockSpec((8, 10, HD), lambda i: (0, 0, 0)),
            pl.BlockSpec(memory_space=pl.ANY),
        ],
        out_specs=pl.BlockSpec((4, 24, 4 * HD), lambda i: (0, 6, 0)),
        input_output_aliases={1: 0},
        scratch_shapes=[pltpu.VMEM((80, HD), F32)],
    )(part, result)


def key_pass(where, own, qd, stats, out_q):
    return call(
        key_body,
        struct((4, ROWS + 24, 4 * HD), BF16),
        "key_pass",
        grid=(1,),
        in_specs=[pl.BlockSpec(memory_space=pltpu.SMEM)]
        + [part_of(1)]
        + [pl.BlockSpec(memory_space=pltpu.VMEM)] * 2
        + [part_of(0)] * 8,
        scratch_shapes=[
            pltpu.VMEM((GROUP, HD), F32),
            pltpu.VMEM((GROUP, HD), F32),
            pltpu.VMEM((SEQ, 2 * HD), BF16),
        ],
    )(where, own, stats, out_q, *qd)


def exchange(x, axis):
    return lax.all_to_all(x, axis, 0, 0, tiled=True)


def share(x, axis, count):
    return exchange(jnp.broadcast_to(x[None], (count,) + x.shape), axis)


def body(
    features, short_filter, long_filter_taps, queries, key_vectors, value_vectors,
    grad_mixed, grad_attended,
):
    feat = features.transpose(1, 0, 2)
    where = lax.axis_index("cz").astype(jnp.int32).reshape(1)
    packed, tail, rim = pack(
        queries, grad_attended, key_vectors, value_vectors, feat, grad_mixed
    )
    prev = lax.ppermute(tail, CTX, [(i, i + 1) for i in range(31)])
    nxt = lax.ppermute(rim, CTX, [(i + 1, i) for i in range(31)])
    own = exchange(packed, "cy").reshape(GROUP, 4 * HD)
    own, prev, nxt = lax.optimization_barrier((own, prev, nxt))
    rising, falling = [own], [own]

    def shift(x, by):
        return lax.ppermute(x, "cz", [(i, (i + by) % 8) for i in range(8)])

    def step():
        rising.append(shift(rising[-1], 1))
        falling.append(shift(falling[-1], -1))

    def order(*values):
        held = lax.optimization_barrier((rising[-1], falling[-1]) + values)
        rising[-1], falling[-1] = held[:2]
        return held[2:]

    short8 = jnp.pad(short_filter, ((0, 0), (0, 1), (0, 0)))
    step()
    first = hyena(0, feat, prev, nxt, grad_mixed, short8, long_filter_taps, ())
    first = order(*first)
    step()
    second = hyena(1, feat, prev, nxt, grad_mixed, short8, long_filter_taps, first[:2])
    mixed, gfeat, glong, gshort = order(*second)
    z = where[0]
    low, high = 0, 2 * HD
    up_side = jnp.where((z >= 2) & (z <= 6), high, low)
    down_side = jnp.where((z >= 1) & (z <= 5), low, high)
    rising.append(shift(lax.dynamic_slice(rising[2], (0, up_side), (GROUP, 2 * HD)), 1))
    falling.append(shift(lax.dynamic_slice(falling[2], (0, down_side), (GROUP, 2 * HD)), -1))
    grads = jnp.concatenate(
        [first[2], glong, first[3].reshape(24, HD), gshort.reshape(24, HD), jnp.zeros((16, HD), F32)],
        0,
    )
    order()
    far_kv = lax.ppermute(rising[3], "cz", [(i, i + 1) for i in range(3, 7)])
    far_qd = lax.ppermute(falling[3], "cz", [(i, i - 1) for i in range(1, 5)])
    far_kv, far_qd, own = lax.optimization_barrier((far_kv, far_qd, own))
    pieces = [own] + rising[1:] + falling[1:]

    received = exchange(after(grads, own).reshape(32, 10, HD), YFT)
    out_q, small = query_pass(where, own, pieces + [far_kv])
    part = jnp.sum(received, axis=0)
    small = jnp.concatenate([small, jnp.broadcast_to(part[None], (8, 10, HD))], 1)
    small = lax.all_to_all(
        small, "cz", 0, 0, tiled=True, axis_index_groups=[[7, 6, 5, 4, 3, 2, 1, 0]]
    )[::-1]
    part = share(jnp.sum(small[:, 10:], axis=0), FT, 8)
    stats = small[:, :10].reshape(8, 2, 640)[:, :, :GROUP].transpose(1, 0, 2)
    stats = stats.reshape(2, CHUNKS, CHUNK).transpose(1, 0, 2)
    result = key_pass(where, own, pieces + [far_qd], stats, out_q)
    result = join(result, part)
    attended, grad_queries, grad_keys, grad_values, grad_long, grad_short = unpack(
        exchange(result, "cy")
    )
    return (
        mixed, attended, gfeat.transpose(1, 0, 2), grad_short, grad_long,
        grad_queries, grad_keys, grad_values,
    )


def solution(mesh):
    fine = Mesh(np.asarray(mesh.devices).reshape(8, 4, 4, 2), ("cz", "cy", "fsdp", "tp"))
    rows = P(CTX, FT)
    wide = P(CTX, None, FT)
    return jax.shard_map(
        body,
        mesh=fine,
        in_specs=(wide, P(), P(), rows, rows, rows, rows, rows),
        out_specs=(rows, rows, wide, P(), P(), rows, rows, rows),
        check_vma=False,
    )
```
